32 devices in a mesh: rep: 8 (over y, x, core), grp: 4 (over z).
Axes of the slice: x: 2, y: 2, z: 4, core: 2. Of those that a mesh axis runs over, the one named last changes fastest.
Arguments:
- images: bfloat16 [32, 577, 1024], P(('rep', 'grp')), may hold values from -6 to 6
- cotangent: bfloat16 [32, 577, 1024], P(('rep', 'grp')), may hold values from -6 to 6
- ln1_gain: bfloat16 [1024], P('grp'), may hold values from 0.5 to 1.5
- ln1_shift: bfloat16 [1024], P('grp'), may hold values from -3 to 3
- qkv_weight: bfloat16 [1024, 3072], P('grp'), may hold values from -1 to 1
- qv_bias: bfloat16 [2048], P('grp'), may hold values from -3 to 3
- out_weight: bfloat16 [1024, 1024], P('grp'), may hold values from -1.5 to 1.5
- out_bias: bfloat16 [1024], P('grp'), may hold values from -3 to 3
- ln2_gain: bfloat16 [1024], P('grp'), may hold values from 0.5 to 1.5
- ln2_shift: bfloat16 [1024], P('grp'), may hold values from -3 to 3
- fc1_weight: bfloat16 [1024, 4096], P('grp'), may hold values from -0.1875 to 0.1875
- fc1_bias: bfloat16 [4096], P('grp'), may hold values from -3 to 3
- fc2_weight: bfloat16 [4096, 1024], P('grp'), may hold values from -0.09375 to 0.09375
- fc2_bias: bfloat16 [1024], P('grp'), may hold values from -3 to 3
Outputs:
- outputs: bfloat16 [32, 577, 1024], P(('rep', 'grp'))
- input_grad: bfloat16 [32, 577, 1024], P(('rep', 'grp'))
- grad_ln1_gain: float32 [1024], P('grp')
- grad_ln1_shift: float32 [1024], P('grp')
- grad_qkv_weight: float32 [1024, 3072], P('grp')
- grad_qv_bias: float32 [2048], P('grp')
- grad_out_weight: float32 [1024, 1024], P('grp')
- grad_out_bias: float32 [1024], P('grp')
- grad_ln2_gain: float32 [1024], P('grp')
- grad_ln2_shift: float32 [1024], P('grp')
- grad_fc1_weight: float32 [1024, 4096], P('grp')
- grad_fc1_bias: float32 [4096], P('grp')
- grad_fc2_weight: float32 [4096, 1024], P('grp')
- grad_fc2_bias: float32 [1024], P('grp')
The draws below stay inside these ranges and needn't reach their ends.
All inputs are finite; a program needn't handle non-finite values.
Results may differ from the reference program's by a relative error of at most 0.012.
Values may be sent and summed in bfloat16 or wider, within the bound.
No kernel may reach another device: no remote copies, remote signals or barrier semaphores. Data moves between devices by JAX's collectives and lax.ppermute only.
A program may use at most 256 MiB of HBM per device.

```python
import jax
import jax.numpy as jnp
from jax import lax

D = 1024
H = 16
HD = 64
FF = 4096
S = 577
IMAGES = 32


def draw_qkv_weight(key, part):
    scale = float(D) ** (-0.5)
    base = jax.random.truncated_normal(key, -4.0, 4.0, (D, 3 * D), jnp.float32) * scale
    return jnp.clip(base, -1.0, 1.0).astype(jnp.bfloat16)


def steps_of(key, extent, cuts, low, largest):
    level, own = 1.0, jax.random.fold_in(key, 6)
    for axis_at, blocks in cuts:
        draws = jnp.exp(jax.random.uniform(jax.random.fold_in(own, axis_at), (blocks,), jnp.float32, low / len(cuts), largest / len(cuts)))
        level = level * jnp.repeat(draws, extent[axis_at] // blocks).reshape([-1 if axis == axis_at else 1 for axis in range(len(extent))])
    return level


def gaussian(rng, dims, spread, most, pieces=(), held_as=jnp.bfloat16):
    values = spread * jax.random.normal(rng, dims, jnp.float32)
    if pieces:
        values = values * steps_of(rng, dims, pieces, -0.22, 0.18)
    return jnp.clip(values, -most, most).astype(held_as)


def setup_inputs(seed: int = 0) -> dict:
    streams_of = jax.random.split(jax.random.key(seed), 15)
    images = gaussian(streams_of[0], (IMAGES, S, D), 1.0, 6.0, ((0, 32),))
    cotangent = gaussian(streams_of[1], (IMAGES, S, D), 1.0, 6.0, ((0, 32),))
    ln1_gain = jnp.clip(1.0 + 0.1 * jax.random.normal(streams_of[2], (D,), jnp.float32), 0.5, 1.5).astype(jnp.bfloat16)
    ln1_shift = gaussian(streams_of[3], (D,), 0.5, 3.0, ((0, 4),))
    qkv_weight = draw_qkv_weight(jax.random.fold_in(streams_of[14], 71), 0)
    qv_bias = gaussian(streams_of[5], (2 * D,), 0.5, 3.0, ((0, 4),))
    out_weight = gaussian(streams_of[6], (D, D), (D // 64) ** -0.5, 1.5, ((0, 4),))
    out_bias = gaussian(streams_of[7], (D,), 0.5, 3.0, ((0, 4),))
    ln2_gain = jnp.clip(1.0 + 0.1 * jax.random.normal(streams_of[8], (D,), jnp.float32), 0.5, 1.5).astype(jnp.bfloat16)
    ln2_shift = gaussian(streams_of[9], (D,), 0.5, 3.0, ((0, 4),))
    fc1_weight = gaussian(streams_of[10], (D, FF), D ** -0.5, 0.1875, ((0, 4),))
    fc1_bias = gaussian(streams_of[11], (FF,), 0.5, 3.0, ((0, 4),))
    fc2_weight = gaussian(streams_of[12], (FF, D), FF ** -0.5, 0.09375, ((0, 4),))
    fc2_bias = gaussian(streams_of[13], (D,), 0.5, 3.0, ((0, 4),))
    return dict(images=images, cotangent=cotangent, ln1_gain=ln1_gain, ln1_shift=ln1_shift, qkv_weight=qkv_weight, qv_bias=qv_bias, out_weight=out_weight, out_bias=out_bias, ln2_gain=ln2_gain, ln2_shift=ln2_shift, fc1_weight=fc1_weight, fc1_bias=fc1_bias, fc2_weight=fc2_weight, fc2_bias=fc2_bias)


root_half = 0.7071067811865476
inv_root_tau = 0.3989422804014327

def norm_forward(values, gain_vec, shift_vec):
    row_mean = lax.optimization_barrier(jnp.mean(values, axis=-1, keepdims=True))
    centred = values - row_mean
    inv_std = lax.rsqrt(lax.optimization_barrier(jnp.mean(centred * centred, axis=-1, keepdims=True)) + 1e-06)
    normed = centred * inv_std
    return (normed * gain_vec + shift_vec, normed, inv_std)

def norm_backward(grad_out, normed, inv_std, gain_vec):
    grad_hat = grad_out * gain_vec
    grad_in = inv_std * (grad_hat - lax.optimization_barrier(jnp.mean(grad_hat, axis=-1, keepdims=True)) - normed * lax.optimization_barrier(jnp.mean(grad_hat * normed, axis=-1, keepdims=True)))
    return (grad_in, lax.optimization_barrier(jnp.sum(grad_out * normed, axis=0)), lax.optimization_barrier(jnp.sum(grad_out, axis=0)))

def split_heads(matrix):
    return matrix.reshape(matrix.shape[0], H, HD).transpose(1, 0, 2)

def join_heads(tensor):
    return tensor.transpose(1, 0, 2).reshape(tensor.shape[1], H * HD)

def image_pass(image, grad_block, params):
    gain_first, shift_first, attn_in, bias_pair, attn_out, bias_attn, gain_second, shift_second, mlp_up, bias_up, mlp_down, bias_down = params
    model_width = attn_out.shape[0]
    incoming = image.astype(jnp.float32)
    normed_f, normed_one, inv_std_one = norm_forward(incoming, gain_first, shift_first)
    normed_in = normed_f.astype(jnp.bfloat16)
    projected = jnp.dot(normed_in, attn_in, preferred_element_type=jnp.float32)
    query_heads = split_heads(((projected[:, :model_width] + bias_pair[:model_width]) * 0.125).astype(jnp.bfloat16))
    key_heads = split_heads(projected[:, model_width:2 * model_width].astype(jnp.bfloat16))
    value_heads = split_heads((projected[:, 2 * model_width:] + bias_pair[model_width:]).astype(jnp.bfloat16))
    query_f = query_heads.astype(jnp.float32)
    key_f = key_heads.astype(jnp.float32)
    value_f = value_heads.astype(jnp.float32)
    scores = jnp.einsum('hqd,hkd->hqk', query_f, key_f)
    row_max = lax.optimization_barrier(jnp.max(scores, axis=-1, keepdims=True))
    log_total = row_max + jnp.log(lax.optimization_barrier(jnp.sum(jnp.exp(scores - row_max), axis=-1, keepdims=True)))
    probs_exact = jnp.exp(scores - log_total)
    probs = probs_exact.astype(jnp.bfloat16)
    mixed = jnp.einsum('hqk,hkd->hqd', probs.astype(jnp.float32), value_f)
    attended = join_heads(mixed).astype(jnp.bfloat16)
    residual = incoming + jnp.dot(attended, attn_out, preferred_element_type=jnp.float32) + bias_attn
    mid_f, normed_two, inv_std_two = norm_forward(residual, gain_second, shift_second)
    normed_mid = mid_f.astype(jnp.bfloat16)
    pre_act = jnp.dot(normed_mid, mlp_up, preferred_element_type=jnp.float32) + bias_up
    normal_cdf = 0.5 * (1.0 + lax.erf(pre_act * root_half))
    activated = (pre_act * normal_cdf).astype(jnp.bfloat16)
    block_out = (residual + jnp.dot(activated, mlp_down, preferred_element_type=jnp.float32) + bias_down).astype(jnp.bfloat16)
    grad_top = grad_block.astype(jnp.float32)
    grad_down = jnp.dot(activated.T, grad_block, preferred_element_type=jnp.float32)
    grad_bias_down = lax.optimization_barrier(jnp.sum(grad_top, axis=0))
    grad_hidden = jnp.dot(grad_block, mlp_down.T, preferred_element_type=jnp.float32)
    density = jnp.exp(-0.5 * pre_act * pre_act) * inv_root_tau
    grad_pre = grad_hidden * (normal_cdf + pre_act * density)
    grad_pre_b = grad_pre.astype(jnp.bfloat16)
    grad_up = jnp.dot(normed_mid.T, grad_pre_b, preferred_element_type=jnp.float32)
    grad_bias_up = lax.optimization_barrier(jnp.sum(grad_pre, axis=0))
    grad_mid = jnp.dot(grad_pre_b, mlp_up.T, preferred_element_type=jnp.float32)
    grad_norm_mid, grad_gain_second, grad_shift_second = norm_backward(grad_mid, normed_two, inv_std_two, gain_second)
    grad_residual = grad_top + grad_norm_mid
    grad_bias_attn = lax.optimization_barrier(jnp.sum(grad_residual, axis=0))
    grad_res_b = grad_residual.astype(jnp.bfloat16)
    grad_attn_out = jnp.dot(attended.T, grad_res_b, preferred_element_type=jnp.float32)
    grad_attended = split_heads(jnp.dot(grad_res_b, attn_out.T, preferred_element_type=jnp.float32).astype(jnp.bfloat16))
    grad_att_f = grad_attended.astype(jnp.float32)
    grad_probs = jnp.einsum('hqd,hkd->hqk', grad_att_f, value_f)
    row_dot = lax.optimization_barrier(jnp.sum(probs_exact * grad_probs, axis=-1, keepdims=True))
    grad_scores = (probs_exact * (grad_probs - row_dot)).astype(jnp.bfloat16).astype(jnp.float32)
    grad_query = jnp.einsum('hqk,hkd->hqd', grad_scores, key_f) * 0.125
    grad_key = jnp.einsum('hqk,hqd->hkd', grad_scores, query_f)
    grad_value = jnp.einsum('hqk,hqd->hkd', probs.astype(jnp.float32), grad_att_f)
    grad_query = join_heads(grad_query)
    grad_key = join_heads(grad_key)
    grad_value = join_heads(grad_value)
    grad_projected = jnp.concatenate([grad_query, grad_key, grad_value], axis=1)
    grad_bias_pair = jnp.concatenate([lax.optimization_barrier(jnp.sum(grad_query, axis=0)), lax.optimization_barrier(jnp.sum(grad_value, axis=0))])
    grad_proj_b = grad_projected.astype(jnp.bfloat16)
    grad_attn_in = jnp.dot(normed_in.T, grad_proj_b, preferred_element_type=jnp.float32)
    grad_in_norm = jnp.dot(grad_proj_b, attn_in.T, preferred_element_type=jnp.float32)
    grad_norm_in, grad_gain_first, grad_shift_first = norm_backward(grad_in_norm, normed_one, inv_std_one, gain_first)
    input_grad = (grad_residual + grad_norm_in).astype(jnp.bfloat16)
    grads = (grad_gain_first, grad_shift_first, grad_attn_in, grad_bias_pair, grad_attn_out, grad_bias_attn, grad_gain_second, grad_shift_second, grad_up, grad_bias_up, grad_down, grad_bias_down)
    return (block_out, input_grad, grads)

def reference(images, cotangent, ln1_gain, ln1_shift, qkv_weight, qv_bias, out_weight, out_bias, ln2_gain, ln2_shift, fc1_weight, fc1_bias, fc2_weight, fc2_bias):
    params = (ln1_gain.astype(jnp.float32), ln1_shift.astype(jnp.float32), qkv_weight, qv_bias.astype(jnp.float32), out_weight, out_bias.astype(jnp.float32), ln2_gain.astype(jnp.float32), ln2_shift.astype(jnp.float32), fc1_weight, fc1_bias.astype(jnp.float32), fc2_weight, fc2_bias.astype(jnp.float32))
    zeros = tuple((jnp.zeros(item.shape, jnp.float32) for item in params))

    def one_image(totals, image_pair):
        block_out, input_grad, grads = image_pass(image_pair[0], image_pair[1], params)
        return (jax.tree.map(jnp.add, totals, grads), (block_out, input_grad))
    totals, stacked = lax.scan(one_image, zeros, (images, cotangent))
    return (stacked[0], stacked[1], totals[0], totals[1], totals[2], totals[3], totals[4], totals[5], totals[6], totals[7], totals[8], totals[9], totals[10], totals[11])
```

```python
import math

import jax
import jax.numpy as jnp
from jax import lax
from jax.sharding import PartitionSpec as P

H = 16
HD = 64


root_half = 0.7071067811865476
inv_root_tau = 0.3989422804014327


def norm_forward(values, gain_vec, shift_vec):
    row_mean = jnp.mean(values, axis=-1, keepdims=True)
    centred = values - row_mean
    inv_std = lax.rsqrt(jnp.mean(centred * centred, axis=-1, keepdims=True) + 1e-06)
    normed = centred * inv_std
    return (normed * gain_vec + shift_vec, normed, inv_std)


def norm_backward(grad_out, normed, inv_std, gain_vec):
    grad_hat = grad_out * gain_vec
    grad_in = inv_std * (
        grad_hat
        - jnp.mean(grad_hat, axis=-1, keepdims=True)
        - normed * jnp.mean(grad_hat * normed, axis=-1, keepdims=True)
    )
    return (grad_in, jnp.sum(grad_out * normed, axis=0), jnp.sum(grad_out, axis=0))


def split_heads(matrix):
    return matrix.reshape(matrix.shape[0], H, HD).transpose(1, 0, 2)


def join_heads(tensor):
    return tensor.transpose(1, 0, 2).reshape(tensor.shape[1], H * HD)


def grouped(tensor):
    group_size = math.gcd(H, 4)
    return tensor.reshape((H // group_size, group_size) + tensor.shape[1:])


def ungrouped(tensor):
    return tensor.reshape((H,) + tensor.shape[2:])


def head_scores(query_group, key_group):
    return jnp.einsum("hqd,hkd->hqk", query_group, key_group, preferred_element_type=jnp.float32)


def attend_group(group):
    query_group, key_group, value_group = group
    scores = head_scores(query_group, key_group)
    row_max = jnp.max(scores, axis=-1, keepdims=True)
    log_total = row_max + jnp.log(jnp.sum(jnp.exp(scores - row_max), axis=-1, keepdims=True))
    probs = jnp.exp(scores - log_total).astype(jnp.bfloat16)
    mixed = jnp.einsum("hqk,hkd->hqd", probs, value_group, preferred_element_type=jnp.float32)
    return (mixed, log_total)


def attend_back(group):
    query_group, key_group, value_group, log_total, grad_mixed = group
    probs_exact = jnp.exp(head_scores(query_group, key_group) - log_total)
    grad_probs = jnp.einsum(
        "hqd,hkd->hqk", grad_mixed, value_group, preferred_element_type=jnp.float32
    )
    row_dot = jnp.sum(probs_exact * grad_probs, axis=-1, keepdims=True)
    grad_scores = (probs_exact * (grad_probs - row_dot)).astype(jnp.bfloat16)
    grad_query = (
        jnp.einsum("hqk,hkd->hqd", grad_scores, key_group, preferred_element_type=jnp.float32)
        * 0.125
    )
    grad_key = jnp.einsum(
        "hqk,hqd->hkd", grad_scores, query_group, preferred_element_type=jnp.float32
    )
    grad_value = jnp.einsum(
        "hqk,hqd->hkd",
        probs_exact.astype(jnp.bfloat16),
        grad_mixed,
        preferred_element_type=jnp.float32,
    )
    return (grad_query, grad_key, grad_value)


def forward_image(image, params):
    (
        gain_first,
        shift_first,
        attn_in,
        bias_pair,
        attn_out,
        bias_attn,
        gain_second,
        shift_second,
        mlp_up,
        bias_up,
        mlp_down,
        bias_down,
    ) = params
    model_width = attn_out.shape[0]
    incoming = image.astype(jnp.float32)
    normed_f, normed_one, inv_std_one = norm_forward(
        incoming, gain_first.astype(jnp.float32), shift_first.astype(jnp.float32)
    )
    normed_in = normed_f.astype(jnp.bfloat16)
    projected = jnp.dot(normed_in, attn_in, preferred_element_type=jnp.float32)
    bias_float = bias_pair.astype(jnp.float32)
    query_heads = split_heads(
        ((projected[:, :model_width] + bias_float[:model_width]) * 0.125).astype(jnp.bfloat16)
    )
    key_heads = split_heads(projected[:, model_width : 2 * model_width].astype(jnp.bfloat16))
    value_heads = split_heads(
        (projected[:, 2 * model_width :] + bias_float[model_width:]).astype(jnp.bfloat16)
    )
    mixed, log_total = lax.map(
        attend_group, (grouped(query_heads), grouped(key_heads), grouped(value_heads))
    )
    attended = join_heads(ungrouped(mixed)).astype(jnp.bfloat16)
    residual = (
        incoming
        + jnp.dot(attended, attn_out, preferred_element_type=jnp.float32)
        + bias_attn.astype(jnp.float32)
    )
    mid_f, normed_two, inv_std_two = norm_forward(
        residual, gain_second.astype(jnp.float32), shift_second.astype(jnp.float32)
    )
    normed_mid = mid_f.astype(jnp.bfloat16)
    pre_act = jnp.dot(normed_mid, mlp_up, preferred_element_type=jnp.float32) + bias_up.astype(
        jnp.float32
    )
    normal_cdf = 0.5 * (1.0 + lax.erf(pre_act * root_half))
    activated = (pre_act * normal_cdf).astype(jnp.bfloat16)
    block_out = (
        residual
        + jnp.dot(activated, mlp_down, preferred_element_type=jnp.float32)
        + bias_down.astype(jnp.float32)
    ).astype(jnp.bfloat16)
    stored = (
        normed_in,
        normed_one,
        inv_std_one,
        query_heads,
        key_heads,
        value_heads,
        ungrouped(log_total),
        attended,
        normed_mid,
        normed_two,
        inv_std_two,
        pre_act,
        normal_cdf,
        activated,
    )
    return (block_out, stored)


def backward_image(grad_block, stored, params):
    (
        gain_first,
        shift_first,
        attn_in,
        bias_pair,
        attn_out,
        bias_attn,
        gain_second,
        shift_second,
        mlp_up,
        bias_up,
        mlp_down,
        bias_down,
    ) = params
    (
        normed_in,
        normed_one,
        inv_std_one,
        query_heads,
        key_heads,
        value_heads,
        log_total,
        attended,
        normed_mid,
        normed_two,
        inv_std_two,
        pre_act,
        normal_cdf,
        activated,
    ) = stored
    grad_top = grad_block.astype(jnp.float32)
    grad_down = jnp.dot(activated.T, grad_block, preferred_element_type=jnp.float32)
    grad_bias_down = jnp.sum(grad_top, axis=0)
    grad_hidden = jnp.dot(grad_block, mlp_down.T, preferred_element_type=jnp.float32)
    density = jnp.exp(-0.5 * pre_act * pre_act) * inv_root_tau
    grad_pre = grad_hidden * (normal_cdf + pre_act * density)
    grad_pre_b = grad_pre.astype(jnp.bfloat16)
    grad_up = jnp.dot(normed_mid.T, grad_pre_b, preferred_element_type=jnp.float32)
    grad_bias_up = jnp.sum(grad_pre, axis=0)
    grad_mid = jnp.dot(grad_pre_b, mlp_up.T, preferred_element_type=jnp.float32)
    grad_norm_mid, grad_gain_second, grad_shift_second = norm_backward(
        grad_mid, normed_two, inv_std_two, gain_second.astype(jnp.float32)
    )
    grad_residual = grad_top + grad_norm_mid
    grad_bias_attn = jnp.sum(grad_residual, axis=0)
    grad_res_b = grad_residual.astype(jnp.bfloat16)
    grad_attn_out = jnp.dot(attended.T, grad_res_b, preferred_element_type=jnp.float32)
    grad_attended = split_heads(
        jnp.dot(grad_res_b, attn_out.T, preferred_element_type=jnp.float32).astype(jnp.bfloat16)
    )
    grad_query, grad_key, grad_value = lax.map(
        attend_back,
        (
            grouped(query_heads),
            grouped(key_heads),
            grouped(value_heads),
            grouped(log_total),
            grouped(grad_attended),
        ),
    )
    grad_query = join_heads(ungrouped(grad_query))
    grad_key = join_heads(ungrouped(grad_key))
    grad_value = join_heads(ungrouped(grad_value))
    grad_projected = jnp.concatenate([grad_query, grad_key, grad_value], axis=1)
    grad_bias_pair = jnp.concatenate([jnp.sum(grad_query, axis=0), jnp.sum(grad_value, axis=0)])
    grad_proj_b = grad_projected.astype(jnp.bfloat16)
    grad_attn_in = jnp.dot(normed_in.T, grad_proj_b, preferred_element_type=jnp.float32)
    grad_in_norm = jnp.dot(grad_proj_b, attn_in.T, preferred_element_type=jnp.float32)
    grad_norm_in, grad_gain_first, grad_shift_first = norm_backward(
        grad_in_norm, normed_one, inv_std_one, gain_first.astype(jnp.float32)
    )
    input_grad = (grad_residual + grad_norm_in).astype(jnp.bfloat16)
    grads = (
        grad_gain_first,
        grad_shift_first,
        grad_attn_in,
        grad_bias_pair,
        grad_attn_out,
        grad_bias_attn,
        grad_gain_second,
        grad_shift_second,
        grad_up,
        grad_bias_up,
        grad_down,
        grad_bias_down,
    )
    return (input_grad, grads)


def on_device(
    images,
    cotangent,
    ln1_gain,
    ln1_shift,
    qkv_weight,
    qv_bias,
    out_weight,
    out_bias,
    ln2_gain,
    ln2_shift,
    fc1_weight,
    fc1_bias,
    fc2_weight,
    fc2_bias,
):
    n_rep = lax.axis_size("rep")
    n_grp = lax.axis_size("grp")
    rep = lax.axis_index("rep")

    def gather_matrix(shard):
        rows, cols = shard.shape
        block = lax.dynamic_slice_in_dim(shard, rep * (cols // n_rep), cols // n_rep, 1)
        full = lax.all_gather(block, ("rep", "grp"), axis=0, tiled=False)
        full = full.reshape(n_rep, n_grp * rows, cols // n_rep)
        return full.transpose(1, 0, 2).reshape(n_grp * rows, cols)

    vectors = (ln1_gain, ln1_shift, qv_bias, out_bias, ln2_gain, ln2_shift, fc1_bias, fc2_bias)
    sizes = [vec.shape[0] for vec in vectors]
    packed = lax.all_gather(jnp.concatenate(vectors), "grp", axis=0, tiled=False)
    full_vectors = []
    offset = 0
    for size in sizes:
        full_vectors.append(packed[:, offset : offset + size].reshape(-1))
        offset += size
    params = (
        full_vectors[0],
        full_vectors[1],
        gather_matrix(qkv_weight),
        full_vectors[2],
        gather_matrix(out_weight),
        full_vectors[3],
        full_vectors[4],
        full_vectors[5],
        gather_matrix(fc1_weight),
        full_vectors[6],
        gather_matrix(fc2_weight),
        full_vectors[7],
    )
    block_out, stored = forward_image(images[0], params)
    input_grad, grads = backward_image(cotangent[0], stored, params)

    def reduce_matrix(grad):
        rows, cols = grad.shape
        part = grad.astype(jnp.bfloat16).reshape(rows, n_rep, cols // n_rep).transpose(1, 0, 2)
        part = lax.psum_scatter(part, "rep", scatter_dimension=0, tiled=False)
        part = lax.psum_scatter(part, "grp", scatter_dimension=0, tiled=True)
        full = lax.all_gather(part, "rep", axis=0, tiled=False)
        return full.transpose(1, 0, 2).reshape(rows // n_grp, cols).astype(jnp.float32)

    order = (0, 1, 3, 5, 6, 7, 9, 11)
    small = jnp.concatenate([grads[at].reshape(n_grp, -1) for at in order], axis=1)
    small = lax.psum(lax.psum_scatter(small, "grp", scatter_dimension=0, tiled=False), "rep")
    totals = [None] * 12
    offset = 0
    for at, size in zip(order, sizes):
        totals[at] = small[offset : offset + size]
        offset += size
    for at in (10, 8, 4, 2):
        totals[at] = reduce_matrix(grads[at])
    return (block_out[None], input_grad[None], *totals)


def solution(mesh):
    return jax.shard_map(
        on_device,
        mesh=mesh,
        in_specs=(
            P(("rep", "grp"), None, None),
            P(("rep", "grp"), None, None),
            P("grp"),
            P("grp"),
            P("grp", None),
            P("grp"),
            P("grp", None),
            P("grp"),
            P("grp"),
            P("grp"),
            P("grp", None),
            P("grp"),
            P("grp", None),
            P("grp"),
        ),
        out_specs=(
            P(("rep", "grp"), None, None),
            P(("rep", "grp"), None, None),
            P("grp"),
            P("grp"),
            P("grp", None),
            P("grp"),
            P("grp", None),
            P("grp"),
            P("grp"),
            P("grp"),
            P("grp", None),
            P("grp"),
            P("grp", None),
            P("grp"),
        ),
        check_vma=False,
    )
```

```python
import jax
import jax.numpy as jnp
from jax import lax
from jax.experimental import pallas as pl
from jax.experimental.pallas import tpu as pltpu
from jax.sharding import PartitionSpec as P


BLOCKS = 8
LANES = 128
TILE = 512
HD = 64
PAIR = 128
EPS = 1e-06

root_half = 0.7071067811865476
inv_root_tau = 0.3989422804014327

NN = (((1,), (0,)), ((), ()))
NT = (((1,), (1,)), ((), ()))
TN = (((0,), (0,)), ((), ()))
ANY = pl.BlockSpec(memory_space=pl.ANY)


def product(left, right, dims=NN):
    return lax.dot_general(left, right, dims, preferred_element_type=jnp.float32)


def aligned(start, unit):
    return pl.multiple_of(start, unit)


def params(**extra):
    return pltpu.CompilerParams(vmem_limit_bytes=60 << 20, **extra)


def cost(flops, moved):
    return pl.CostEstimate(flops=int(flops), bytes_accessed=int(moved), transcendentals=0)


def start_loads(where, own, pieces, strips, target, sems, mode):
    share = own.shape[0]
    groups = target.shape[0] // share
    mine = where[1]

    def go(source, rows, columns, key):
        pltpu.make_async_copy(source, target.at[rows, columns], sems.at[key]).start()

    own_rows = pl.ds(aligned(mine * share, share), share)
    if mode == "row":
        pltpu.make_async_copy(own, target.at[own_rows, :], sems.at[0]).start()
    for which, (source, size, base) in enumerate(strips):
        for at in range(BLOCKS):
            block = jnp.bitwise_xor(where[0], at)
            columns = pl.ds(aligned(base + block * size, LANES), size)
            key = {"part": which, "block": at}.get(mode)
            if mode != "row":
                go(own.at[:, columns], own_rows, columns, key)
            for hop in range(1, groups):
                first = jnp.bitwise_xor(mine, hop) * share
                low = 0
                for ref in pieces[at]:
                    high = low + ref.shape[0]
                    begin, end = max(low, (hop - 1) * share), min(high, hop * share)
                    if begin < end:
                        shift = begin - (hop - 1) * share
                        rows = pl.ds(aligned(first + shift, 16), end - begin)
                        go(
                            ref.at[begin - low : end - low, source : source + size],
                            rows,
                            columns,
                            hop if mode == "row" else key,
                        )
                    low = high


def finish(region, sem):
    pltpu.make_async_copy(region, region, sem).wait()


def wait_rows(where, target, sems, hop, share):
    rows = pl.ds(aligned(jnp.bitwise_xor(where[1], hop) * share, share), share)
    finish(target.at[rows, :], sems.at[hop])


def flat(pieces):
    return [array for piece in pieces for array in piece]


def regroup(refs, pieces):
    grouped, at = [], 0
    for piece in pieces:
        grouped.append(refs[at : at + len(piece)])
        at += len(piece)
    return grouped


def center(values):
    mean = jnp.mean(values, axis=-1, keepdims=True)
    centred = values - mean
    inv_std = lax.rsqrt(jnp.mean(centred * centred, axis=-1, keepdims=True) + EPS)
    return centred * inv_std, inv_std


def center_back(grad_out, normed, inv_std, gain):
    grad_hat = grad_out * gain
    return inv_std * (
        grad_hat
        - jnp.mean(grad_hat, axis=-1, keepdims=True)
        - normed * jnp.mean(grad_hat * normed, axis=-1, keepdims=True)
    )


def column_sum(values):
    return jnp.sum(values, axis=0, keepdims=True)


def qkv_forward(where, image, gain, shift, bias, own, pieces):
    tokens, width = image.shape
    wide = own.shape[1]
    per = width // TILE
    strips = [(part * LANES, LANES, part * width) for part in range(3)]

    def body(where_ref, image_ref, gain_ref, shift_ref, bias_ref, own_ref, *rest):
        piece_refs = regroup(rest[: len(flat(pieces))], pieces)
        normed_ref, out_ref, weight, sems = rest[len(flat(pieces)) :]
        at = pl.program_id(0)

        @pl.when(at == 0)
        def _():
            start_loads(where_ref, own_ref, piece_refs, strips, weight, sems, "part")
            normed, _ = center(image_ref[...].astype(jnp.float32))
            normed_ref[...] = (normed * gain_ref[...] + shift_ref[...]).astype(jnp.bfloat16)

        for part in range(3):

            @pl.when(at == part * per)
            def _(part=part):
                finish(weight.at[:, part * width : (part + 1) * width], sems.at[part])

        columns = pl.ds(aligned(at * TILE, TILE), TILE)
        total = product(normed_ref[...], weight[:, columns]) + bias_ref[...]
        scale = jnp.where(at < per, 0.125, 1.0)
        out_ref[...] = (total * scale).astype(jnp.bfloat16)

    full = lambda at, _: (0, 0)
    return pl.pallas_call(
        body,
        grid_spec=pltpu.PrefetchScalarGridSpec(
            num_scalar_prefetch=1,
            grid=(wide // TILE,),
            in_specs=[
                pl.BlockSpec((tokens, width), full),
                pl.BlockSpec((1, width), full),
                pl.BlockSpec((1, width), full),
                pl.BlockSpec((1, TILE), lambda at, _: (0, at)),
            ]
            + [ANY] * (1 + len(flat(pieces))),
            out_specs=[
                pl.BlockSpec((tokens, width), full),
                pl.BlockSpec((tokens, TILE), lambda at, _: (0, at)),
            ],
            scratch_shapes=[
                pltpu.VMEM((width, wide), jnp.bfloat16),
                pltpu.SemaphoreType.DMA((3,)),
            ],
        ),
        out_shape=[
            jax.ShapeDtypeStruct((tokens, width), jnp.bfloat16),
            jax.ShapeDtypeStruct((tokens, wide), jnp.bfloat16),
        ],
        cost_estimate=cost(2 * tokens * width * wide, 2 * width * wide),
        compiler_params=params(),
        name="qkv_forward",
    )(where, image, gain, shift, bias, own, *flat(pieces))


def out_forward(where, image, attended, bias, gain, shift, own, pieces, source):
    tokens, width = image.shape
    share = own.shape[0]
    groups = width // share
    chunk = 256

    def body(where_ref, image_ref, attended_ref, bias_ref, gain_ref, shift_ref, own_ref, *rest):
        piece_refs = regroup(rest[: len(flat(pieces))], pieces)
        residual_ref, normed_ref, weight, sems = rest[len(flat(pieces)) :]
        start_loads(where_ref, own_ref, piece_refs, [(source, LANES, 0)], weight, sems, "row")
        for hop in range(groups):
            wait_rows(where_ref, weight, sems, hop, share)

        @pl.loop(0, width // chunk)
        def _(at):
            columns = pl.ds(aligned(at * chunk, chunk), chunk)
            residual_ref[:, columns] = (
                image_ref[:, columns].astype(jnp.float32)
                + product(attended_ref[...], weight[:, columns])
                + bias_ref[:, columns]
            )

        normed, _ = center(residual_ref[...])
        normed_ref[...] = (normed * gain_ref[...] + shift_ref[...]).astype(jnp.bfloat16)

    full = lambda at, _: (0, 0)
    return pl.pallas_call(
        body,
        grid_spec=pltpu.PrefetchScalarGridSpec(
            num_scalar_prefetch=1,
            grid=(1,),
            in_specs=[pl.BlockSpec((tokens, width), full)] * 2
            + [pl.BlockSpec((1, width), full)] * 3
            + [ANY] * (1 + len(flat(pieces))),
            out_specs=[pl.BlockSpec((tokens, width), full)] * 2,
            scratch_shapes=[
                pltpu.VMEM((width, width), jnp.bfloat16),
                pltpu.SemaphoreType.DMA((groups,)),
            ],
        ),
        out_shape=[
            jax.ShapeDtypeStruct((tokens, width), jnp.float32),
            jax.ShapeDtypeStruct((tokens, width), jnp.bfloat16),
        ],
        cost_estimate=cost(2 * tokens * width * width, 2 * width * width),
        compiler_params=params(),
        name="out_forward",
    )(where, image, attended, bias, gain, shift, own, *flat(pieces))


def up_forward(where, normed, bias, own, pieces):
    tokens, width = normed.shape
    wide = own.shape[1]
    size = wide // BLOCKS

    def body(where_ref, normed_ref, bias_ref, own_ref, *rest):
        piece_refs = regroup(rest[: len(flat(pieces))], pieces)
        active_ref, slope_ref, weight, sems = rest[len(flat(pieces)) :]
        at = pl.program_id(0)

        @pl.when(at == 0)
        def _():
            start_loads(where_ref, own_ref, piece_refs, [(0, size, 0)], weight, sems, "block")

        columns = pl.ds(aligned(jnp.bitwise_xor(where_ref[0], at) * size, size), size)
        finish(weight.at[:, columns], sems.at[at])
        pre_act = product(normed_ref[...], weight[:, columns]) + bias_ref[...]
        cdf = 0.5 * (1.0 + lax.erf(pre_act * root_half))
        density = jnp.exp(-0.5 * pre_act * pre_act) * inv_root_tau
        active_ref[...] = (pre_act * cdf).astype(jnp.bfloat16)
        slope_ref[...] = (cdf + pre_act * density).astype(jnp.bfloat16)

    full = lambda at, _: (0, 0)
    mine = lambda at, where_ref: (0, jnp.bitwise_xor(where_ref[0], at))
    return pl.pallas_call(
        body,
        grid_spec=pltpu.PrefetchScalarGridSpec(
            num_scalar_prefetch=1,
            grid=(BLOCKS,),
            in_specs=[pl.BlockSpec((tokens, width), full), pl.BlockSpec((1, size), mine)]
            + [ANY] * (1 + len(flat(pieces))),
            out_specs=[pl.BlockSpec((tokens, size), mine)] * 2,
            scratch_shapes=[
                pltpu.VMEM((width, wide), jnp.bfloat16),
                pltpu.SemaphoreType.DMA((BLOCKS,)),
            ],
        ),
        out_shape=[jax.ShapeDtypeStruct((tokens, wide), jnp.bfloat16)] * 2,
        cost_estimate=cost(2 * tokens * width * wide, 2 * width * wide),
        compiler_params=params(),
        name="up_forward",
    )(where, normed, bias, own, *flat(pieces))


def down_forward(where, residual, active, bias, own, pieces):
    tokens, wide = active.shape
    width = residual.shape[1]
    share = own.shape[0]
    groups = wide // share
    chunk = 256

    def body(where_ref, residual_ref, active_ref, bias_ref, own_ref, *rest):
        piece_refs = regroup(rest[: len(flat(pieces))], pieces)
        out_ref, weight, sems = rest[len(flat(pieces)) :]
        at = pl.program_id(0)

        @pl.when(at == 0)
        def _():
            start_loads(where_ref, own_ref, piece_refs, [(0, LANES, 0)], weight, sems, "row")
            for hop in range(groups):
                wait_rows(where_ref, weight, sems, hop, share)

        columns = pl.ds(aligned(at * chunk, chunk), chunk)
        out_ref[...] = (
            residual_ref[...] + product(active_ref[...], weight[:, columns]) + bias_ref[...]
        ).astype(jnp.bfloat16)

    block = lambda at, _: (0, at)
    return pl.pallas_call(
        body,
        grid_spec=pltpu.PrefetchScalarGridSpec(
            num_scalar_prefetch=1,
            grid=(width // chunk,),
            in_specs=[
                pl.BlockSpec((tokens, chunk), block),
                pl.BlockSpec((tokens, wide), lambda at, _: (0, 0)),
                pl.BlockSpec((1, chunk), block),
            ]
            + [ANY] * (1 + len(flat(pieces))),
            out_specs=pl.BlockSpec((tokens, chunk), block),
            scratch_shapes=[
                pltpu.VMEM((wide, width), jnp.bfloat16),
                pltpu.SemaphoreType.DMA((groups,)),
            ],
        ),
        out_shape=jax.ShapeDtypeStruct((tokens, width), jnp.bfloat16),
        cost_estimate=cost(2 * tokens * width * wide, 2 * width * wide),
        compiler_params=params(),
        name="down_forward",
    )(where, residual, active, bias, own, *flat(pieces))


def down_backward(where, grad_block, slope, own, pieces):
    tokens, wide = slope.shape
    width = grad_block.shape[1]
    share = own.shape[0]
    groups = wide // share
    tile = min(TILE, share)
    per = share // tile

    def body(where_ref, grad_ref, slope_ref, own_ref, *rest):
        piece_refs = regroup(rest[: len(flat(pieces))], pieces)
        out_ref, sum_ref, weight, sems = rest[len(flat(pieces)) :]
        at = pl.program_id(0)

        @pl.when(at == 0)
        def _():
            start_loads(where_ref, own_ref, piece_refs, [(0, LANES, 0)], weight, sems, "row")

        hop = at // per

        @pl.when(at % per == 0)
        def _():
            wait_rows(where_ref, weight, sems, hop, share)

        row = jnp.bitwise_xor(where_ref[1], hop) * share + (at % per) * tile
        rows = pl.ds(aligned(row, tile), tile)
        grad_pre = product(grad_ref[...], weight[rows, :], NT) * slope_ref[...].astype(jnp.float32)
        out_ref[...] = grad_pre.astype(jnp.bfloat16)
        sum_ref[...] = column_sum(grad_pre)

    mine = lambda at, where_ref: (0, jnp.bitwise_xor(where_ref[1], at // per) * per + at % per)
    return pl.pallas_call(
        body,
        grid_spec=pltpu.PrefetchScalarGridSpec(
            num_scalar_prefetch=1,
            grid=(wide // tile,),
            in_specs=[
                pl.BlockSpec((tokens, width), lambda at, _: (0, 0)),
                pl.BlockSpec((tokens, tile), mine),
            ]
            + [ANY] * (1 + len(flat(pieces))),
            out_specs=[pl.BlockSpec((tokens, tile), mine), pl.BlockSpec((1, tile), mine)],
            scratch_shapes=[
                pltpu.VMEM((wide, width), jnp.bfloat16),
                pltpu.SemaphoreType.DMA((groups,)),
            ],
        ),
        out_shape=[
            jax.ShapeDtypeStruct((tokens, wide), jnp.bfloat16),
            jax.ShapeDtypeStruct((1, wide), jnp.float32),
        ],
        cost_estimate=cost(2 * tokens * width * wide, 2 * width * wide),
        compiler_params=params(),
        name="down_backward",
    )(where, grad_block, slope, own, *flat(pieces))


def middle_backward(where, grad_pre, grad_block, residual, gain, own_up, own_out, pieces, size):
    tokens, wide = grad_pre.shape
    width = grad_block.shape[1]
    share = own_up.shape[0]
    groups = width // share
    chunk = 256

    def body(where_ref, pre_ref, block_ref, residual_ref, gain_ref, up_ref, own_ref, *rest):
        piece_refs = regroup(rest[: len(flat(pieces))], pieces)
        (full_ref, half_ref, att_ref, gain_sum, shift_sum, res_sum, top_sum) = rest[
            len(flat(pieces)) : len(flat(pieces)) + 7
        ]
        weight, weight_out, middle, sems, out_sems = rest[len(flat(pieces)) + 7 :]
        at = pl.program_id(0)

        @pl.when(at == 0)
        def _():
            start_loads(where_ref, up_ref, piece_refs, [(0, size, 0)], weight, sems, "row")
            start_loads(
                where_ref, own_ref, piece_refs, [(size, LANES, 0)], weight_out, out_sems, "row"
            )

        wait_rows(where_ref, weight, sems, at, share)
        rows = pl.ds(aligned(jnp.bitwise_xor(where_ref[1], at) * share, share), share)
        middle[:, rows] = product(pre_ref[...], weight[rows, :], NT)

        @pl.when(at == groups - 1)
        def _():
            normed, inv_std = center(residual_ref[...])
            grad_mid = middle[...]
            gain_sum[...] = column_sum(grad_mid * normed)
            shift_sum[...] = column_sum(grad_mid)
            top = block_ref[...].astype(jnp.float32)
            top_sum[...] = column_sum(top)
            grad_res = top + center_back(grad_mid, normed, inv_std, gain_ref[...])
            full_ref[...] = grad_res
            res_sum[...] = column_sum(grad_res)
            half_ref[...] = grad_res.astype(jnp.bfloat16)
            for hop in range(groups):
                wait_rows(where_ref, weight_out, out_sems, hop, share)

            @pl.loop(0, width // chunk)
            def _(step):
                part = pl.ds(aligned(step * chunk, chunk), chunk)
                att_ref[:, part] = product(half_ref[...], weight_out[part, :], NT).astype(
                    jnp.bfloat16
                )

    full = lambda at, _: (0, 0)
    line = pl.BlockSpec((1, width), full)
    square = pl.BlockSpec((tokens, width), full)
    return pl.pallas_call(
        body,
        grid_spec=pltpu.PrefetchScalarGridSpec(
            num_scalar_prefetch=1,
            grid=(groups,),
            in_specs=[pl.BlockSpec((tokens, wide), full), square, square, line]
            + [ANY] * (2 + len(flat(pieces))),
            out_specs=[square] * 3 + [line] * 4,
            scratch_shapes=[
                pltpu.VMEM((width, wide), jnp.bfloat16),
                pltpu.VMEM((width, width), jnp.bfloat16),
                pltpu.VMEM((tokens, width), jnp.float32),
                pltpu.SemaphoreType.DMA((groups,)),
                pltpu.SemaphoreType.DMA((groups,)),
            ],
        ),
        out_shape=[
            jax.ShapeDtypeStruct((tokens, width), jnp.float32),
            jax.ShapeDtypeStruct((tokens, width), jnp.bfloat16),
            jax.ShapeDtypeStruct((tokens, width), jnp.bfloat16),
        ]
        + [jax.ShapeDtypeStruct((1, width), jnp.float32)] * 4,
        cost_estimate=cost(2 * tokens * width * (wide + width), 2 * width * (wide + width)),
        compiler_params=params(),
        name="middle_backward",
    )(where, grad_pre, grad_block, residual, gain, own_up, own_out, *flat(pieces))


def qkv_backward(where, grad_proj, image, grad_res, gain, own, pieces):
    tokens, width = image.shape
    wide = own.shape[1]
    share = own.shape[0]
    groups = width // share
    strips = [(part * LANES, LANES, part * width) for part in range(3)]

    def body(where_ref, proj_ref, image_ref, res_ref, gain_ref, own_ref, *rest):
        piece_refs = regroup(rest[: len(flat(pieces))], pieces)
        out_ref, gain_sum, shift_sum, weight, inner, sems = rest[len(flat(pieces)) :]
        at = pl.program_id(0)

        @pl.when(at == 0)
        def _():
            start_loads(where_ref, own_ref, piece_refs, strips, weight, sems, "row")

        wait_rows(where_ref, weight, sems, at, share)
        rows = pl.ds(aligned(jnp.bitwise_xor(where_ref[1], at) * share, share), share)
        inner[:, rows] = (
            product(proj_ref[0], weight[rows, :width], NT)
            + product(proj_ref[1], weight[rows, width : 2 * width], NT)
            + product(proj_ref[2], weight[rows, 2 * width :], NT)
        )

        @pl.when(at == groups - 1)
        def _():
            normed, inv_std = center(image_ref[...].astype(jnp.float32))
            grad_in = inner[...]
            gain_sum[...] = column_sum(grad_in * normed)
            shift_sum[...] = column_sum(grad_in)
            out_ref[...] = (
                res_ref[...] + center_back(grad_in, normed, inv_std, gain_ref[...])
            ).astype(jnp.bfloat16)

    full = lambda at, _: (0, 0)
    line = pl.BlockSpec((1, width), full)
    square = pl.BlockSpec((tokens, width), full)
    return pl.pallas_call(
        body,
        grid_spec=pltpu.PrefetchScalarGridSpec(
            num_scalar_prefetch=1,
            grid=(groups,),
            in_specs=[pl.BlockSpec((3, tokens, width), lambda at, _: (0, 0, 0))]
            + [square, square, line]
            + [ANY] * (1 + len(flat(pieces))),
            out_specs=[square, line, line],
            scratch_shapes=[
                pltpu.VMEM((width, wide), jnp.bfloat16),
                pltpu.VMEM((tokens, width), jnp.float32),
                pltpu.SemaphoreType.DMA((groups,)),
            ],
        ),
        out_shape=[
            jax.ShapeDtypeStruct((tokens, width), jnp.bfloat16),
            jax.ShapeDtypeStruct((1, width), jnp.float32),
            jax.ShapeDtypeStruct((1, width), jnp.float32),
        ],
        cost_estimate=cost(2 * tokens * width * wide, 2 * width * wide),
        compiler_params=params(),
        name="qkv_backward",
    )(where, grad_proj, image, grad_res, gain, own, *flat(pieces))


def attention_forward(projected):
    tokens, triple = projected.shape
    width = triple // 3
    count = width // PAIR

    def body(query_ref, key_ref, value_ref, mixed_ref, total_ref):
        values = value_ref[...].T
        halves = []
        for half in range(PAIR // HD):
            lanes = slice(half * HD, (half + 1) * HD)
            scores = product(key_ref[:, lanes], query_ref[:, lanes], NT)
            top = jnp.max(scores, axis=0, keepdims=True)
            weights = jnp.exp(scores - top)
            total = jnp.sum(weights, axis=0, keepdims=True)
            halves.append(product(values[lanes, :], weights.astype(jnp.bfloat16)) / total)
            total_ref[0, half : half + 1, :] = top + jnp.log(total)
        mixed_ref[...] = jnp.concatenate(halves, axis=0).T.astype(jnp.bfloat16)

    def spec(part):
        return pl.BlockSpec((tokens, PAIR), lambda at: (0, part * count + at))

    return pl.pallas_call(
        body,
        grid=(count,),
        in_specs=[spec(0), spec(1), spec(2)],
        out_specs=[
            pl.BlockSpec((tokens, PAIR), lambda at: (0, at)),
            pl.BlockSpec((1, PAIR // HD, tokens), lambda at: (at, 0, 0)),
        ],
        out_shape=[
            jax.ShapeDtypeStruct((tokens, width), jnp.bfloat16),
            jax.ShapeDtypeStruct((count, PAIR // HD, tokens), jnp.float32),
        ],
        cost_estimate=cost(16 * tokens * tokens * width, 8 * tokens * width),
        compiler_params=params(),
        name="attention_forward",
    )(projected, projected, projected)


def attention_backward(projected, grad_mixed, totals):
    tokens, triple = projected.shape
    width = triple // 3
    count = width // PAIR

    def body(query_ref, key_ref, value_ref, grad_ref, total_ref, out_ref, sq_ref, sv_ref):
        keys = key_ref[...].T
        outs_q, outs_k, outs_v = [], [], []
        for half in range(PAIR // HD):
            lanes = slice(half * HD, (half + 1) * HD)
            scores = product(key_ref[:, lanes], query_ref[:, lanes], NT)
            probs = jnp.exp(scores - total_ref[0, half : half + 1, :])
            grad_probs = product(value_ref[:, lanes], grad_ref[:, lanes], NT)
            row_dot = jnp.sum(probs * grad_probs, axis=0, keepdims=True)
            grad_scores = (probs * (grad_probs - row_dot)).astype(jnp.bfloat16)
            outs_q.append(product(keys[lanes, :], grad_scores))
            outs_k.append(product(grad_scores, query_ref[:, lanes]))
            outs_v.append(product(probs.astype(jnp.bfloat16), grad_ref[:, lanes]))
        grad_query = jnp.concatenate(outs_q, axis=0).T * 0.125
        grad_value = jnp.concatenate(outs_v, axis=1)
        out_ref[0] = grad_query.astype(jnp.bfloat16)
        out_ref[1] = jnp.concatenate(outs_k, axis=1).astype(jnp.bfloat16)
        out_ref[2] = grad_value.astype(jnp.bfloat16)
        sq_ref[...] = column_sum(grad_query)
        sv_ref[...] = column_sum(grad_value)

    def spec(part):
        return pl.BlockSpec((tokens, PAIR), lambda at: (0, part * count + at))

    block = pl.BlockSpec((tokens, PAIR), lambda at: (0, at))
    line = pl.BlockSpec((1, PAIR), lambda at: (0, at))
    return pl.pallas_call(
        body,
        grid=(count,),
        in_specs=[spec(0), spec(1), spec(2), block]
        + [pl.BlockSpec((1, PAIR // HD, tokens), lambda at: (at, 0, 0))],
        out_specs=[pl.BlockSpec((3, tokens, PAIR), lambda at: (0, 0, at)), line, line],
        out_shape=[jax.ShapeDtypeStruct((3, tokens, width), jnp.bfloat16)]
        + [jax.ShapeDtypeStruct((1, width), jnp.float32)] * 2,
        cost_estimate=cost(40 * tokens * tokens * width, 16 * tokens * width),
        compiler_params=params(),
        name="attention_backward",
    )(projected, projected, projected, grad_mixed, totals)


def weight_grads(where, pairs):
    tokens, rows = pairs[0][0].shape
    sizes = [pair[4] for pair in pairs]
    parts = [pair[2].shape[0] if pair[2].ndim == 3 else 1 for pair in pairs]
    spans = [size * part for size, part in zip(sizes, parts)]
    width = sum(spans)
    step = 256
    count = rows // step
    half = count // 2
    operands, in_specs = [], []
    for left, left_pair, right, right_pair, _ in pairs:
        operands += [left, left_pair, right, right_pair]
        in_specs += [pl.BlockSpec((tokens, step), lambda at, _: (0, at))] * 2 + [ANY] * 2

    def body(where_ref, *refs):
        ins = refs[: len(operands)]
        send_a, keep_a, send_b, keep_b = refs[len(operands) : len(operands) + 4]
        joined, sems = refs[len(operands) + 4 : -1], refs[-1]
        at = pl.program_id(0)

        @pl.when(at == 0)
        def _():
            for pair, (size, part_count) in enumerate(zip(sizes, parts)):
                for side in range(2):
                    source = ins[4 * pair + 2 + side]
                    for which in range(4):
                        block = jnp.bitwise_xor(where_ref[0], 2 * which)
                        columns = pl.ds(aligned(block * size, LANES), size)
                        for part in range(part_count):
                            begin = (which * part_count + part) * size
                            taken = (
                                source.at[part, :, columns]
                                if part_count > 1
                                else source.at[:, columns]
                            )
                            pltpu.make_async_copy(
                                taken,
                                joined[2 * pair + side].at[:, begin : begin + size],
                                sems.at[2 * pair + side],
                            ).start()
            for which in range(2 * len(pairs)):
                finish(joined[which], sems.at[which])

        results = []
        for pair in range(len(pairs)):
            total = product(ins[4 * pair][...], joined[2 * pair][...], TN)
            total = total + product(ins[4 * pair + 1][...], joined[2 * pair + 1][...], TN)
            results.append(total.astype(jnp.bfloat16))

        def put(targets):
            base = 0
            for pair, span in enumerate(spans):
                for which in range(4):
                    ref, slot = targets[which]
                    ref[slot, :, base : base + span] = results[pair][
                        :, which * span : (which + 1) * span
                    ]
                base += span

        @pl.when(at < half)
        def _():
            put([(keep_a, 0), (send_a, 0), (keep_a, 1), (send_a, 1)])

        @pl.when(at >= half)
        def _():
            put([(keep_b, 0), (keep_b, 1), (send_b, 0), (send_b, 1)])

    spec_a = pl.BlockSpec((2, step, width), lambda at, _: (0, jnp.minimum(at, half - 1), 0))
    spec_b = pl.BlockSpec((2, step, width), lambda at, _: (0, jnp.maximum(at - half, 0), 0))
    return pl.pallas_call(
        body,
        grid_spec=pltpu.PrefetchScalarGridSpec(
            num_scalar_prefetch=1,
            grid=(count,),
            in_specs=in_specs,
            out_specs=[spec_a, spec_a, spec_b, spec_b],
            scratch_shapes=[
                pltpu.VMEM((tokens, 4 * span), jnp.bfloat16) for span in spans for _ in range(2)
            ]
            + [pltpu.SemaphoreType.DMA((2 * len(pairs),))],
        ),
        out_shape=[jax.ShapeDtypeStruct((2, rows // 2, width), jnp.bfloat16)] * 4,
        cost_estimate=cost(16 * rows * tokens * width, 8 * rows * width + 4 * tokens * rows),
        compiler_params=params(),
        name="weight_grads",
    )(where, *operands)


def pack_blocks(where, qkv, out, up, down, vectors):
    rows, _ = qkv.shape
    size = up.shape[1] // BLOCKS
    lengths = [vec.shape[1] for vec in vectors]
    row = 3 * LANES

    def body(where_ref, query_ref, key_ref, value_ref, out_ref, up_ref, down_ref, *rest):
        vector_refs = rest[: len(vectors)]
        first_ref, second_ref, third_ref = rest[len(vectors) :]
        first_ref[:rows, :LANES] = query_ref[...]
        first_ref[:rows, LANES : 2 * LANES] = key_ref[...]
        first_ref[:rows, 2 * LANES :] = value_ref[...]
        flat_vectors = jnp.concatenate([ref[...].astype(jnp.float32) for ref in vector_refs], axis=1)
        total = flat_vectors.shape[1]
        lines = [flat_vectors[:, at : at + row] for at in range(0, total, row)]
        lines.append(jnp.zeros((16 - len(lines), row), jnp.float32))
        first_ref[rows:, :] = jnp.concatenate(lines, axis=0).astype(jnp.bfloat16)
        second_ref[:, :size] = up_ref[...]
        second_ref[:, size:] = out_ref[...]
        third_ref[...] = down_ref[...]

    def mine(array, width, part=0):
        return pl.BlockSpec(
            (array.shape[0], width),
            lambda at, where_ref: (0, part * BLOCKS + where_ref[0]),
        )

    whole = lambda shape: pl.BlockSpec(shape, lambda at, _: (0, 0))
    shapes = [(rows + 16, row), (rows, size + LANES), (down.shape[0], LANES)]
    return pl.pallas_call(
        body,
        grid_spec=pltpu.PrefetchScalarGridSpec(
            num_scalar_prefetch=1,
            grid=(1,),
            in_specs=[mine(qkv, LANES, part) for part in range(3)]
            + [mine(out, LANES), mine(up, size), mine(down, LANES)]
            + [whole((1, length)) for length in lengths],
            out_specs=[whole(shape) for shape in shapes],
        ),
        out_shape=[jax.ShapeDtypeStruct(shape, jnp.bfloat16) for shape in shapes],
        compiler_params=params(),
        name="pack_blocks",
    )(where, qkv, qkv, qkv, out, up, down, *vectors)


def unpack_vectors(where, sources, rows, lengths, pair_at, width):
    groups = len(sources)
    row = sources[0].shape[1]
    outs = [3 * width if at == pair_at else length * groups for at, length in enumerate(lengths)]

    def body(where_ref, *refs):
        source_refs, out_refs = refs[:groups], refs[groups:]
        out_refs[pair_at][...] = jnp.zeros((1, 3 * width), jnp.float32)
        for hop in range(groups):
            block = source_refs[hop][...].astype(jnp.float32)
            owner = jnp.bitwise_xor(where_ref[1], hop)
            place = 0
            for which, length in enumerate(lengths):
                start = owner * length
                if which == pair_at:
                    start = start + jnp.where(start >= width, width, 0)
                for begin in range(0, length, LANES):
                    line, lane = (place + begin) // row, (place + begin) % row
                    target = pl.ds(aligned(start + begin, LANES), LANES)
                    out_refs[which][:, target] = block[line : line + 1, lane : lane + LANES]
                place += length

    return pl.pallas_call(
        body,
        grid_spec=pltpu.PrefetchScalarGridSpec(
            num_scalar_prefetch=1,
            grid=(1,),
            in_specs=[pl.BlockSpec((16, row), lambda at, _: (rows // 16, 0))] * groups,
            out_specs=[pl.BlockSpec((1, size), lambda at, _: (0, 0)) for size in outs],
        ),
        out_shape=[jax.ShapeDtypeStruct((1, size), jnp.float32) for size in outs],
        compiler_params=params(),
        name="unpack_vectors",
    )(where, *sources)


def pack_sums(vectors, groups):
    total = sum(vec.shape[1] for vec in vectors) // groups

    def body(*refs):
        for owner in range(groups):
            pieces = []
            for ref in refs[:-1]:
                length = ref.shape[1] // groups
                pieces.append(ref[:, owner * length : (owner + 1) * length])
            refs[-1][owner : owner + 1, :] = jnp.concatenate(pieces, axis=1)

    return pl.pallas_call(
        body,
        out_shape=jax.ShapeDtypeStruct((groups, total), jnp.float32),
        compiler_params=params(),
        name="pack_sums",
    )(*vectors)


def unpack_sums(where, first, second, lengths):
    groups, total = first.shape

    def body(where_ref, first_ref, second_ref, *outs):
        line = jnp.zeros((1, total), jnp.float32)
        for owner in range(groups):
            both = first_ref[owner : owner + 1, :] + second_ref[owner : owner + 1, :]
            line = jnp.where(where_ref[1] == owner, both, line)
        place = 0
        for out, length in zip(outs, lengths):
            out[...] = line[:, place : place + length]
            place += length

    whole = pl.BlockSpec((groups, total), lambda at, _: (0, 0))
    return pl.pallas_call(
        body,
        grid_spec=pltpu.PrefetchScalarGridSpec(
            num_scalar_prefetch=1,
            grid=(1,),
            in_specs=[whole, whole],
            out_specs=[pl.BlockSpec((1, length), lambda at, _: (0, 0)) for length in lengths],
        ),
        out_shape=[jax.ShapeDtypeStruct((1, length), jnp.float32) for length in lengths],
        compiler_params=params(),
        name="unpack_sums",
    )(where, first, second)


def finish_blocks(blocks):
    count, rows, size = blocks.shape
    step = min(rows, 128)

    def body(in_ref, out_ref):
        for at in range(count):
            out_ref[:, at * size : (at + 1) * size] = in_ref[at].astype(jnp.float32)

    return pl.pallas_call(
        body,
        grid=(rows // step,),
        in_specs=[pl.BlockSpec((count, step, size), lambda at: (0, at, 0))],
        out_specs=pl.BlockSpec((step, count * size), lambda at: (at, 0)),
        out_shape=jax.ShapeDtypeStruct((rows, count * size), jnp.float32),
        compiler_params=params(),
        name="finish_blocks",
    )(blocks)


def finish_grads(where, pieces, strips):
    rows = pieces[0].shape[0]
    step = min(rows, 128)
    totals = {}
    for _, size, out, base in strips:
        totals[out] = max(totals.get(out, 0), base + size * BLOCKS)

    def body(where_ref, *refs):
        piece_refs, out_refs = refs[:BLOCKS], refs[BLOCKS:]
        for at in range(BLOCKS):
            block = jnp.bitwise_xor(where_ref[0], at)
            for start, size, out, base in strips:
                target = pl.ds(aligned(base + block * size, LANES), size)
                out_refs[out][:, target] = piece_refs[at][:, start : start + size].astype(
                    jnp.float32
                )

    return pl.pallas_call(
        body,
        grid_spec=pltpu.PrefetchScalarGridSpec(
            num_scalar_prefetch=1,
            grid=(rows // step,),
            in_specs=[
                pl.BlockSpec((step, piece.shape[1]), lambda at, _: (at, 0)) for piece in pieces
            ],
            out_specs=[
                pl.BlockSpec((step, totals[out]), lambda at, _: (at, 0)) for out in sorted(totals)
            ],
        ),
        out_shape=[
            jax.ShapeDtypeStruct((rows, totals[out]), jnp.float32) for out in sorted(totals)
        ],
        compiler_params=params(),
        name="finish_grads",
    )(where, *pieces)


def exchange(tensor, mask, axis="rep"):
    size = lax.axis_size(axis)
    return lax.ppermute(tensor, axis, [(at, at ^ mask) for at in range(size)])


def tie(value, *others):
    return lax.optimization_barrier((value, others))[0]


def all_hops(block):
    return [exchange(block, hop, "grp") for hop in range(1, lax.axis_size("grp"))]


def spread(own):
    by_x = exchange(own, 2)
    by_y = exchange(own, 4)
    half = own.shape[0] // 2
    sent = (by_x[:half], by_y[half:])
    top = exchange(sent[0], 4)
    bottom = exchange(sent[1], 2)
    pieces = []
    for piece in ((own,), (by_x,), (by_y,), (top, bottom)):
        pieces += [piece, tuple(exchange(array, 1) for array in piece)]
    return pieces, sent, (top, bottom)


def add_rounded(left, right):
    return (left.astype(jnp.float32) + right.astype(jnp.float32)).astype(jnp.bfloat16)


def first_sends(parts):
    return exchange(parts[0], 2), exchange(parts[2], 4)


def second_sends(parts, got):
    keep_a, keep_b = parts[1], parts[3]
    got_a, got_b = got
    next_a = exchange(add_rounded(keep_a[1], got_a[1]), 4)
    next_b = exchange(add_rounded(keep_b[1], got_b[1]), 2)
    rest_a = add_rounded(keep_a[0], got_a[0])
    rest_b = add_rounded(keep_b[0], got_b[0])
    return (rest_a, rest_b), (next_a, next_b)


def block_total(rest, got):
    total = jnp.concatenate([add_rounded(*pair) for pair in zip(rest, got)], axis=0)
    mask = BLOCKS
    while mask < lax.axis_size("rep"):
        total = add_rounded(total, exchange(total, mask))
        mask *= 2
    return total


def grp_sum(total):
    groups = lax.axis_size("grp")
    share = total.shape[0] // groups
    place = lax.axis_index("grp")
    sent = [
        lax.dynamic_slice_in_dim(total, (place ^ hop) * share, share, 0) for hop in range(groups)
    ]
    got = [exchange(sent[hop], hop, "grp") for hop in range(1, groups)]
    return sent[0], got


def sum_rounded(own, got):
    total = own.astype(jnp.float32)
    for other in got:
        total = total + other.astype(jnp.float32)
    return total.astype(jnp.bfloat16)


def layer(
    images,
    cotangent,
    ln1_gain,
    ln1_shift,
    qkv_weight,
    qv_bias,
    out_weight,
    out_bias,
    ln2_gain,
    ln2_shift,
    fc1_weight,
    fc1_bias,
    fc2_weight,
    fc2_bias,
):
    n_grp = lax.axis_size("grp")
    place = jnp.bitwise_and(lax.axis_index("rep"), BLOCKS - 1)
    where = jnp.stack([place, lax.axis_index("grp")])
    rows, width = out_weight.shape
    hidden_block = fc1_weight.shape[1] // BLOCKS

    vectors = (ln1_gain, ln1_shift, qv_bias, out_bias, ln2_gain, ln2_shift, fc1_bias, fc2_bias)
    sizes = [vec.shape[0] for vec in vectors]
    block_a, block_b, block_c = pack_blocks(
        where,
        qkv_weight,
        out_weight,
        fc1_weight,
        fc2_weight,
        [vec.reshape(1, -1) for vec in vectors],
    )
    got_a = all_hops(block_a)
    pieces_a, sent_a, _ = spread(jnp.concatenate([got[:rows] for got in got_a]))
    got_b = tie(all_hops(tie(block_b, got_a)), sent_a)
    pieces_b, sent_b, _ = spread(jnp.concatenate(got_b))
    got_c = tie(all_hops(tie(block_c, got_b)), sent_b)
    pieces_c, _, _ = spread(jnp.concatenate(got_c))
    gain_1, shift_1, bias_in, bias_attn, gain_2, shift_2, bias_up, bias_down = unpack_vectors(
        where, [block_a] + got_a, rows, sizes, 2, width
    )

    image = images[0]
    grad_block = cotangent[0]
    cot_pair = exchange(grad_block, 1)

    normed_in, projected = qkv_forward(where, image, gain_1, shift_1, bias_in, qkv_weight, pieces_a)
    normed_pair = exchange(normed_in, 1)
    attended, totals = attention_forward(projected)
    attended_pair = exchange(attended, 1)
    residual, normed_mid = out_forward(
        where, image, attended, bias_attn, gain_2, shift_2, out_weight, pieces_b, hidden_block
    )
    mid_pair = exchange(normed_mid, 1)
    active, slope = up_forward(where, normed_mid, bias_up, fc1_weight, pieces_b)
    active_pair = exchange(active, 1)

    grad_pre, sum_up = down_backward(where, grad_block, slope, fc2_weight, pieces_c)
    pre_pair = exchange(grad_pre, 1)
    down_parts = weight_grads(
        tie(where, grad_pre), [(active, active_pair, grad_block, cot_pair, LANES)]
    )
    down_got = first_sends(down_parts)
    middle = middle_backward(
        tie(where, down_parts),
        grad_pre,
        grad_block,
        residual,
        gain_2,
        fc1_weight,
        out_weight,
        pieces_b,
        hidden_block,
    )
    grad_res, grad_res_b, grad_attended, sum_gain_2, sum_shift_2, sum_res, sum_top = middle
    res_pair = exchange(grad_res_b, 1)
    down_rest, down_got = second_sends(down_parts, tie(down_got, grad_res))
    up_parts = weight_grads(
        tie(where, grad_res, down_rest),
        [(normed_mid, mid_pair, grad_pre, pre_pair, hidden_block)],
    )
    up_got = first_sends(up_parts)
    down_total = block_total(down_rest, tie(down_got, up_parts))
    down_own = lax.psum_scatter(down_total, "grp", scatter_dimension=0, tiled=True)
    grad_proj, sum_query, sum_value = attention_backward(
        projected, tie(grad_attended, up_parts, down_total), totals
    )
    proj_pair = exchange(grad_proj, 1)
    up_rest, up_got = second_sends(up_parts, tie(up_got, grad_proj))
    attn_parts = weight_grads(
        tie(where, up_rest),
        [
            (normed_in, normed_pair, grad_proj, proj_pair, LANES),
            (attended, attended_pair, grad_res_b, res_pair, LANES),
        ],
    )
    attn_got = first_sends(attn_parts)
    down_blocks = lax.all_gather(tie(down_own, attn_parts), "rep", axis=0, tiled=False)[:BLOCKS]
    up_total = block_total(up_rest, tie(up_got, attn_parts))
    up_own = lax.psum_scatter(up_total, "grp", scatter_dimension=0, tiled=True)
    input_grad, sum_gain_1, sum_shift_1 = qkv_backward(
        tie(where, attn_parts, up_total),
        grad_proj,
        image,
        grad_res,
        gain_1,
        qkv_weight,
        pieces_a,
    )
    sums = pack_sums(
        [
            sum_gain_1,
            sum_shift_1,
            jnp.concatenate([sum_query, sum_value], axis=1),
            sum_res,
            sum_gain_2,
            sum_shift_2,
            sum_up,
            sum_top,
        ],
        n_grp,
    )
    got = exchange(sums, 1)
    block_out = down_forward(
        tie(where, input_grad, sums), residual, active, bias_down, fc2_weight, pieces_c
    )
    sums = sums + tie(got, block_out)
    up_blocks = lax.all_gather(tie(up_own, block_out), "rep", axis=0, tiled=False)[:BLOCKS]
    attn_rest, attn_got = second_sends(attn_parts, tie(attn_got, block_out))
    sums = sums + tie(exchange(sums, 2), attn_rest)
    mask = BLOCKS
    while mask < lax.axis_size("rep"):
        sums = sums + exchange(sums, mask)
        mask *= 2
    attn_total = block_total(attn_rest, attn_got)
    own, got = grp_sum(attn_total)
    sums = sums + tie(exchange(sums, 4), attn_total)
    grad_down = finish_blocks(tie(down_blocks, attn_total))
    own = sum_rounded(own, tie(got, grad_down))
    mask = 1
    while mask * 2 < n_grp:
        sums = sums + tie(exchange(sums, mask, "grp"), own)
        mask *= 2
    by_x = exchange(own, 2)
    by_y = exchange(own, 4)
    both = exchange(by_x, 4)
    last = exchange(sums, mask, "grp")
    attn_pieces = []
    for piece in (own, by_x, by_y, both):
        attn_pieces += [piece, exchange(piece, 1)]
    grad_up = finish_blocks(tie(up_blocks, by_x, by_y))
    grad_qkv, grad_out = finish_grads(
        where,
        attn_pieces,
        [(at * LANES, LANES, 0, at * width) for at in range(3)] + [(3 * LANES, LANES, 1, 0)],
    )
    sums = [vec.reshape(-1) for vec in unpack_sums(where, sums, last, sizes)]
    return (
        block_out[None],
        input_grad[None],
        sums[0],
        sums[1],
        grad_qkv,
        sums[2],
        grad_out,
        sums[3],
        sums[4],
        sums[5],
        grad_up,
        sums[6],
        grad_down,
        sums[7],
    )


def solution(mesh):
    return jax.shard_map(
        layer,
        mesh=mesh,
        in_specs=(
            P(("rep", "grp"), None, None),
            P(("rep", "grp"), None, None),
            P("grp"),
            P("grp"),
            P("grp", None),
            P("grp"),
            P("grp", None),
            P("grp"),
            P("grp"),
            P("grp"),
            P("grp", None),
            P("grp"),
            P("grp", None),
            P("grp"),
        ),
        out_specs=(
            P(("rep", "grp"), None, None),
            P(("rep", "grp"), None, None),
            P("grp"),
            P("grp"),
            P("grp", None),
            P("grp"),
            P("grp", None),
            P("grp"),
            P("grp"),
            P("grp"),
            P("grp", None),
            P("grp"),
            P("grp", None),
            P("grp"),
        ),
        check_vma=False,
    )
```

```python
import jax
import jax.numpy as jnp
from jax import lax
from jax.experimental import pallas as pl
from jax.experimental.pallas import tpu as pltpu
from jax.sharding import PartitionSpec as P


BLOCKS = 8
ROW, PART, BLOCK = range(3)
LANES = 128
TILE = 512
HD = 64
PAIR = 128
EPS = 1e-06

root_half = 0.7071067811865476
inv_root_tau = 0.3989422804014327

NN = (((1,), (0,)), ((), ()))
NT = (((1,), (1,)), ((), ()))
TN = (((0,), (0,)), ((), ()))
ANY = pl.BlockSpec(memory_space=pl.ANY)


def product(left, right, dims=NN):
    return lax.dot_general(left, right, dims, preferred_element_type=jnp.float32)


def aligned(start, unit):
    return pl.multiple_of(start, unit)


def params(**extra):
    return pltpu.CompilerParams(vmem_limit_bytes=60 << 20, **extra)


def cost(flops, moved):
    return pl.CostEstimate(flops=int(flops), bytes_accessed=int(moved), transcendentals=0)


def start_loads(where, own, pieces, strips, target, sems, mode):
    share = own.shape[0]
    groups = target.shape[0] // share
    mine = where[1]

    def go(source, rows, columns, key):
        pltpu.make_async_copy(source, target.at[rows, columns], sems.at[key]).start()

    own_rows = pl.ds(aligned(mine * share, share), share)
    if mode == ROW:
        pltpu.make_async_copy(own, target.at[own_rows, :], sems.at[0]).start()
    for which, (source, size, base) in enumerate(strips):
        for at in range(BLOCKS):
            block = jnp.bitwise_xor(where[0], at)
            columns = pl.ds(aligned(base + block * size, LANES), size)
            key = which if mode == PART else at
            if mode != ROW:
                go(own.at[:, columns], own_rows, columns, key)
            for hop in range(1, groups):
                first = jnp.bitwise_xor(mine, hop) * share
                low = 0
                for ref in pieces[at]:
                    high = low + ref.shape[0]
                    begin, end = max(low, (hop - 1) * share), min(high, hop * share)
                    if begin < end:
                        shift = begin - (hop - 1) * share
                        rows = pl.ds(aligned(first + shift, 16), end - begin)
                        go(
                            ref.at[begin - low : end - low, source : source + size],
                            rows,
                            columns,
                            hop if mode == ROW else key,
                        )
                    low = high


def finish(region, sem):
    pltpu.make_async_copy(region, region, sem).wait()


def wait_rows(where, target, sems, hop, share):
    rows = pl.ds(aligned(jnp.bitwise_xor(where[1], hop) * share, share), share)
    finish(target.at[rows, :], sems.at[hop])


def flat(pieces):
    return [array for piece in pieces for array in piece]


def regroup(refs, pieces):
    grouped, at = [], 0
    for piece in pieces:
        grouped.append(refs[at : at + len(piece)])
        at += len(piece)
    return grouped


def center(values):
    mean = jnp.mean(values, axis=-1, keepdims=True)
    centred = values - mean
    inv_std = lax.rsqrt(jnp.mean(centred * centred, axis=-1, keepdims=True) + EPS)
    return centred * inv_std, inv_std


def center_back(grad_out, normed, inv_std, gain):
    grad_hat = grad_out * gain
    return inv_std * (
        grad_hat
        - jnp.mean(grad_hat, axis=-1, keepdims=True)
        - normed * jnp.mean(grad_hat * normed, axis=-1, keepdims=True)
    )


def column_sum(values):
    return jnp.sum(values, axis=0, keepdims=True)


def qkv_forward(where, image, gain, shift, bias, own, pieces):
    tokens, width = image.shape
    wide = own.shape[1]
    per = width // TILE
    strips = [(part * LANES, LANES, part * width) for part in range(3)]

    def body(where_ref, image_ref, gain_ref, shift_ref, bias_ref, own_ref, *rest):
        piece_refs = regroup(rest[: len(flat(pieces))], pieces)
        normed_ref, out_ref, weight, sems = rest[len(flat(pieces)) :]
        at = pl.program_id(0)

        @pl.when(at == 0)
        def _():
            start_loads(where_ref, own_ref, piece_refs, strips, weight, sems, PART)
            normed, _ = center(image_ref[...].astype(jnp.float32))
            normed_ref[...] = (normed * gain_ref[...] + shift_ref[...]).astype(jnp.bfloat16)

        for part in range(3):

            @pl.when(at == part * per)
            def _(part=part):
                finish(weight.at[:, part * width : (part + 1) * width], sems.at[part])

        columns = pl.ds(aligned(at * TILE, TILE), TILE)
        total = product(normed_ref[...], weight[:, columns]) + bias_ref[...]
        scale = jnp.where(at < per, 0.125, 1.0)
        out_ref[...] = (total * scale).astype(jnp.bfloat16)

    full = lambda at, _: (0, 0)
    return pl.pallas_call(
        body,
        grid_spec=pltpu.PrefetchScalarGridSpec(
            num_scalar_prefetch=1,
            grid=(wide // TILE,),
            in_specs=[
                pl.BlockSpec((tokens, width), full),
                pl.BlockSpec((1, width), full),
                pl.BlockSpec((1, width), full),
                pl.BlockSpec((1, TILE), lambda at, _: (0, at)),
            ]
            + [ANY] * (1 + len(flat(pieces))),
            out_specs=[
                pl.BlockSpec((tokens, width), full),
                pl.BlockSpec((tokens, TILE), lambda at, _: (0, at)),
            ],
            scratch_shapes=[
                pltpu.VMEM((width, wide), jnp.bfloat16),
                pltpu.SemaphoreType.DMA((3,)),
            ],
        ),
        out_shape=[
            jax.ShapeDtypeStruct((tokens, width), jnp.bfloat16),
            jax.ShapeDtypeStruct((tokens, wide), jnp.bfloat16),
        ],
        cost_estimate=cost(2 * tokens * width * wide, 2 * width * wide),
        compiler_params=params(),
    )(where, image, gain, shift, bias, own, *flat(pieces))


def out_forward(where, image, attended, bias, gain, shift, own, pieces, source):
    tokens, width = image.shape
    share = own.shape[0]
    groups = width // share
    chunk = 256

    def body(where_ref, image_ref, attended_ref, bias_ref, gain_ref, shift_ref, own_ref, *rest):
        piece_refs = regroup(rest[: len(flat(pieces))], pieces)
        residual_ref, normed_ref, weight, sems = rest[len(flat(pieces)) :]
        start_loads(where_ref, own_ref, piece_refs, [(source, LANES, 0)], weight, sems, ROW)
        for hop in range(groups):
            wait_rows(where_ref, weight, sems, hop, share)

        @pl.loop(0, width // chunk)
        def _(at):
            columns = pl.ds(aligned(at * chunk, chunk), chunk)
            residual_ref[:, columns] = (
                image_ref[:, columns].astype(jnp.float32)
                + product(attended_ref[...], weight[:, columns])
                + bias_ref[:, columns]
            )

        normed, _ = center(residual_ref[...])
        normed_ref[...] = (normed * gain_ref[...] + shift_ref[...]).astype(jnp.bfloat16)

    full = lambda at, _: (0, 0)
    return pl.pallas_call(
        body,
        grid_spec=pltpu.PrefetchScalarGridSpec(
            num_scalar_prefetch=1,
            grid=(1,),
            in_specs=[pl.BlockSpec((tokens, width), full)] * 2
            + [pl.BlockSpec((1, width), full)] * 3
            + [ANY] * (1 + len(flat(pieces))),
            out_specs=[pl.BlockSpec((tokens, width), full)] * 2,
            scratch_shapes=[
                pltpu.VMEM((width, width), jnp.bfloat16),
                pltpu.SemaphoreType.DMA((groups,)),
            ],
        ),
        out_shape=[
            jax.ShapeDtypeStruct((tokens, width), jnp.float32),
            jax.ShapeDtypeStruct((tokens, width), jnp.bfloat16),
        ],
        cost_estimate=cost(2 * tokens * width * width, 2 * width * width),
        compiler_params=params(),
    )(where, image, attended, bias, gain, shift, own, *flat(pieces))


def up_forward(where, normed, bias, own, pieces):
    tokens, width = normed.shape
    wide = own.shape[1]
    size = wide // BLOCKS

    def body(where_ref, normed_ref, bias_ref, own_ref, *rest):
        piece_refs = regroup(rest[: len(flat(pieces))], pieces)
        active_ref, slope_ref, weight, sems = rest[len(flat(pieces)) :]
        at = pl.program_id(0)

        @pl.when(at == 0)
        def _():
            start_loads(where_ref, own_ref, piece_refs, [(0, size, 0)], weight, sems, BLOCK)

        columns = pl.ds(aligned(jnp.bitwise_xor(where_ref[0], at) * size, size), size)
        finish(weight.at[:, columns], sems.at[at])
        pre_act = product(normed_ref[...], weight[:, columns]) + bias_ref[...]
        cdf = 0.5 * (1.0 + lax.erf(pre_act * root_half))
        density = jnp.exp(-0.5 * pre_act * pre_act) * inv_root_tau
        active_ref[...] = (pre_act * cdf).astype(jnp.bfloat16)
        slope_ref[...] = (cdf + pre_act * density).astype(jnp.bfloat16)

    full = lambda at, _: (0, 0)
    mine = lambda at, where_ref: (0, jnp.bitwise_xor(where_ref[0], at))
    return pl.pallas_call(
        body,
        grid_spec=pltpu.PrefetchScalarGridSpec(
            num_scalar_prefetch=1,
            grid=(BLOCKS,),
            in_specs=[pl.BlockSpec((tokens, width), full), pl.BlockSpec((1, size), mine)]
            + [ANY] * (1 + len(flat(pieces))),
            out_specs=[pl.BlockSpec((tokens, size), mine)] * 2,
            scratch_shapes=[
                pltpu.VMEM((width, wide), jnp.bfloat16),
                pltpu.SemaphoreType.DMA((BLOCKS,)),
            ],
        ),
        out_shape=[jax.ShapeDtypeStruct((tokens, wide), jnp.bfloat16)] * 2,
        cost_estimate=cost(2 * tokens * width * wide, 2 * width * wide),
        compiler_params=params(),
    )(where, normed, bias, own, *flat(pieces))


def down_forward(where, residual, active, bias, own, pieces):
    tokens, wide = active.shape
    width = residual.shape[1]
    share = own.shape[0]
    groups = wide // share
    chunk = 256

    def body(where_ref, residual_ref, active_ref, bias_ref, own_ref, *rest):
        piece_refs = regroup(rest[: len(flat(pieces))], pieces)
        out_ref, weight, sems = rest[len(flat(pieces)) :]
        at = pl.program_id(0)

        @pl.when(at == 0)
        def _():
            start_loads(where_ref, own_ref, piece_refs, [(0, LANES, 0)], weight, sems, ROW)
            for hop in range(groups):
                wait_rows(where_ref, weight, sems, hop, share)

        columns = pl.ds(aligned(at * chunk, chunk), chunk)
        out_ref[...] = (
            residual_ref[...] + product(active_ref[...], weight[:, columns]) + bias_ref[...]
        ).astype(jnp.bfloat16)

    block = lambda at, _: (0, at)
    return pl.pallas_call(
        body,
        grid_spec=pltpu.PrefetchScalarGridSpec(
            num_scalar_prefetch=1,
            grid=(width // chunk,),
            in_specs=[
                pl.BlockSpec((tokens, chunk), block),
                pl.BlockSpec((tokens, wide), lambda at, _: (0, 0)),
                pl.BlockSpec((1, chunk), block),
            ]
            + [ANY] * (1 + len(flat(pieces))),
            out_specs=pl.BlockSpec((tokens, chunk), block),
            scratch_shapes=[
                pltpu.VMEM((wide, width), jnp.bfloat16),
                pltpu.SemaphoreType.DMA((groups,)),
            ],
        ),
        out_shape=jax.ShapeDtypeStruct((tokens, width), jnp.bfloat16),
        cost_estimate=cost(2 * tokens * width * wide, 2 * width * wide),
        compiler_params=params(),
    )(where, residual, active, bias, own, *flat(pieces))


def down_backward(where, grad_block, slope, own, pieces):
    tokens, wide = slope.shape
    width = grad_block.shape[1]
    share = own.shape[0]
    groups = wide // share
    tile = min(TILE, share)
    per = share // tile

    def body(where_ref, grad_ref, slope_ref, own_ref, *rest):
        piece_refs = regroup(rest[: len(flat(pieces))], pieces)
        out_ref, sum_ref, weight, sems = rest[len(flat(pieces)) :]
        at = pl.program_id(0)

        @pl.when(at == 0)
        def _():
            start_loads(where_ref, own_ref, piece_refs, [(0, LANES, 0)], weight, sems, ROW)

        hop = at // per

        @pl.when(at % per == 0)
        def _():
            wait_rows(where_ref, weight, sems, hop, share)

        row = jnp.bitwise_xor(where_ref[1], hop) * share + (at % per) * tile
        rows = pl.ds(aligned(row, tile), tile)
        grad_pre = product(grad_ref[...], weight[rows, :], NT) * slope_ref[...].astype(jnp.float32)
        out_ref[...] = grad_pre.astype(jnp.bfloat16)
        sum_ref[...] = column_sum(grad_pre)

    mine = lambda at, where_ref: (0, jnp.bitwise_xor(where_ref[1], at // per) * per + at % per)
    return pl.pallas_call(
        body,
        grid_spec=pltpu.PrefetchScalarGridSpec(
            num_scalar_prefetch=1,
            grid=(wide // tile,),
            in_specs=[
                pl.BlockSpec((tokens, width), lambda at, _: (0, 0)),
                pl.BlockSpec((tokens, tile), mine),
            ]
            + [ANY] * (1 + len(flat(pieces))),
            out_specs=[pl.BlockSpec((tokens, tile), mine), pl.BlockSpec((1, tile), mine)],
            scratch_shapes=[
                pltpu.VMEM((wide, width), jnp.bfloat16),
                pltpu.SemaphoreType.DMA((groups,)),
            ],
        ),
        out_shape=[
            jax.ShapeDtypeStruct((tokens, wide), jnp.bfloat16),
            jax.ShapeDtypeStruct((1, wide), jnp.float32),
        ],
        cost_estimate=cost(2 * tokens * width * wide, 2 * width * wide),
        compiler_params=params(),
    )(where, grad_block, slope, own, *flat(pieces))


def middle_backward(where, grad_pre, grad_block, residual, gain, own_up, own_out, pieces, size):
    tokens, wide = grad_pre.shape
    width = grad_block.shape[1]
    share = own_up.shape[0]
    groups = width // share
    chunk = 256

    def body(where_ref, pre_ref, block_ref, residual_ref, gain_ref, up_ref, own_ref, *rest):
        piece_refs = regroup(rest[: len(flat(pieces))], pieces)
        (full_ref, half_ref, att_ref, gain_sum, shift_sum, res_sum, top_sum) = rest[
            len(flat(pieces)) : len(flat(pieces)) + 7
        ]
        weight, weight_out, middle, sems, out_sems = rest[len(flat(pieces)) + 7 :]
        at = pl.program_id(0)

        @pl.when(at == 0)
        def _():
            start_loads(where_ref, up_ref, piece_refs, [(0, size, 0)], weight, sems, ROW)
            start_loads(
                where_ref, own_ref, piece_refs, [(size, LANES, 0)], weight_out, out_sems, ROW
            )

        wait_rows(where_ref, weight, sems, at, share)
        rows = pl.ds(aligned(jnp.bitwise_xor(where_ref[1], at) * share, share), share)
        middle[:, rows] = product(pre_ref[...], weight[rows, :], NT)

        @pl.when(at == groups - 1)
        def _():
            normed, inv_std = center(residual_ref[...])
            grad_mid = middle[...]
            gain_sum[...] = column_sum(grad_mid * normed)
            shift_sum[...] = column_sum(grad_mid)
            top = block_ref[...].astype(jnp.float32)
            top_sum[...] = column_sum(top)
            grad_res = top + center_back(grad_mid, normed, inv_std, gain_ref[...])
            full_ref[...] = grad_res
            res_sum[...] = column_sum(grad_res)
            half_ref[...] = grad_res.astype(jnp.bfloat16)
            for hop in range(groups):
                wait_rows(where_ref, weight_out, out_sems, hop, share)

            @pl.loop(0, width // chunk)
            def _(step):
                part = pl.ds(aligned(step * chunk, chunk), chunk)
                att_ref[:, part] = product(half_ref[...], weight_out[part, :], NT).astype(
                    jnp.bfloat16
                )

    full = lambda at, _: (0, 0)
    line = pl.BlockSpec((1, width), full)
    square = pl.BlockSpec((tokens, width), full)
    return pl.pallas_call(
        body,
        grid_spec=pltpu.PrefetchScalarGridSpec(
            num_scalar_prefetch=1,
            grid=(groups,),
            in_specs=[pl.BlockSpec((tokens, wide), full), square, square, line]
            + [ANY] * (2 + len(flat(pieces))),
            out_specs=[square] * 3 + [line] * 4,
            scratch_shapes=[
                pltpu.VMEM((width, wide), jnp.bfloat16),
                pltpu.VMEM((width, width), jnp.bfloat16),
                pltpu.VMEM((tokens, width), jnp.float32),
                pltpu.SemaphoreType.DMA((groups,)),
                pltpu.SemaphoreType.DMA((groups,)),
            ],
        ),
        out_shape=[
            jax.ShapeDtypeStruct((tokens, width), jnp.float32),
            jax.ShapeDtypeStruct((tokens, width), jnp.bfloat16),
            jax.ShapeDtypeStruct((tokens, width), jnp.bfloat16),
        ]
        + [jax.ShapeDtypeStruct((1, width), jnp.float32)] * 4,
        cost_estimate=cost(2 * tokens * width * (wide + width), 2 * width * (wide + width)),
        compiler_params=params(),
    )(where, grad_pre, grad_block, residual, gain, own_up, own_out, *flat(pieces))


def qkv_backward(where, grad_proj, image, grad_res, gain, own, pieces):
    tokens, width = image.shape
    wide = own.shape[1]
    share = own.shape[0]
    groups = width // share
    strips = [(part * LANES, LANES, part * width) for part in range(3)]

    def body(where_ref, proj_ref, image_ref, res_ref, gain_ref, own_ref, *rest):
        piece_refs = regroup(rest[: len(flat(pieces))], pieces)
        out_ref, gain_sum, shift_sum, weight, inner, sems = rest[len(flat(pieces)) :]
        at = pl.program_id(0)

        @pl.when(at == 0)
        def _():
            start_loads(where_ref, own_ref, piece_refs, strips, weight, sems, ROW)

        wait_rows(where_ref, weight, sems, at, share)
        rows = pl.ds(aligned(jnp.bitwise_xor(where_ref[1], at) * share, share), share)
        inner[:, rows] = (
            product(proj_ref[0], weight[rows, :width], NT)
            + product(proj_ref[1], weight[rows, width : 2 * width], NT)
            + product(proj_ref[2], weight[rows, 2 * width :], NT)
        )

        @pl.when(at == groups - 1)
        def _():
            normed, inv_std = center(image_ref[...].astype(jnp.float32))
            grad_in = inner[...]
            gain_sum[...] = column_sum(grad_in * normed)
            shift_sum[...] = column_sum(grad_in)
            out_ref[...] = (
                res_ref[...] + center_back(grad_in, normed, inv_std, gain_ref[...])
            ).astype(jnp.bfloat16)

    full = lambda at, _: (0, 0)
    line = pl.BlockSpec((1, width), full)
    square = pl.BlockSpec((tokens, width), full)
    return pl.pallas_call(
        body,
        grid_spec=pltpu.PrefetchScalarGridSpec(
            num_scalar_prefetch=1,
            grid=(groups,),
            in_specs=[pl.BlockSpec((3, tokens, width), lambda at, _: (0, 0, 0))]
            + [square, square, line]
            + [ANY] * (1 + len(flat(pieces))),
            out_specs=[square, line, line],
            scratch_shapes=[
                pltpu.VMEM((width, wide), jnp.bfloat16),
                pltpu.VMEM((tokens, width), jnp.float32),
                pltpu.SemaphoreType.DMA((groups,)),
            ],
        ),
        out_shape=[
            jax.ShapeDtypeStruct((tokens, width), jnp.bfloat16),
            jax.ShapeDtypeStruct((1, width), jnp.float32),
            jax.ShapeDtypeStruct((1, width), jnp.float32),
        ],
        cost_estimate=cost(2 * tokens * width * wide, 2 * width * wide),
        compiler_params=params(),
    )(where, grad_proj, image, grad_res, gain, own, *flat(pieces))


def attention_forward(projected):
    tokens, triple = projected.shape
    width = triple // 3
    count = width // PAIR

    def body(query_ref, key_ref, value_ref, mixed_ref, total_ref):
        values = value_ref[...].T
        halves = []
        for half in range(PAIR // HD):
            lanes = slice(half * HD, (half + 1) * HD)
            scores = product(key_ref[:, lanes], query_ref[:, lanes], NT)
            top = jnp.max(scores, axis=0, keepdims=True)
            weights = jnp.exp(scores - top)
            total = jnp.sum(weights, axis=0, keepdims=True)
            halves.append(product(values[lanes, :], weights.astype(jnp.bfloat16)) / total)
            total_ref[0, half : half + 1, :] = top + jnp.log(total)
        mixed_ref[...] = jnp.concatenate(halves, axis=0).T.astype(jnp.bfloat16)

    def spec(part):
        return pl.BlockSpec((tokens, PAIR), lambda at: (0, part * count + at))

    return pl.pallas_call(
        body,
        grid=(count,),
        in_specs=[spec(0), spec(1), spec(2)],
        out_specs=[
            pl.BlockSpec((tokens, PAIR), lambda at: (0, at)),
            pl.BlockSpec((1, PAIR // HD, tokens), lambda at: (at, 0, 0)),
        ],
        out_shape=[
            jax.ShapeDtypeStruct((tokens, width), jnp.bfloat16),
            jax.ShapeDtypeStruct((count, PAIR // HD, tokens), jnp.float32),
        ],
        cost_estimate=cost(16 * tokens * tokens * width, 8 * tokens * width),
        compiler_params=params(),
    )(projected, projected, projected)


def attention_backward(projected, grad_mixed, totals):
    tokens, triple = projected.shape
    width = triple // 3
    count = width // PAIR

    def body(query_ref, key_ref, value_ref, grad_ref, total_ref, out_ref, sq_ref, sv_ref):
        keys = key_ref[...].T
        outs_q, outs_k, outs_v = [], [], []
        for half in range(PAIR // HD):
            lanes = slice(half * HD, (half + 1) * HD)
            scores = product(key_ref[:, lanes], query_ref[:, lanes], NT)
            probs = jnp.exp(scores - total_ref[0, half : half + 1, :])
            grad_probs = product(value_ref[:, lanes], grad_ref[:, lanes], NT)
            row_dot = jnp.sum(probs * grad_probs, axis=0, keepdims=True)
            grad_scores = (probs * (grad_probs - row_dot)).astype(jnp.bfloat16)
            outs_q.append(product(keys[lanes, :], grad_scores))
            outs_k.append(product(grad_scores, query_ref[:, lanes]))
            outs_v.append(product(probs.astype(jnp.bfloat16), grad_ref[:, lanes]))
        grad_query = jnp.concatenate(outs_q, axis=0).T * 0.125
        grad_value = jnp.concatenate(outs_v, axis=1)
        out_ref[0] = grad_query.astype(jnp.bfloat16)
        out_ref[1] = jnp.concatenate(outs_k, axis=1).astype(jnp.bfloat16)
        out_ref[2] = grad_value.astype(jnp.bfloat16)
        sq_ref[...] = column_sum(grad_query)
        sv_ref[...] = column_sum(grad_value)

    def spec(part):
        return pl.BlockSpec((tokens, PAIR), lambda at: (0, part * count + at))

    block = pl.BlockSpec((tokens, PAIR), lambda at: (0, at))
    line = pl.BlockSpec((1, PAIR), lambda at: (0, at))
    return pl.pallas_call(
        body,
        grid=(count,),
        in_specs=[spec(0), spec(1), spec(2), block]
        + [pl.BlockSpec((1, PAIR // HD, tokens), lambda at: (at, 0, 0))],
        out_specs=[pl.BlockSpec((3, tokens, PAIR), lambda at: (0, 0, at)), line, line],
        out_shape=[jax.ShapeDtypeStruct((3, tokens, width), jnp.bfloat16)]
        + [jax.ShapeDtypeStruct((1, width), jnp.float32)] * 2,
        cost_estimate=cost(40 * tokens * tokens * width, 16 * tokens * width),
        compiler_params=params(),
    )(projected, projected, projected, grad_mixed, totals)


def weight_grads(where, pairs):
    tokens, rows = pairs[0][0].shape
    sizes = [pair[4] for pair in pairs]
    parts = [pair[2].shape[0] if pair[2].ndim == 3 else 1 for pair in pairs]
    spans = [size * part for size, part in zip(sizes, parts)]
    width = sum(spans)
    step = 256
    count = rows // step
    half = count // 2
    operands, in_specs = [], []
    for left, left_pair, right, right_pair, _ in pairs:
        operands += [left, left_pair, right, right_pair]
        in_specs += [pl.BlockSpec((tokens, step), lambda at, _: (0, at))] * 2 + [ANY] * 2

    def body(where_ref, *refs):
        ins = refs[: len(operands)]
        send_a, keep_a, send_b, keep_b = refs[len(operands) : len(operands) + 4]
        joined, sems = refs[len(operands) + 4 : -1], refs[-1]
        at = pl.program_id(0)

        @pl.when(at == 0)
        def _():
            for pair, (size, part_count) in enumerate(zip(sizes, parts)):
                for side in range(2):
                    source = ins[4 * pair + 2 + side]
                    for which in range(4):
                        block = jnp.bitwise_xor(where_ref[0], 2 * which)
                        columns = pl.ds(aligned(block * size, LANES), size)
                        for part in range(part_count):
                            begin = (which * part_count + part) * size
                            taken = (
                                source.at[part, :, columns]
                                if part_count > 1
                                else source.at[:, columns]
                            )
                            pltpu.make_async_copy(
                                taken,
                                joined[2 * pair + side].at[:, begin : begin + size],
                                sems.at[2 * pair + side],
                            ).start()
            for which in range(2 * len(pairs)):
                finish(joined[which], sems.at[which])

        results = []
        for pair in range(len(pairs)):
            total = product(ins[4 * pair][...], joined[2 * pair][...], TN)
            total = total + product(ins[4 * pair + 1][...], joined[2 * pair + 1][...], TN)
            results.append(total.astype(jnp.bfloat16))

        def put(targets):
            base = 0
            for pair, span in enumerate(spans):
                for which in range(4):
                    ref, slot = targets[which]
                    ref[slot, :, base : base + span] = results[pair][
                        :, which * span : (which + 1) * span
                    ]
                base += span

        @pl.when(at < half)
        def _():
            put([(keep_a, 0), (send_a, 0), (keep_a, 1), (send_a, 1)])

        @pl.when(at >= half)
        def _():
            put([(keep_b, 0), (keep_b, 1), (send_b, 0), (send_b, 1)])

    spec_a = pl.BlockSpec((2, step, width), lambda at, _: (0, jnp.minimum(at, half - 1), 0))
    spec_b = pl.BlockSpec((2, step, width), lambda at, _: (0, jnp.maximum(at - half, 0), 0))
    return pl.pallas_call(
        body,
        grid_spec=pltpu.PrefetchScalarGridSpec(
            num_scalar_prefetch=1,
            grid=(count,),
            in_specs=in_specs,
            out_specs=[spec_a, spec_a, spec_b, spec_b],
            scratch_shapes=[
                pltpu.VMEM((tokens, 4 * span), jnp.bfloat16) for span in spans for _ in range(2)
            ]
            + [pltpu.SemaphoreType.DMA((2 * len(pairs),))],
        ),
        out_shape=[jax.ShapeDtypeStruct((2, rows // 2, width), jnp.bfloat16)] * 4,
        cost_estimate=cost(16 * rows * tokens * width, 8 * rows * width + 4 * tokens * rows),
        compiler_params=params(),
    )(where, *operands)


def weight_grads_flipped(where, left, left_pair, right, right_pair, groups):
    tokens, rows = left.shape
    share = rows // groups
    step = min(TILE, share)
    per = share // step
    count = rows // step
    half = count // 2
    span = 4 * LANES

    def body(where_ref, left_ref, pair_ref, right_ref, right_pair_ref, *rest):
        send_a, keep_a, send_b, keep_b, joined, turned, sems = rest
        at = pl.program_id(0)

        @pl.when(at == 0)
        def _():
            for side, source in enumerate((right_ref, right_pair_ref)):
                for which in range(4):
                    block = jnp.bitwise_xor(where_ref[0], 2 * which)
                    columns = pl.ds(aligned(block * LANES, LANES), LANES)
                    pltpu.make_async_copy(
                        source.at[:, columns],
                        joined.at[side, :, which * LANES : (which + 1) * LANES],
                        sems.at[side],
                    ).start()
            for side in range(2):
                finish(joined.at[side], sems.at[side])
                turned[side] = joined[side].T

        total = product(turned[0], left_ref[...]) + product(turned[1], pair_ref[...])
        total = total.astype(jnp.bfloat16)

        def put(targets):
            for which in range(4):
                ref, slot = targets[which]
                ref[slot, 0] = total[which * LANES : (which + 1) * LANES, :]

        @pl.when(at < half)
        def _():
            put([(keep_a, 0), (send_a, 0), (keep_a, 1), (send_a, 1)])

        @pl.when(at >= half)
        def _():
            put([(keep_b, 0), (keep_b, 1), (send_b, 0), (send_b, 1)])

    def spec(clip):
        return pl.BlockSpec(
            (2, 1, LANES, step), lambda at, _: (0, clip(at) // per, 0, clip(at) % per)
        )

    spec_a = spec(lambda at: jnp.minimum(at, half - 1))
    spec_b = spec(lambda at: jnp.maximum(at - half, 0))
    return pl.pallas_call(
        body,
        grid_spec=pltpu.PrefetchScalarGridSpec(
            num_scalar_prefetch=1,
            grid=(count,),
            in_specs=[pl.BlockSpec((tokens, step), lambda at, _: (0, at))] * 2 + [ANY] * 2,
            out_specs=[spec_a, spec_a, spec_b, spec_b],
            scratch_shapes=[
                pltpu.VMEM((2, tokens, span), jnp.bfloat16),
                pltpu.VMEM((2, span, tokens), jnp.bfloat16),
                pltpu.SemaphoreType.DMA((2,)),
            ],
        ),
        out_shape=[jax.ShapeDtypeStruct((2, groups // 2, LANES, share), jnp.bfloat16)] * 4,
        cost_estimate=cost(4 * rows * tokens * span, 2 * rows * span + 4 * tokens * rows),
        compiler_params=params(),
    )(where, left, left_pair, right, right_pair)


def finish_flipped(blocks):
    count, size, rows = blocks.shape
    step = min(rows, 256)

    def body(in_ref, out_ref):
        for at in range(count):
            out_ref[:, at * size : (at + 1) * size] = in_ref[at].astype(jnp.float32).T

    return pl.pallas_call(
        body,
        grid=(rows // step,),
        in_specs=[pl.BlockSpec((count, size, step), lambda at: (0, 0, at))],
        out_specs=pl.BlockSpec((step, count * size), lambda at: (at, 0)),
        out_shape=jax.ShapeDtypeStruct((rows, count * size), jnp.float32),
        compiler_params=params(),
    )(blocks)


def pick_blocks(where, sources, outs):
    flat_outs = [item for out in outs for item in out]

    def body(where_ref, *refs):
        in_refs, out_refs = refs[: len(flat_outs)], refs[len(flat_outs) :]
        at = 0
        for out_ref, out in zip(out_refs, outs):
            base = 0
            for _, size, _ in out:
                out_ref[:, base : base + size] = in_refs[at][...]
                base += size
                at += 1

    def mine(source, size, part):
        return pl.BlockSpec(
            (sources[source].shape[0], size),
            lambda at, where_ref: (0, part * BLOCKS + where_ref[0]),
        )

    shapes = [(sources[out[0][0]].shape[0], sum(item[1] for item in out)) for out in outs]
    return pl.pallas_call(
        body,
        grid_spec=pltpu.PrefetchScalarGridSpec(
            num_scalar_prefetch=1,
            grid=(1,),
            in_specs=[mine(*item) for item in flat_outs],
            out_specs=[pl.BlockSpec(shape, lambda at, _: (0, 0)) for shape in shapes],
        ),
        out_shape=[jax.ShapeDtypeStruct(shape, jnp.bfloat16) for shape in shapes],
        compiler_params=params(),
    )(where, *[sources[item[0]] for item in flat_outs])


def unpack_vectors(where, sources, lengths, pair_at, width):
    groups = len(sources)
    row = sources[0].shape[1]
    outs = [3 * width if at == pair_at else length * groups for at, length in enumerate(lengths)]

    def body(where_ref, *refs):
        source_refs, out_refs = refs[:groups], refs[groups:]
        out_refs[pair_at][...] = jnp.zeros((1, 3 * width), jnp.float32)
        for hop in range(groups):
            block = source_refs[hop][...].astype(jnp.float32)
            owner = jnp.bitwise_xor(where_ref[1], hop)
            place = 0
            for which, length in enumerate(lengths):
                start = owner * length
                if which == pair_at:
                    start = start + jnp.where(start >= width, width, 0)
                for begin in range(0, length, LANES):
                    line, lane = (place + begin) // row, (place + begin) % row
                    target = pl.ds(aligned(start + begin, LANES), LANES)
                    out_refs[which][:, target] = block[line : line + 1, lane : lane + LANES]
                place += length

    return pl.pallas_call(
        body,
        grid_spec=pltpu.PrefetchScalarGridSpec(
            num_scalar_prefetch=1,
            grid=(1,),
            in_specs=[pl.BlockSpec((16, row), lambda at, _: (0, 0))] * groups,
            out_specs=[pl.BlockSpec((1, size), lambda at, _: (0, 0)) for size in outs],
        ),
        out_shape=[jax.ShapeDtypeStruct((1, size), jnp.float32) for size in outs],
        compiler_params=params(),
    )(where, *sources)


def pack_sums(vectors, groups):
    total = sum(vec.shape[1] for vec in vectors) // groups

    def body(*refs):
        for owner in range(groups):
            pieces = []
            for ref in refs[:-1]:
                length = ref.shape[1] // groups
                pieces.append(ref[:, owner * length : (owner + 1) * length])
            refs[-1][owner : owner + 1, :] = jnp.concatenate(pieces, axis=1)

    return pl.pallas_call(
        body,
        out_shape=jax.ShapeDtypeStruct((groups, total), jnp.float32),
        compiler_params=params(),
    )(*vectors)


def unpack_sums(where, first, second, lengths):
    groups, total = first.shape

    def body(where_ref, first_ref, second_ref, *outs):
        line = jnp.zeros((1, total), jnp.float32)
        for owner in range(groups):
            both = first_ref[owner : owner + 1, :] + second_ref[owner : owner + 1, :]
            line = jnp.where(where_ref[1] == owner, both, line)
        place = 0
        for out, length in zip(outs, lengths):
            out[...] = line[:, place : place + length]
            place += length

    whole = pl.BlockSpec((groups, total), lambda at, _: (0, 0))
    return pl.pallas_call(
        body,
        grid_spec=pltpu.PrefetchScalarGridSpec(
            num_scalar_prefetch=1,
            grid=(1,),
            in_specs=[whole, whole],
            out_specs=[pl.BlockSpec((1, length), lambda at, _: (0, 0)) for length in lengths],
        ),
        out_shape=[jax.ShapeDtypeStruct((1, length), jnp.float32) for length in lengths],
        compiler_params=params(),
    )(where, first, second)


def finish_blocks(blocks, sizes):
    count, rows, width = blocks.shape
    step = min(rows, 128)

    def body(in_ref, *out_refs):
        base = 0
        for out_ref, size in zip(out_refs, sizes):
            for at in range(count):
                out_ref[:, at * size : (at + 1) * size] = in_ref[
                    at, :, base : base + size
                ].astype(jnp.float32)
            base += size

    return pl.pallas_call(
        body,
        grid=(rows // step,),
        in_specs=[pl.BlockSpec((count, step, width), lambda at: (0, at, 0))],
        out_specs=[pl.BlockSpec((step, count * size), lambda at: (at, 0)) for size in sizes],
        out_shape=[jax.ShapeDtypeStruct((rows, count * size), jnp.float32) for size in sizes],
        compiler_params=params(),
    )(blocks)


def finish_grads(where, pieces, strips):
    rows = pieces[0].shape[0]
    step = min(rows, 128)
    totals = {}
    for _, size, out, base in strips:
        totals[out] = max(totals.get(out, 0), base + size * BLOCKS)

    def body(where_ref, *refs):
        piece_refs, out_refs = refs[:BLOCKS], refs[BLOCKS:]
        for at in range(BLOCKS):
            block = jnp.bitwise_xor(where_ref[0], at)
            for start, size, out, base in strips:
                target = pl.ds(aligned(base + block * size, LANES), size)
                out_refs[out][:, target] = piece_refs[at][:, start : start + size].astype(
                    jnp.float32
                )

    return pl.pallas_call(
        body,
        grid_spec=pltpu.PrefetchScalarGridSpec(
            num_scalar_prefetch=1,
            grid=(rows // step,),
            in_specs=[
                pl.BlockSpec((step, piece.shape[1]), lambda at, _: (at, 0)) for piece in pieces
            ],
            out_specs=[
                pl.BlockSpec((step, totals[out]), lambda at, _: (at, 0)) for out in sorted(totals)
            ],
        ),
        out_shape=[
            jax.ShapeDtypeStruct((rows, totals[out]), jnp.float32) for out in sorted(totals)
        ],
        compiler_params=params(),
    )(where, *pieces)


REP, GRP = "rep", "grp"


def exchange(tensor, mask, axis=REP):
    size = lax.axis_size(axis)
    return lax.ppermute(tensor, axis, [(at, at ^ mask) for at in range(size)])


def tie(value, *others):
    return lax.optimization_barrier((value, others))[0]


def all_hops(block):
    return [exchange(block, hop, GRP) for hop in range(1, lax.axis_size(GRP))]


def spread(own):
    by_x = exchange(own, 2)
    by_y = exchange(own, 4)
    half = own.shape[0] // 2
    sent = (by_x[:half], by_y[half:])
    top = exchange(sent[0], 4)
    bottom = exchange(sent[1], 2)
    pieces = []
    for piece in ((own,), (by_x,), (by_y,), (top, bottom)):
        pieces += [piece, tuple(exchange(array, 1) for array in piece)]
    return pieces, sent


def add_rounded(left, right):
    return (left.astype(jnp.float32) + right.astype(jnp.float32)).astype(jnp.bfloat16)


def first_sends(parts):
    return exchange(parts[0], 2), exchange(parts[2], 4)


def second_sends(parts, got):
    keep_a, keep_b = parts[1], parts[3]
    got_a, got_b = got
    next_a = exchange(add_rounded(keep_a[1], got_a[1]), 4)
    next_b = exchange(add_rounded(keep_b[1], got_b[1]), 2)
    rest_a = add_rounded(keep_a[0], got_a[0])
    rest_b = add_rounded(keep_b[0], got_b[0])
    return (rest_a, rest_b), (next_a, next_b)


def block_total(rest, got):
    total = jnp.concatenate([add_rounded(*pair) for pair in zip(rest, got)], axis=0)
    mask = BLOCKS
    while mask < lax.axis_size(REP):
        total = add_rounded(total, exchange(total, mask))
        mask *= 2
    return total


def scatter(total):
    return lax.psum_scatter(total, GRP, scatter_dimension=0, tiled=True)


def gather(own):
    return lax.all_gather(own, REP, axis=0, tiled=False)[:BLOCKS]


def grp_sum(total):
    groups = lax.axis_size(GRP)
    share = total.shape[0] // groups
    place = lax.axis_index(GRP)
    sent = [
        lax.dynamic_slice_in_dim(total, (place ^ hop) * share, share, 0) for hop in range(groups)
    ]
    got = [exchange(sent[hop], hop, GRP) for hop in range(1, groups)]
    return sent[0], got


def sum_rounded(own, got):
    total = own.astype(jnp.float32)
    for other in got:
        total = total + other.astype(jnp.float32)
    return total.astype(jnp.bfloat16)


def layer(
    images,
    cotangent,
    ln1_gain,
    ln1_shift,
    qkv_weight,
    qv_bias,
    out_weight,
    out_bias,
    ln2_gain,
    ln2_shift,
    fc1_weight,
    fc1_bias,
    fc2_weight,
    fc2_bias,
):
    groups = lax.axis_size(GRP)
    place = jnp.bitwise_and(lax.axis_index(REP), BLOCKS - 1)
    where = jnp.stack([place, lax.axis_index(GRP)])
    _, width = out_weight.shape
    hidden_block = fc1_weight.shape[1] // BLOCKS

    (block_a,) = pick_blocks(where, [qkv_weight], [[(0, LANES, part) for part in range(3)]])
    got_a = all_hops(block_a)
    block_b, block_c = pick_blocks(
        where,
        [fc1_weight, out_weight, fc2_weight],
        [[(0, hidden_block, 0), (1, LANES, 0)], [(2, LANES, 0)]],
    )
    vectors = (ln1_gain, ln1_shift, qv_bias, out_bias, ln2_gain, ln2_shift, fc1_bias, fc2_bias)
    sizes = [vec.shape[0] for vec in vectors]
    length = 16 * 2 * LANES
    packed, offset = jnp.zeros((length,), jnp.bfloat16), 0
    for vec, size in zip(vectors, sizes):
        packed = packed + jnp.pad(vec, (offset, length - offset - size))
        offset += size
    packed = packed.reshape(16, 2 * LANES)
    got_v = all_hops(packed)

    pieces_a, sent_a = spread(jnp.concatenate(got_a))
    got_b = all_hops(tie(block_b, got_a))
    pieces_b, sent_b = spread(jnp.concatenate(tie(got_b, sent_a)))
    got_c = all_hops(tie(block_c, got_b))
    pieces_c, _ = spread(jnp.concatenate(tie(got_c, sent_b)))
    gain_1, shift_1, bias_in, bias_attn, gain_2, shift_2, bias_up, bias_down = unpack_vectors(
        where, [packed] + got_v, sizes, 2, width
    )

    image = images[0]
    grad_block = cotangent[0]
    cot_pair = exchange(grad_block, 1)

    normed_in, projected = qkv_forward(where, image, gain_1, shift_1, bias_in, qkv_weight, pieces_a)
    normed_pair = exchange(normed_in, 1)
    attended, totals = attention_forward(projected)
    attended_pair = exchange(attended, 1)
    residual, normed_mid = out_forward(
        where, image, attended, bias_attn, gain_2, shift_2, out_weight, pieces_b, hidden_block
    )
    mid_pair = exchange(normed_mid, 1)
    active, slope = up_forward(where, normed_mid, bias_up, fc1_weight, pieces_b)
    active_pair = exchange(active, 1)

    grad_pre, sum_up = down_backward(where, grad_block, slope, fc2_weight, pieces_c)
    pre_pair = exchange(grad_pre, 1)
    down_parts = weight_grads_flipped(
        tie(where, grad_pre), active, active_pair, grad_block, cot_pair, groups
    )
    down_got = first_sends(down_parts)
    middle = middle_backward(
        tie(where, down_parts),
        grad_pre,
        grad_block,
        residual,
        gain_2,
        fc1_weight,
        out_weight,
        pieces_b,
        hidden_block,
    )
    grad_res, grad_res_b, grad_attended, sum_gain_2, sum_shift_2, sum_res, sum_top = middle
    res_pair = exchange(grad_res_b, 1)
    down_rest, down_got = second_sends(down_parts, tie(down_got, grad_res))
    up_parts = weight_grads(
        tie(where, grad_res, down_rest),
        [
            (normed_mid, mid_pair, grad_pre, pre_pair, hidden_block),
            (attended, attended_pair, grad_res_b, res_pair, LANES),
        ],
    )
    up_got = first_sends(up_parts)
    down_total = block_total(down_rest, tie(down_got, up_parts))
    down_own = scatter(down_total)
    grad_proj, sum_query, sum_value = attention_backward(
        projected, tie(grad_attended, up_parts, down_total), totals
    )
    proj_pair = exchange(grad_proj, 1)
    up_rest, up_got = second_sends(up_parts, tie(up_got, grad_proj))
    down_blocks = gather(tie(down_own, grad_proj))
    qkv_parts = weight_grads(
        tie(where, up_rest), [(normed_in, normed_pair, grad_proj, proj_pair, LANES)]
    )
    qkv_got = first_sends(qkv_parts)
    up_total = block_total(up_rest, tie(up_got, qkv_parts))
    up_own = scatter(up_total)
    input_grad, sum_gain_1, sum_shift_1 = qkv_backward(
        tie(where, qkv_parts, up_total),
        grad_proj,
        image,
        grad_res,
        gain_1,
        qkv_weight,
        pieces_a,
    )
    sums = pack_sums(
        [
            sum_gain_1,
            sum_shift_1,
            jnp.concatenate([sum_query, sum_value], axis=1),
            sum_res,
            sum_gain_2,
            sum_shift_2,
            sum_up,
            sum_top,
        ],
        groups,
    )
    got = exchange(sums, 1)
    grad_down = finish_flipped(tie(down_blocks, sums)[:, 0])
    sums = sums + tie(got, grad_down)
    qkv_rest, qkv_got = second_sends(qkv_parts, tie(qkv_got, grad_down))
    got = exchange(tie(sums, qkv_rest), 2)
    block_out = down_forward(
        tie(where, input_grad, sums, qkv_rest), residual, active, bias_down, fc2_weight, pieces_c
    )
    up_blocks = gather(tie(up_own, block_out))
    sums = sums + tie(got, block_out)
    mask = BLOCKS
    while mask < lax.axis_size(REP):
        sums = sums + exchange(sums, mask)
        mask *= 2
    qkv_total = block_total(qkv_rest, tie(qkv_got, block_out, sums))
    own, qkv_got = grp_sum(qkv_total)
    sums = sums + exchange(tie(sums, qkv_total), 4)
    own = sum_rounded(own, tie(qkv_got, sums))
    by_x = exchange(own, 2)
    by_y = exchange(own, 4)
    mask = 1
    while mask * 2 < groups:
        sums = sums + exchange(tie(sums, own), mask, GRP)
        mask *= 2
    both = exchange(tie(by_x, sums), 4)
    last = exchange(tie(sums, by_x), mask, GRP)
    grad_up, grad_out = finish_blocks(tie(up_blocks, by_x, by_y), [hidden_block, LANES])
    qkv_pieces = []
    for piece in (own, by_x, by_y, both):
        qkv_pieces += [piece, exchange(piece, 1)]
    (grad_qkv,) = finish_grads(
        where, qkv_pieces, [(at * LANES, LANES, 0, at * width) for at in range(3)]
    )
    sums = [vec.reshape(-1) for vec in unpack_sums(where, sums, last, sizes)]
    return (
        block_out[None],
        input_grad[None],
        sums[0],
        sums[1],
        grad_qkv,
        sums[2],
        grad_out,
        sums[3],
        sums[4],
        sums[5],
        grad_up,
        sums[6],
        grad_down,
        sums[7],
    )


def solution(mesh):
    tokens = P((REP, GRP), None, None)
    vector, matrix = P(GRP), P(GRP, None)
    weights = (vector, vector, matrix, vector, matrix, vector)
    weights += (vector, vector, matrix, vector, matrix, vector)
    specs = (tokens, tokens) + weights
    return jax.shard_map(layer, mesh=mesh, in_specs=specs, out_specs=specs, check_vma=False)
```

```python
import jax
import jax.numpy as jnp
from jax import lax
from jax.experimental import pallas as pl
from jax.experimental.pallas import tpu as pltpu
from jax.sharding import PartitionSpec as P


BLOCKS = 8
ROW, PART, BLOCK = range(3)
LANES = 128
TILE = 512
HD = 64
PAIR = 128
EPS = 1e-06

root_half = 0.7071067811865476
inv_root_tau = 0.3989422804014327

NN = (((1,), (0,)), ((), ()))
NT = (((1,), (1,)), ((), ()))
TN = (((0,), (0,)), ((), ()))
ANY = pl.BlockSpec(memory_space=pl.ANY)


def product(left, right, dims=NN):
    return lax.dot_general(left, right, dims, preferred_element_type=jnp.float32)


def aligned(start, unit):
    return pl.multiple_of(start, unit)


def params(mebibytes=60):
    return pltpu.CompilerParams(vmem_limit_bytes=mebibytes << 20)


def cost(flops, moved):
    return pl.CostEstimate(flops=int(flops), bytes_accessed=int(moved), transcendentals=0)


def start_loads(where, own, pieces, strips, target, sems, mode):
    share = own.shape[0]
    groups = target.shape[0] // share
    mine = where[1]

    def go(source, rows, columns, key):
        pltpu.make_async_copy(source, target.at[rows, columns], sems.at[key]).start()

    own_rows = pl.ds(aligned(mine * share, share), share)
    if mode == ROW:
        pltpu.make_async_copy(own, target.at[own_rows, :], sems.at[0]).start()
    for which, (source, size, base) in enumerate(strips):
        for at in range(BLOCKS):
            block = jnp.bitwise_xor(where[0], at)
            columns = pl.ds(aligned(base + block * size, LANES), size)
            key = which if mode == PART else at
            if mode != ROW:
                go(own.at[:, columns], own_rows, columns, key)
            for hop in range(1, groups):
                first = jnp.bitwise_xor(mine, hop) * share
                low = 0
                for ref in pieces[at]:
                    high = low + ref.shape[0]
                    begin, end = max(low, (hop - 1) * share), min(high, hop * share)
                    if begin < end:
                        shift = begin - (hop - 1) * share
                        rows = pl.ds(aligned(first + shift, 16), end - begin)
                        go(
                            ref.at[begin - low : end - low, source : source + size],
                            rows,
                            columns,
                            hop if mode == ROW else key,
                        )
                    low = high


def finish(region, sem):
    pltpu.make_async_copy(region, region, sem).wait()


def wait_rows(where, target, sems, hop, share):
    rows = pl.ds(aligned(jnp.bitwise_xor(where[1], hop) * share, share), share)
    finish(target.at[rows, :], sems.at[hop])


def flat(pieces):
    return [array for piece in pieces for array in piece]


def regroup(refs, pieces):
    grouped, at = [], 0
    for piece in pieces:
        grouped.append(refs[at : at + len(piece)])
        at += len(piece)
    return grouped


def center(values):
    mean = jnp.mean(values, axis=-1, keepdims=True)
    centred = values - mean
    inv_std = lax.rsqrt(jnp.mean(centred * centred, axis=-1, keepdims=True) + EPS)
    return centred * inv_std, inv_std


def center_back(grad_out, normed, inv_std, gain):
    grad_hat = grad_out * gain
    return inv_std * (
        grad_hat
        - jnp.mean(grad_hat, axis=-1, keepdims=True)
        - normed * jnp.mean(grad_hat * normed, axis=-1, keepdims=True)
    )


def column_sum(values):
    return jnp.sum(values, axis=0, keepdims=True)


def qkv_forward(where, image, gain, shift, bias, own, pieces):
    tokens, width = image.shape
    wide = own.shape[1]
    per = width // TILE
    strips = [(part * LANES, LANES, part * width) for part in range(3)]

    def body(where_ref, image_ref, gain_ref, shift_ref, bias_ref, own_ref, *rest):
        piece_refs = regroup(rest[: len(flat(pieces))], pieces)
        normed_ref, out_ref, weight, sems = rest[len(flat(pieces)) :]
        at = pl.program_id(0)

        @pl.when(at == 0)
        def _():
            start_loads(where_ref, own_ref, piece_refs, strips, weight, sems, PART)
            normed, _ = center(image_ref[...].astype(jnp.float32))
            normed_ref[...] = (normed * gain_ref[...] + shift_ref[...]).astype(jnp.bfloat16)

        for part in range(3):

            @pl.when(at == part * per)
            def _(part=part):
                finish(weight.at[:, part * width : (part + 1) * width], sems.at[part])

        columns = pl.ds(aligned(at * TILE, TILE), TILE)
        total = product(normed_ref[...], weight[:, columns]) + bias_ref[...]
        scale = jnp.where(at < per, 0.125, 1.0)
        out_ref[...] = (total * scale).astype(jnp.bfloat16)

    full = lambda at, _: (0, 0)
    return pl.pallas_call(
        body,
        grid_spec=pltpu.PrefetchScalarGridSpec(
            num_scalar_prefetch=1,
            grid=(wide // TILE,),
            in_specs=[
                pl.BlockSpec((tokens, width), full),
                pl.BlockSpec((1, width), full),
                pl.BlockSpec((1, width), full),
                pl.BlockSpec((1, TILE), lambda at, _: (0, at)),
            ]
            + [ANY] * (1 + len(flat(pieces))),
            out_specs=[
                pl.BlockSpec((tokens, width), full),
                pl.BlockSpec((tokens, TILE), lambda at, _: (0, at)),
            ],
            scratch_shapes=[
                pltpu.VMEM((width, wide), jnp.bfloat16),
                pltpu.SemaphoreType.DMA((3,)),
            ],
        ),
        out_shape=[
            jax.ShapeDtypeStruct((tokens, width), jnp.bfloat16),
            jax.ShapeDtypeStruct((tokens, wide), jnp.bfloat16),
        ],
        cost_estimate=cost(2 * tokens * width * wide, 2 * width * wide),
        compiler_params=params(22),
    )(where, image, gain, shift, bias, own, *flat(pieces))


def out_forward(where, image, attended, bias, gain, shift, own, pieces, source):
    tokens, width = image.shape
    share = own.shape[0]
    groups = width // share
    chunk = 256

    def body(where_ref, image_ref, attended_ref, bias_ref, gain_ref, shift_ref, own_ref, *rest):
        piece_refs = regroup(rest[: len(flat(pieces))], pieces)
        residual_ref, normed_ref, weight, sems = rest[len(flat(pieces)) :]
        start_loads(where_ref, own_ref, piece_refs, [(source, LANES, 0)], weight, sems, ROW)
        for hop in range(groups):
            wait_rows(where_ref, weight, sems, hop, share)

        @pl.loop(0, width // chunk)
        def _(at):
            columns = pl.ds(aligned(at * chunk, chunk), chunk)
            residual_ref[:, columns] = (
                image_ref[:, columns].astype(jnp.float32)
                + product(attended_ref[...], weight[:, columns])
                + bias_ref[:, columns]
            )

        normed, _ = center(residual_ref[...])
        normed_ref[...] = (normed * gain_ref[...] + shift_ref[...]).astype(jnp.bfloat16)

    full = lambda at, _: (0, 0)
    return pl.pallas_call(
        body,
        grid_spec=pltpu.PrefetchScalarGridSpec(
            num_scalar_prefetch=1,
            grid=(1,),
            in_specs=[pl.BlockSpec((tokens, width), full)] * 2
            + [pl.BlockSpec((1, width), full)] * 3
            + [ANY] * (1 + len(flat(pieces))),
            out_specs=[pl.BlockSpec((tokens, width), full)] * 2,
            scratch_shapes=[
                pltpu.VMEM((width, width), jnp.bfloat16),
                pltpu.SemaphoreType.DMA((groups,)),
            ],
        ),
        out_shape=[
            jax.ShapeDtypeStruct((tokens, width), jnp.float32),
            jax.ShapeDtypeStruct((tokens, width), jnp.bfloat16),
        ],
        cost_estimate=cost(2 * tokens * width * width, 2 * width * width),
        compiler_params=params(32),
    )(where, image, attended, bias, gain, shift, own, *flat(pieces))


def up_forward(where, normed, bias, own, pieces):
    tokens, width = normed.shape
    wide = own.shape[1]
    size = wide // BLOCKS

    def body(where_ref, normed_ref, bias_ref, own_ref, *rest):
        piece_refs = regroup(rest[: len(flat(pieces))], pieces)
        active_ref, slope_ref, weight, sems = rest[len(flat(pieces)) :]
        at = pl.program_id(0)

        @pl.when(at == 0)
        def _():
            start_loads(where_ref, own_ref, piece_refs, [(0, size, 0)], weight, sems, BLOCK)

        for which in range(2):
            block = jnp.bitwise_xor(where_ref[0], 2 * at + which)
            finish(
                weight.at[:, pl.ds(aligned(block * size, size), size)], sems.at[2 * at + which]
            )
        pair = jnp.bitwise_xor(where_ref[0], 2 * at) // 2
        columns = pl.ds(aligned(pair * 2 * size, size), 2 * size)
        pre_act = product(normed_ref[...], weight[:, columns]) + bias_ref[...]
        cdf = 0.5 * (1.0 + lax.erf(pre_act * root_half))
        density = jnp.exp(-0.5 * pre_act * pre_act) * inv_root_tau
        active_ref[...] = (pre_act * cdf).astype(jnp.bfloat16)
        slope_ref[...] = (cdf + pre_act * density).astype(jnp.bfloat16)

    full = lambda at, _: (0, 0)
    mine = lambda at, where_ref: (0, jnp.bitwise_xor(where_ref[0], 2 * at) // 2)
    return pl.pallas_call(
        body,
        grid_spec=pltpu.PrefetchScalarGridSpec(
            num_scalar_prefetch=1,
            grid=(BLOCKS // 2,),
            in_specs=[pl.BlockSpec((tokens, width), full), pl.BlockSpec((1, 2 * size), mine)]
            + [ANY] * (1 + len(flat(pieces))),
            out_specs=[pl.BlockSpec((tokens, 2 * size), mine)] * 2,
            scratch_shapes=[
                pltpu.VMEM((width, wide), jnp.bfloat16),
                pltpu.SemaphoreType.DMA((BLOCKS,)),
            ],
        ),
        out_shape=[jax.ShapeDtypeStruct((tokens, wide), jnp.bfloat16)] * 2,
        cost_estimate=cost(2 * tokens * width * wide, 2 * width * wide),
        compiler_params=params(38),
    )(where, normed, bias, own, *flat(pieces))


def down_forward(where, residual, active, bias, own, pieces):
    tokens, wide = active.shape
    width = residual.shape[1]
    chunk = 2 * LANES

    def body(where_ref, residual_ref, active_ref, bias_ref, own_ref, *rest):
        piece_refs = regroup(rest[: len(flat(pieces))], pieces)
        out_ref, weight, sems = rest[len(flat(pieces)) :]
        at = pl.program_id(0)

        @pl.when(at == 0)
        def _():
            start_loads(where_ref, own_ref, piece_refs, [(0, LANES, 0)], weight, sems, BLOCK)

        for which in range(2):
            block = jnp.bitwise_xor(where_ref[0], 2 * at + which)
            finish(
                weight.at[:, pl.ds(aligned(block * LANES, LANES), LANES)],
                sems.at[2 * at + which],
            )
        pair = jnp.bitwise_xor(where_ref[0], 2 * at) // 2
        columns = pl.ds(aligned(pair * chunk, chunk), chunk)
        out_ref[...] = (
            residual_ref[...] + product(active_ref[...], weight[:, columns]) + bias_ref[...]
        ).astype(jnp.bfloat16)

    block = lambda at, where_ref: (0, jnp.bitwise_xor(where_ref[0], 2 * at) // 2)
    return pl.pallas_call(
        body,
        grid_spec=pltpu.PrefetchScalarGridSpec(
            num_scalar_prefetch=1,
            grid=(width // chunk,),
            in_specs=[
                pl.BlockSpec((tokens, chunk), block),
                pl.BlockSpec((tokens, wide), lambda at, _: (0, 0)),
                pl.BlockSpec((1, chunk), block),
            ]
            + [ANY] * (1 + len(flat(pieces))),
            out_specs=pl.BlockSpec((tokens, chunk), block),
            scratch_shapes=[
                pltpu.VMEM((wide, width), jnp.bfloat16),
                pltpu.SemaphoreType.DMA((BLOCKS,)),
            ],
        ),
        out_shape=jax.ShapeDtypeStruct((tokens, width), jnp.bfloat16),
        cost_estimate=cost(2 * tokens * width * wide, 2 * width * wide),
        compiler_params=params(32),
    )(where, residual, active, bias, own, *flat(pieces))


def down_backward(where, grad_block, slope, own, pieces):
    tokens, wide = slope.shape
    width = grad_block.shape[1]
    share = own.shape[0]
    groups = wide // share
    tile = min(2 * TILE, share)
    per = share // tile

    def body(where_ref, grad_ref, slope_ref, own_ref, *rest):
        piece_refs = regroup(rest[: len(flat(pieces))], pieces)
        out_ref, sum_ref, weight, sems = rest[len(flat(pieces)) :]
        at = pl.program_id(0)

        @pl.when(at == 0)
        def _():
            start_loads(where_ref, own_ref, piece_refs, [(0, LANES, 0)], weight, sems, ROW)

        hop = at // per

        @pl.when(at % per == 0)
        def _():
            wait_rows(where_ref, weight, sems, hop, share)

        row = jnp.bitwise_xor(where_ref[1], hop) * share + (at % per) * tile
        rows = pl.ds(aligned(row, tile), tile)
        grad_pre = product(grad_ref[...], weight[rows, :], NT) * slope_ref[...].astype(jnp.float32)
        out_ref[...] = grad_pre.astype(jnp.bfloat16)
        sum_ref[...] = column_sum(grad_pre)

    mine = lambda at, where_ref: (0, jnp.bitwise_xor(where_ref[1], at // per) * per + at % per)
    return pl.pallas_call(
        body,
        grid_spec=pltpu.PrefetchScalarGridSpec(
            num_scalar_prefetch=1,
            grid=(wide // tile,),
            in_specs=[
                pl.BlockSpec((tokens, width), lambda at, _: (0, 0)),
                pl.BlockSpec((tokens, tile), mine),
            ]
            + [ANY] * (1 + len(flat(pieces))),
            out_specs=[pl.BlockSpec((tokens, tile), mine), pl.BlockSpec((1, tile), mine)],
            scratch_shapes=[
                pltpu.VMEM((wide, width), jnp.bfloat16),
                pltpu.SemaphoreType.DMA((groups,)),
            ],
        ),
        out_shape=[
            jax.ShapeDtypeStruct((tokens, wide), jnp.bfloat16),
            jax.ShapeDtypeStruct((1, wide), jnp.float32),
        ],
        cost_estimate=cost(2 * tokens * width * wide, 2 * width * wide),
        compiler_params=params(34),
    )(where, grad_block, slope, own, *flat(pieces))


def middle_backward(where, grad_pre, grad_block, residual, gain, own_up, own_out, pieces, pieces_out, size):
    tokens, wide = grad_pre.shape
    width = grad_block.shape[1]
    share = own_up.shape[0]
    groups = width // share
    chunk = 256

    def body(where_ref, pre_ref, block_ref, residual_ref, gain_ref, up_ref, own_ref, *rest):
        piece_refs = regroup(rest[: len(flat(pieces))], pieces)
        rest = rest[len(flat(pieces)) :]
        out_piece_refs = regroup(rest[: len(flat(pieces_out))], pieces_out)
        rest = rest[len(flat(pieces_out)) :]
        (full_ref, half_ref, att_ref, gain_sum, shift_sum, res_sum, top_sum) = rest[:7]
        weight, weight_out, middle, sems, out_sems = rest[7:]
        at = pl.program_id(0)

        @pl.when(at == 0)
        def _():
            start_loads(where_ref, up_ref, piece_refs, [(0, size, 0)], weight, sems, ROW)
            start_loads(
                where_ref,
                own_ref,
                out_piece_refs,
                [(3 * LANES, LANES, 0)],
                weight_out,
                out_sems,
                ROW,
            )

        wait_rows(where_ref, weight, sems, at, share)
        rows = pl.ds(aligned(jnp.bitwise_xor(where_ref[1], at) * share, share), share)
        middle[:, rows] = product(pre_ref[...], weight[rows, :], NT)

        @pl.when(at == groups - 1)
        def _():
            normed, inv_std = center(residual_ref[...])
            grad_mid = middle[...]
            gain_sum[...] = column_sum(grad_mid * normed)
            shift_sum[...] = column_sum(grad_mid)
            top = block_ref[...].astype(jnp.float32)
            top_sum[...] = column_sum(top)
            grad_res = top + center_back(grad_mid, normed, inv_std, gain_ref[...])
            full_ref[...] = grad_res
            res_sum[...] = column_sum(grad_res)
            half_ref[...] = grad_res.astype(jnp.bfloat16)
            for hop in range(groups):
                wait_rows(where_ref, weight_out, out_sems, hop, share)

            @pl.loop(0, width // chunk)
            def _(step):
                part = pl.ds(aligned(step * chunk, chunk), chunk)
                att_ref[:, part] = product(half_ref[...], weight_out[part, :], NT).astype(
                    jnp.bfloat16
                )

    full = lambda at, _: (0, 0)
    line = pl.BlockSpec((1, width), full)
    square = pl.BlockSpec((tokens, width), full)
    return pl.pallas_call(
        body,
        grid_spec=pltpu.PrefetchScalarGridSpec(
            num_scalar_prefetch=1,
            grid=(groups,),
            in_specs=[pl.BlockSpec((tokens, wide), full), square, square, line]
            + [ANY] * (2 + len(flat(pieces)) + len(flat(pieces_out))),
            out_specs=[square] * 3 + [line] * 4,
            scratch_shapes=[
                pltpu.VMEM((width, wide), jnp.bfloat16),
                pltpu.VMEM((width, width), jnp.bfloat16),
                pltpu.VMEM((tokens, width), jnp.float32),
                pltpu.SemaphoreType.DMA((groups,)),
                pltpu.SemaphoreType.DMA((groups,)),
            ],
        ),
        out_shape=[
            jax.ShapeDtypeStruct((tokens, width), jnp.float32),
            jax.ShapeDtypeStruct((tokens, width), jnp.bfloat16),
            jax.ShapeDtypeStruct((tokens, width), jnp.bfloat16),
        ]
        + [jax.ShapeDtypeStruct((1, width), jnp.float32)] * 4,
        cost_estimate=cost(2 * tokens * width * (wide + width), 2 * width * (wide + width)),
        compiler_params=params(),
    )(where, grad_pre, grad_block, residual, gain, own_up, own_out, *flat(pieces), *flat(pieces_out))


def qkv_backward(where, grad_proj, image, grad_res, gain, own, pieces):
    tokens, width = image.shape
    wide = own.shape[1]
    share = own.shape[0]
    groups = width // share
    strips = [(part * LANES, LANES, part * width) for part in range(3)]

    def body(where_ref, proj_ref, image_ref, res_ref, gain_ref, own_ref, *rest):
        piece_refs = regroup(rest[: len(flat(pieces))], pieces)
        out_ref, gain_sum, shift_sum, weight, inner, sems = rest[len(flat(pieces)) :]
        at = pl.program_id(0)

        @pl.when(at == 0)
        def _():
            start_loads(where_ref, own_ref, piece_refs, strips, weight, sems, ROW)

        wait_rows(where_ref, weight, sems, at, share)
        rows = pl.ds(aligned(jnp.bitwise_xor(where_ref[1], at) * share, share), share)
        inner[:, rows] = (
            product(proj_ref[0], weight[rows, :width], NT)
            + product(proj_ref[1], weight[rows, width : 2 * width], NT)
            + product(proj_ref[2], weight[rows, 2 * width :], NT)
        )

        @pl.when(at == groups - 1)
        def _():
            normed, inv_std = center(image_ref[...].astype(jnp.float32))
            grad_in = inner[...]
            gain_sum[...] = column_sum(grad_in * normed)
            shift_sum[...] = column_sum(grad_in)
            out_ref[...] = (
                res_ref[...] + center_back(grad_in, normed, inv_std, gain_ref[...])
            ).astype(jnp.bfloat16)

    full = lambda at, _: (0, 0)
    line = pl.BlockSpec((1, width), full)
    square = pl.BlockSpec((tokens, width), full)
    return pl.pallas_call(
        body,
        grid_spec=pltpu.PrefetchScalarGridSpec(
            num_scalar_prefetch=1,
            grid=(groups,),
            in_specs=[pl.BlockSpec((3, tokens, width), lambda at, _: (0, 0, 0))]
            + [square, square, line]
            + [ANY] * (1 + len(flat(pieces))),
            out_specs=[square, line, line],
            scratch_shapes=[
                pltpu.VMEM((width, wide), jnp.bfloat16),
                pltpu.VMEM((tokens, width), jnp.float32),
                pltpu.SemaphoreType.DMA((groups,)),
            ],
        ),
        out_shape=[
            jax.ShapeDtypeStruct((tokens, width), jnp.bfloat16),
            jax.ShapeDtypeStruct((1, width), jnp.float32),
            jax.ShapeDtypeStruct((1, width), jnp.float32),
        ],
        cost_estimate=cost(2 * tokens * width * wide, 2 * width * wide),
        compiler_params=params(46),
    )(where, grad_proj, image, grad_res, gain, own, *flat(pieces))


def attention_forward(projected):
    tokens, triple = projected.shape
    width = triple // 3
    count = width // PAIR

    def body(query_ref, key_ref, value_ref, mixed_ref, total_ref):
        values = value_ref[...].T
        halves = []
        for half in range(PAIR // HD):
            lanes = slice(half * HD, (half + 1) * HD)
            scores = product(key_ref[:, lanes], query_ref[:, lanes], NT)
            top = jnp.max(scores, axis=0, keepdims=True)
            weights = jnp.exp(scores - top)
            total = jnp.sum(weights, axis=0, keepdims=True)
            halves.append(product(values[lanes, :], weights.astype(jnp.bfloat16)) / total)
            total_ref[0, half : half + 1, :] = top + jnp.log(total)
        mixed_ref[...] = jnp.concatenate(halves, axis=0).T.astype(jnp.bfloat16)

    def spec(part):
        return pl.BlockSpec((tokens, PAIR), lambda at: (0, part * count + at))

    return pl.pallas_call(
        body,
        grid=(count,),
        in_specs=[spec(0), spec(1), spec(2)],
        out_specs=[
            pl.BlockSpec((tokens, PAIR), lambda at: (0, at)),
            pl.BlockSpec((1, PAIR // HD, tokens), lambda at: (at, 0, 0)),
        ],
        out_shape=[
            jax.ShapeDtypeStruct((tokens, width), jnp.bfloat16),
            jax.ShapeDtypeStruct((count, PAIR // HD, tokens), jnp.float32),
        ],
        cost_estimate=cost(16 * tokens * tokens * width, 8 * tokens * width),
        compiler_params=params(24),
    )(projected, projected, projected)


def attention_backward(projected, grad_mixed, totals):
    tokens, triple = projected.shape
    width = triple // 3
    count = width // PAIR

    def body(query_ref, key_ref, value_ref, grad_ref, total_ref, out_ref, sq_ref, sv_ref):
        keys = key_ref[...].T
        outs_q, outs_k, outs_v = [], [], []
        for half in range(PAIR // HD):
            lanes = slice(half * HD, (half + 1) * HD)
            scores = product(key_ref[:, lanes], query_ref[:, lanes], NT)
            probs = jnp.exp(scores - total_ref[0, half : half + 1, :])
            grad_probs = product(value_ref[:, lanes], grad_ref[:, lanes], NT)
            row_dot = jnp.sum(probs * grad_probs, axis=0, keepdims=True)
            grad_scores = (probs * (grad_probs - row_dot)).astype(jnp.bfloat16)
            outs_q.append(product(keys[lanes, :], grad_scores))
            outs_k.append(product(grad_scores, query_ref[:, lanes]))
            outs_v.append(product(probs.astype(jnp.bfloat16), grad_ref[:, lanes]))
        grad_query = jnp.concatenate(outs_q, axis=0).T * 0.125
        grad_value = jnp.concatenate(outs_v, axis=1)
        out_ref[0] = grad_query.astype(jnp.bfloat16)
        out_ref[1] = jnp.concatenate(outs_k, axis=1).astype(jnp.bfloat16)
        out_ref[2] = grad_value.astype(jnp.bfloat16)
        sq_ref[...] = column_sum(grad_query)
        sv_ref[...] = column_sum(grad_value)

    def spec(part):
        return pl.BlockSpec((tokens, PAIR), lambda at: (0, part * count + at))

    block = pl.BlockSpec((tokens, PAIR), lambda at: (0, at))
    line = pl.BlockSpec((1, PAIR), lambda at: (0, at))
    return pl.pallas_call(
        body,
        grid=(count,),
        in_specs=[spec(0), spec(1), spec(2), block]
        + [pl.BlockSpec((1, PAIR // HD, tokens), lambda at: (at, 0, 0))],
        out_specs=[pl.BlockSpec((3, tokens, PAIR), lambda at: (0, 0, at)), line, line],
        out_shape=[jax.ShapeDtypeStruct((3, tokens, width), jnp.bfloat16)]
        + [jax.ShapeDtypeStruct((1, width), jnp.float32)] * 2,
        cost_estimate=cost(40 * tokens * tokens * width, 16 * tokens * width),
        compiler_params=params(28),
    )(projected, projected, projected, grad_mixed, totals)


def weight_grads(where, pairs):
    tokens, rows = pairs[0][0].shape
    sizes = [pair[4] for pair in pairs]
    parts = [pair[2].shape[0] if pair[2].ndim == 3 else 1 for pair in pairs]
    spans = [size * part for size, part in zip(sizes, parts)]
    width = sum(spans)
    step = 256
    count = rows // step
    half = count // 2
    operands, in_specs = [], []
    for left, left_pair, right, right_pair, _ in pairs:
        operands += [left, left_pair, right, right_pair]
        in_specs += [pl.BlockSpec((tokens, step), lambda at, _: (0, at))] * 2 + [ANY] * 2

    def body(where_ref, *refs):
        ins = refs[: len(operands)]
        send_a, keep_a, send_b, keep_b = refs[len(operands) : len(operands) + 4]
        joined, sems = refs[len(operands) + 4 : -1], refs[-1]
        at = pl.program_id(0)

        @pl.when(at == 0)
        def _():
            for pair, (size, part_count) in enumerate(zip(sizes, parts)):
                for side in range(2):
                    source = ins[4 * pair + 2 + side]
                    for which in range(4):
                        block = jnp.bitwise_xor(where_ref[0], 2 * which)
                        columns = pl.ds(aligned(block * size, LANES), size)
                        for part in range(part_count):
                            begin = (which * part_count + part) * size
                            taken = (
                                source.at[part, :, columns]
                                if part_count > 1
                                else source.at[:, columns]
                            )
                            pltpu.make_async_copy(
                                taken,
                                joined[2 * pair + side].at[:, begin : begin + size],
                                sems.at[2 * pair + side],
                            ).start()
            for which in range(2 * len(pairs)):
                finish(joined[which], sems.at[which])

        results = []
        for pair in range(len(pairs)):
            total = product(ins[4 * pair][...], joined[2 * pair][...], TN)
            total = total + product(ins[4 * pair + 1][...], joined[2 * pair + 1][...], TN)
            results.append(total.astype(jnp.bfloat16))

        def put(targets):
            base = 0
            for pair, span in enumerate(spans):
                for which in range(4):
                    ref, slot = targets[which]
                    ref[slot, :, base : base + span] = results[pair][
                        :, which * span : (which + 1) * span
                    ]
                base += span

        @pl.when(at < half)
        def _():
            put([(keep_a, 0), (send_a, 0), (keep_a, 1), (send_a, 1)])

        @pl.when(at >= half)
        def _():
            put([(keep_b, 0), (keep_b, 1), (send_b, 0), (send_b, 1)])

    spec_a = pl.BlockSpec((2, step, width), lambda at, _: (0, jnp.minimum(at, half - 1), 0))
    spec_b = pl.BlockSpec((2, step, width), lambda at, _: (0, jnp.maximum(at - half, 0), 0))
    return pl.pallas_call(
        body,
        grid_spec=pltpu.PrefetchScalarGridSpec(
            num_scalar_prefetch=1,
            grid=(count,),
            in_specs=in_specs,
            out_specs=[spec_a, spec_a, spec_b, spec_b],
            scratch_shapes=[
                pltpu.VMEM((tokens, 4 * span), jnp.bfloat16) for span in spans for _ in range(2)
            ]
            + [pltpu.SemaphoreType.DMA((2 * len(pairs),))],
        ),
        out_shape=[jax.ShapeDtypeStruct((2, rows // 2, width), jnp.bfloat16)] * 4,
        cost_estimate=cost(16 * rows * tokens * width, 8 * rows * width + 4 * tokens * rows),
        compiler_params=params(30),
    )(where, *operands)


def weight_grads_flipped(where, left, left_pair, right, right_pair, groups):
    tokens, rows = left.shape
    share = rows // groups
    step = min(TILE, share)
    per = share // step
    count = rows // step
    half = count // 2
    span = 4 * LANES

    def body(where_ref, left_ref, pair_ref, right_ref, right_pair_ref, *rest):
        send_a, keep_a, send_b, keep_b, joined, turned, sems = rest
        at = pl.program_id(0)

        @pl.when(at == 0)
        def _():
            for side, source in enumerate((right_ref, right_pair_ref)):
                for which in range(4):
                    block = jnp.bitwise_xor(where_ref[0], 2 * which)
                    columns = pl.ds(aligned(block * LANES, LANES), LANES)
                    pltpu.make_async_copy(
                        source.at[:, columns],
                        joined.at[side, :, which * LANES : (which + 1) * LANES],
                        sems.at[side],
                    ).start()
            for side in range(2):
                finish(joined.at[side], sems.at[side])
                turned[side] = joined[side].T

        total = product(turned[0], left_ref[...]) + product(turned[1], pair_ref[...])
        total = total.astype(jnp.bfloat16)

        def put(targets):
            for which in range(4):
                ref, slot = targets[which]
                ref[slot, 0] = total[which * LANES : (which + 1) * LANES, :]

        @pl.when(at < half)
        def _():
            put([(keep_a, 0), (send_a, 0), (keep_a, 1), (send_a, 1)])

        @pl.when(at >= half)
        def _():
            put([(keep_b, 0), (keep_b, 1), (send_b, 0), (send_b, 1)])

    def spec(clip):
        return pl.BlockSpec(
            (2, 1, LANES, step), lambda at, _: (0, clip(at) // per, 0, clip(at) % per)
        )

    spec_a = spec(lambda at: jnp.minimum(at, half - 1))
    spec_b = spec(lambda at: jnp.maximum(at - half, 0))
    return pl.pallas_call(
        body,
        grid_spec=pltpu.PrefetchScalarGridSpec(
            num_scalar_prefetch=1,
            grid=(count,),
            in_specs=[pl.BlockSpec((tokens, step), lambda at, _: (0, at))] * 2 + [ANY] * 2,
            out_specs=[spec_a, spec_a, spec_b, spec_b],
            scratch_shapes=[
                pltpu.VMEM((2, tokens, span), jnp.bfloat16),
                pltpu.VMEM((2, span, tokens), jnp.bfloat16),
                pltpu.SemaphoreType.DMA((2,)),
            ],
        ),
        out_shape=[jax.ShapeDtypeStruct((2, groups // 2, LANES, share), jnp.bfloat16)] * 4,
        cost_estimate=cost(4 * rows * tokens * span, 2 * rows * span + 4 * tokens * rows),
        compiler_params=params(22),
    )(where, left, left_pair, right, right_pair)


def finish_flipped(where, pieces):
    size, rows = pieces[0].shape
    step = min(rows, 256)

    def body(where_ref, *refs):
        for at in range(BLOCKS):
            block = jnp.bitwise_xor(where_ref[0], at)
            columns = pl.ds(aligned(block * size, LANES), size)
            refs[-1][:, columns] = refs[at][...].astype(jnp.float32).T

    return pl.pallas_call(
        body,
        grid_spec=pltpu.PrefetchScalarGridSpec(
            num_scalar_prefetch=1,
            grid=(rows // step,),
            in_specs=[pl.BlockSpec((size, step), lambda at, _: (0, at))] * BLOCKS,
            out_specs=pl.BlockSpec((step, BLOCKS * size), lambda at, _: (at, 0)),
        ),
        out_shape=jax.ShapeDtypeStruct((rows, BLOCKS * size), jnp.float32),
        compiler_params=params(12),
    )(where, *pieces)


def join_rows(arrays):
    rows, width = arrays[0].shape

    def body(*refs):
        for at, ref in enumerate(refs[:-1]):
            refs[-1][at * rows : (at + 1) * rows, :] = ref[...]

    return pl.pallas_call(
        body,
        out_shape=jax.ShapeDtypeStruct((rows * len(arrays), width), jnp.bfloat16),
        compiler_params=params(12),
    )(*arrays)


def hop_totals(where, rest, got, groups):
    half, width = rest[0].shape
    share = 2 * half // groups

    def body(where_ref, rest_a, rest_b, got_a, got_b, *outs):
        total = outs[-1]
        for at, (left, right) in enumerate(((rest_a, got_a), (rest_b, got_b))):
            total[at * half : (at + 1) * half, :] = left[...].astype(jnp.float32) + right[
                ...
            ].astype(jnp.float32)
        for hop in range(groups):
            first = jnp.bitwise_xor(where_ref[1], hop) * share
            outs[hop][...] = total[pl.ds(aligned(first, share), share), :].astype(jnp.bfloat16)

    whole = lambda shape: pl.BlockSpec(shape, lambda at, _: (0, 0))
    return pl.pallas_call(
        body,
        grid_spec=pltpu.PrefetchScalarGridSpec(
            num_scalar_prefetch=1,
            grid=(1,),
            in_specs=[whole((half, width))] * 4,
            out_specs=[whole((share, width))] * groups,
            scratch_shapes=[pltpu.VMEM((2 * half, width), jnp.float32)],
        ),
        out_shape=[jax.ShapeDtypeStruct((share, width), jnp.bfloat16)] * groups,
        compiler_params=params(12),
    )(where, *rest, *got)


def pick_blocks(where, sources, outs):
    flat_outs = [item for out in outs for item in out]

    def body(where_ref, *refs):
        in_refs, out_refs = refs[: len(flat_outs)], refs[len(flat_outs) :]
        at = 0
        for out_ref, out in zip(out_refs, outs):
            base = 0
            for _, size, _ in out:
                out_ref[:, base : base + size] = in_refs[at][...]
                base += size
                at += 1

    def mine(source, size, part):
        return pl.BlockSpec(
            (sources[source].shape[0], size),
            lambda at, where_ref: (0, part * BLOCKS + where_ref[0]),
        )

    shapes = [(sources[out[0][0]].shape[0], sum(item[1] for item in out)) for out in outs]
    return pl.pallas_call(
        body,
        grid_spec=pltpu.PrefetchScalarGridSpec(
            num_scalar_prefetch=1,
            grid=(1,),
            in_specs=[mine(*item) for item in flat_outs],
            out_specs=[pl.BlockSpec(shape, lambda at, _: (0, 0)) for shape in shapes],
        ),
        out_shape=[jax.ShapeDtypeStruct(shape, jnp.bfloat16) for shape in shapes],
        compiler_params=params(12),
    )(where, *[sources[item[0]] for item in flat_outs])


def unpack_vectors(where, sources, lengths, pair_at, width):
    groups = len(sources)
    row = sources[0].shape[1]
    outs = [3 * width if at == pair_at else length * groups for at, length in enumerate(lengths)]

    def body(where_ref, *refs):
        source_refs, out_refs = refs[:groups], refs[groups:]
        out_refs[pair_at][...] = jnp.zeros((1, 3 * width), jnp.float32)
        for hop in range(groups):
            block = source_refs[hop][...].astype(jnp.float32)
            owner = jnp.bitwise_xor(where_ref[1], hop)
            place = 0
            for which, length in enumerate(lengths):
                start = owner * length
                if which == pair_at:
                    start = start + jnp.where(start >= width, width, 0)
                for begin in range(0, length, LANES):
                    line, lane = (place + begin) // row, (place + begin) % row
                    target = pl.ds(aligned(start + begin, LANES), LANES)
                    out_refs[which][:, target] = block[line : line + 1, lane : lane + LANES]
                place += length

    return pl.pallas_call(
        body,
        grid_spec=pltpu.PrefetchScalarGridSpec(
            num_scalar_prefetch=1,
            grid=(1,),
            in_specs=[pl.BlockSpec((16, row), lambda at, _: (0, 0))] * groups,
            out_specs=[pl.BlockSpec((1, size), lambda at, _: (0, 0)) for size in outs],
        ),
        out_shape=[jax.ShapeDtypeStruct((1, size), jnp.float32) for size in outs],
        compiler_params=params(8),
    )(where, *sources)


def pack_sums(vectors, groups):
    total = sum(vec.shape[1] for vec in vectors) // groups

    def body(*refs):
        for owner in range(groups):
            pieces = []
            for ref in refs[:-1]:
                length = ref.shape[1] // groups
                pieces.append(ref[:, owner * length : (owner + 1) * length])
            refs[-1][owner : owner + 1, :] = jnp.concatenate(pieces, axis=1)

    return pl.pallas_call(
        body,
        out_shape=jax.ShapeDtypeStruct((groups, total), jnp.float32),
        compiler_params=params(8),
    )(*vectors)


def unpack_sums(where, first, second, lengths):
    groups, total = first.shape

    def body(where_ref, first_ref, second_ref, *outs):
        line = jnp.zeros((1, total), jnp.float32)
        for owner in range(groups):
            both = first_ref[owner : owner + 1, :] + second_ref[owner : owner + 1, :]
            line = jnp.where(where_ref[1] == owner, both, line)
        place = 0
        for out, length in zip(outs, lengths):
            out[...] = line[:, place : place + length]
            place += length

    whole = pl.BlockSpec((groups, total), lambda at, _: (0, 0))
    return pl.pallas_call(
        body,
        grid_spec=pltpu.PrefetchScalarGridSpec(
            num_scalar_prefetch=1,
            grid=(1,),
            in_specs=[whole, whole],
            out_specs=[pl.BlockSpec((1, length), lambda at, _: (0, 0)) for length in lengths],
        ),
        out_shape=[jax.ShapeDtypeStruct((1, length), jnp.float32) for length in lengths],
        compiler_params=params(8),
    )(where, first, second)


def finish_blocks(blocks, sizes):
    count, rows, width = blocks.shape
    step = min(rows, 128)

    def body(in_ref, *out_refs):
        base = 0
        for out_ref, size in zip(out_refs, sizes):
            for at in range(count):
                out_ref[:, at * size : (at + 1) * size] = in_ref[
                    at, :, base : base + size
                ].astype(jnp.float32)
            base += size

    return pl.pallas_call(
        body,
        grid=(rows // step,),
        in_specs=[pl.BlockSpec((count, step, width), lambda at: (0, at, 0))],
        out_specs=[pl.BlockSpec((step, count * size), lambda at: (at, 0)) for size in sizes],
        out_shape=[jax.ShapeDtypeStruct((rows, count * size), jnp.float32) for size in sizes],
        compiler_params=params(12),
    )(blocks)


def finish_grads(where, pieces, strips):
    rows = pieces[0].shape[0]
    step = min(rows, 128)
    totals = {}
    for _, size, out, base in strips:
        totals[out] = max(totals.get(out, 0), base + size * BLOCKS)

    def body(where_ref, *refs):
        piece_refs, out_refs = refs[:BLOCKS], refs[BLOCKS:]
        for at in range(BLOCKS):
            block = jnp.bitwise_xor(where_ref[0], at)
            for start, size, out, base in strips:
                target = pl.ds(aligned(base + block * size, LANES), size)
                out_refs[out][:, target] = piece_refs[at][:, start : start + size].astype(
                    jnp.float32
                )

    return pl.pallas_call(
        body,
        grid_spec=pltpu.PrefetchScalarGridSpec(
            num_scalar_prefetch=1,
            grid=(rows // step,),
            in_specs=[
                pl.BlockSpec((step, piece.shape[1]), lambda at, _: (at, 0)) for piece in pieces
            ],
            out_specs=[
                pl.BlockSpec((step, totals[out]), lambda at, _: (at, 0)) for out in sorted(totals)
            ],
        ),
        out_shape=[
            jax.ShapeDtypeStruct((rows, totals[out]), jnp.float32) for out in sorted(totals)
        ],
        compiler_params=params(12),
    )(where, *pieces)


REP, GRP = "rep", "grp"


def exchange(tensor, mask, axis=REP):
    size = lax.axis_size(axis)
    return lax.ppermute(tensor, axis, [(at, at ^ mask) for at in range(size)])


def tie(value, *others):
    return lax.optimization_barrier((value, others))[0]


def all_hops(block):
    return [exchange(block, hop, GRP) for hop in range(1, lax.axis_size(GRP))]


def spread(own):
    by_x = exchange(own, 2)
    by_y = exchange(own, 4)
    half = own.shape[0] // 2
    sent = (by_x[:half], by_y[half:])
    top = exchange(sent[0], 4)
    bottom = exchange(sent[1], 2)
    pieces = []
    for piece in ((own,), (by_x,), (by_y,), (top, bottom)):
        pair = tuple(exchange(array, 1) for array in piece)
        pieces += [piece, pair]
    return pieces, sent


def add_rounded(left, right):
    return (left.astype(jnp.float32) + right.astype(jnp.float32)).astype(jnp.bfloat16)


def first_sends(parts):
    return exchange(parts[0], 2), exchange(parts[2], 4)


def second_sends(parts, got):
    keep_a, keep_b = parts[1], parts[3]
    got_a, got_b = got
    next_a = exchange(add_rounded(keep_a[1], got_a[1]), 4)
    next_b = exchange(add_rounded(keep_b[1], got_b[1]), 2)
    rest_a = add_rounded(keep_a[0], got_a[0])
    rest_b = add_rounded(keep_b[0], got_b[0])
    return (rest_a, rest_b), (next_a, next_b)


def block_total(rest, got):
    total = jnp.concatenate([add_rounded(*pair) for pair in zip(rest, got)], axis=0)
    mask = BLOCKS
    while mask < lax.axis_size(REP):
        total = add_rounded(total, exchange(total, mask))
        mask *= 2
    return total


def scatter(total):
    return lax.psum_scatter(total, GRP, scatter_dimension=0, tiled=True)


def gather(own):
    return lax.all_gather(own, REP, axis=0, tiled=False)[:BLOCKS]


def widened(rest, got):
    mask = BLOCKS
    while mask < lax.axis_size(REP):
        rest = [add_rounded(*pair) for pair in zip(rest, got)]
        got = [exchange(array, mask) for array in rest]
        mask *= 2
    return rest, got


def sum_rounded(own, got):
    total = own.astype(jnp.float32)
    for other in got:
        total = total + other.astype(jnp.float32)
    return total.astype(jnp.bfloat16)


def layer(
    images,
    cotangent,
    ln1_gain,
    ln1_shift,
    qkv_weight,
    qv_bias,
    out_weight,
    out_bias,
    ln2_gain,
    ln2_shift,
    fc1_weight,
    fc1_bias,
    fc2_weight,
    fc2_bias,
):
    groups = lax.axis_size(GRP)
    place = jnp.bitwise_and(lax.axis_index(REP), BLOCKS - 1)
    where = jnp.stack([place, lax.axis_index(GRP)])
    _, width = out_weight.shape
    hidden_block = fc1_weight.shape[1] // BLOCKS

    (block_a,) = pick_blocks(
        where,
        [qkv_weight, out_weight],
        [[(0, LANES, part) for part in range(3)] + [(1, LANES, 0)]],
    )
    got_a = all_hops(block_a)
    vectors = (ln1_gain, ln1_shift, qv_bias, out_bias, ln2_gain, ln2_shift, fc1_bias, fc2_bias)
    sizes = [vec.shape[0] for vec in vectors]
    length = 16 * 2 * LANES
    packed, offset = jnp.zeros((length,), jnp.bfloat16), 0
    for vec, size in zip(vectors, sizes):
        packed = packed + jnp.pad(vec, (offset, length - offset - size))
        offset += size
    packed = packed.reshape(16, 2 * LANES)
    got_v = all_hops(packed)
    block_b, block_c = pick_blocks(
        where,
        [fc1_weight, fc2_weight],
        [[(0, hidden_block, 0)], [(1, LANES, 0)]],
    )
    got_b = all_hops(block_b)
    got_c = all_hops(block_c)
    pieces_a, sent_a = spread(join_rows(got_a))
    pieces_b, sent_b = spread(join_rows(tie(got_b, sent_a)))
    pieces_c, _ = spread(join_rows(tie(got_c, sent_b)))
    gain_1, shift_1, bias_in, bias_attn, gain_2, shift_2, bias_up, bias_down = unpack_vectors(
        where, [packed] + got_v, sizes, 2, width
    )

    image = images[0]
    grad_block = cotangent[0]
    cot_pair = exchange(grad_block, 1)

    normed_in, projected = qkv_forward(where, image, gain_1, shift_1, bias_in, qkv_weight, pieces_a)
    normed_pair = exchange(normed_in, 1)
    attended, totals = attention_forward(projected)
    attended_pair = exchange(attended, 1)
    residual, normed_mid = out_forward(
        where, image, attended, bias_attn, gain_2, shift_2, out_weight, pieces_a, 3 * LANES
    )
    mid_pair = exchange(normed_mid, 1)
    active, slope = up_forward(where, normed_mid, bias_up, fc1_weight, pieces_b)
    active_pair = exchange(active, 1)

    down_parts = weight_grads_flipped(
        where, active, active_pair, grad_block, cot_pair, groups
    )
    down_got = first_sends(down_parts)
    grad_pre, sum_up = down_backward(
        tie(where, down_parts), grad_block, slope, fc2_weight, pieces_c
    )
    pre_pair = exchange(grad_pre, 1)
    middle = middle_backward(
        where,
        grad_pre,
        grad_block,
        residual,
        gain_2,
        fc1_weight,
        out_weight,
        pieces_b,
        pieces_a,
        hidden_block,
    )
    grad_res, grad_res_b, grad_attended, sum_gain_2, sum_shift_2, sum_res, sum_top = middle
    res_pair = exchange(grad_res_b, 1)
    down_rest, down_got = second_sends(down_parts, tie(down_got, grad_res))
    up_parts = weight_grads(
        tie(where, grad_res, down_rest),
        [
            (normed_mid, mid_pair, grad_pre, pre_pair, hidden_block),
            (attended, attended_pair, grad_res_b, res_pair, LANES),
        ],
    )
    up_got = first_sends(up_parts)
    down_total = block_total(down_rest, tie(down_got, up_parts))
    down_own = scatter(down_total)
    grad_proj, sum_query, sum_value = attention_backward(
        projected, tie(grad_attended, up_parts, down_total), totals
    )
    proj_pair = exchange(grad_proj, 1)
    up_rest, up_got = second_sends(up_parts, tie(up_got, grad_proj))
    qkv_parts = weight_grads(
        tie(where, up_rest), [(normed_in, normed_pair, grad_proj, proj_pair, LANES)]
    )
    qkv_got = first_sends(qkv_parts)
    up_total = block_total(up_rest, tie(up_got, qkv_parts))
    up_own = scatter(up_total)
    input_grad, sum_gain_1, sum_shift_1 = qkv_backward(
        tie(where, qkv_parts, up_total),
        grad_proj,
        image,
        grad_res,
        gain_1,
        qkv_weight,
        pieces_a,
    )
    sums = pack_sums(
        [
            sum_gain_1,
            sum_shift_1,
            jnp.concatenate([sum_query, sum_value], axis=1),
            sum_res,
            sum_gain_2,
            sum_shift_2,
            sum_up,
            sum_top,
        ],
        groups,
    )
    got = exchange(sums, 1)
    qkv_rest, qkv_got = second_sends(qkv_parts, tie(qkv_got, sums))
    sums = sums + tie(got, qkv_rest)
    got = exchange(sums, 2)
    block_out = down_forward(
        tie(where, input_grad, sums, qkv_rest), residual, active, bias_down, fc2_weight, pieces_c
    )
    sums = sums + tie(got, block_out)
    mask = BLOCKS
    while mask < lax.axis_size(REP):
        sums = sums + exchange(sums, mask)
        mask *= 2
    qkv_rest, qkv_got = widened(qkv_rest, tie(qkv_got, block_out, sums))
    own, *qkv_sent = hop_totals(where, qkv_rest, qkv_got, groups)
    qkv_got = [exchange(sent, hop, GRP) for hop, sent in enumerate(qkv_sent, start=1)]
    down_own = tie(down_own, own)[0]
    down_x = exchange(down_own, 2)
    down_y = exchange(down_own, 4)
    up_blocks = gather(tie(up_own, own))
    sums = sums + exchange(tie(sums, own), 4)
    down_both = exchange(tie(down_x, sums), 4)
    own = sum_rounded(own, tie(qkv_got, sums, down_x, down_y))
    by_x = exchange(own, 2)
    by_y = exchange(own, 4)
    mask = 1
    while mask * 2 < groups:
        sums = sums + exchange(tie(sums, own), mask, GRP)
        mask *= 2
    down_pieces = []
    for piece in (down_own, down_x, down_y, down_both):
        down_pieces += [piece, exchange(piece, 1)]
    both = exchange(tie(by_x, sums), 4)
    last = exchange(tie(sums, by_x), mask, GRP)
    grad_down = finish_flipped(tie(where, own), down_pieces)
    qkv_pieces = []
    for piece in (own, by_x, by_y, both):
        qkv_pieces += [piece, exchange(piece, 1)]
    grad_up, grad_out = finish_blocks(tie(up_blocks, grad_down, by_x, by_y), [hidden_block, LANES])
    (grad_qkv,) = finish_grads(
        where, qkv_pieces, [(at * LANES, LANES, 0, at * width) for at in range(3)]
    )
    sums = [vec.reshape(-1) for vec in unpack_sums(where, sums, last, sizes)]
    return (
        block_out[None],
        input_grad[None],
        sums[0],
        sums[1],
        grad_qkv,
        sums[2],
        grad_out,
        sums[3],
        sums[4],
        sums[5],
        grad_up,
        sums[6],
        grad_down,
        sums[7],
    )


def solution(mesh):
    tokens = P((REP, GRP), None, None)
    vector, matrix = P(GRP), P(GRP, None)
    weights = (vector, vector, matrix, vector, matrix, vector)
    weights += (vector, vector, matrix, vector, matrix, vector)
    specs = (tokens, tokens) + weights
    return jax.shard_map(layer, mesh=mesh, in_specs=specs, out_specs=specs, check_vma=False)
```

```python
import jax
import jax.numpy as jnp
from jax import lax
from jax.experimental import pallas as pl
from jax.experimental.pallas import tpu as pltpu
from jax.sharding import PartitionSpec as P


BLOCKS = 8
ROW, PART, BLOCK = range(3)
LANES = 128
TILE = 512
HD = 64
PAIR = 128
EPS = 1e-06

root_half = 0.7071067811865476
inv_root_tau = 0.3989422804014327

NN = (((1,), (0,)), ((), ()))
NT = (((1,), (1,)), ((), ()))
TN = (((0,), (0,)), ((), ()))
ANY = pl.BlockSpec(memory_space=pl.ANY)


def product(left, right, dims=NN):
    return lax.dot_general(left, right, dims, preferred_element_type=jnp.float32)


def aligned(start, unit):
    return pl.multiple_of(start, unit)


def params(mebibytes=60):
    return pltpu.CompilerParams(vmem_limit_bytes=mebibytes << 20)


def cost(flops, moved):
    return pl.CostEstimate(flops=int(flops), bytes_accessed=int(moved), transcendentals=0)


def start_loads(where, own, pieces, strips, target, sems, mode):
    share = own.shape[0]
    groups = target.shape[0] // share
    mine = where[1]

    def go(source, rows, columns, key):
        pltpu.make_async_copy(source, target.at[rows, columns], sems.at[key]).start()

    own_rows = pl.ds(aligned(mine * share, share), share)
    if mode == ROW:
        pltpu.make_async_copy(own, target.at[own_rows, :], sems.at[0]).start()
    for which, (source, size, base) in enumerate(strips):
        for at in range(BLOCKS):
            block = jnp.bitwise_xor(where[0], at)
            columns = pl.ds(aligned(base + block * size, LANES), size)
            key = which if mode == PART else at
            if mode != ROW:
                go(own.at[:, columns], own_rows, columns, key)
            for hop in range(1, groups):
                first = jnp.bitwise_xor(mine, hop) * share
                low = 0
                for ref in pieces[at]:
                    high = low + ref.shape[0]
                    begin, end = max(low, (hop - 1) * share), min(high, hop * share)
                    if begin < end:
                        shift = begin - (hop - 1) * share
                        rows = pl.ds(aligned(first + shift, 16), end - begin)
                        go(
                            ref.at[begin - low : end - low, source : source + size],
                            rows,
                            columns,
                            hop if mode == ROW else key,
                        )
                    low = high


def finish(region, sem):
    pltpu.make_async_copy(region, region, sem).wait()


def wait_rows(where, target, sems, hop, share):
    rows = pl.ds(aligned(jnp.bitwise_xor(where[1], hop) * share, share), share)
    finish(target.at[rows, :], sems.at[hop])


def flat(pieces):
    return [array for piece in pieces for array in piece]


def regroup(refs, pieces):
    grouped, at = [], 0
    for piece in pieces:
        grouped.append(refs[at : at + len(piece)])
        at += len(piece)
    return grouped


def center(values):
    mean = jnp.mean(values, axis=-1, keepdims=True)
    centred = values - mean
    inv_std = lax.rsqrt(jnp.mean(centred * centred, axis=-1, keepdims=True) + EPS)
    return centred * inv_std, inv_std


def center_back(grad_out, normed, inv_std, gain):
    grad_hat = grad_out * gain
    return inv_std * (
        grad_hat
        - jnp.mean(grad_hat, axis=-1, keepdims=True)
        - normed * jnp.mean(grad_hat * normed, axis=-1, keepdims=True)
    )


def column_sum(values):
    return jnp.sum(values, axis=0, keepdims=True)


def qkv_forward(where, image, gain, shift, bias, own, pieces):
    tokens, width = image.shape
    wide = own.shape[1]
    per = width // TILE
    strips = [(part * LANES, LANES, part * width) for part in range(3)]

    def body(where_ref, image_ref, gain_ref, shift_ref, bias_ref, own_ref, *rest):
        piece_refs = regroup(rest[: len(flat(pieces))], pieces)
        normed_ref, out_ref, weight, sems = rest[len(flat(pieces)) :]
        at = pl.program_id(0)

        @pl.when(at == 0)
        def _():
            start_loads(where_ref, own_ref, piece_refs, strips, weight, sems, PART)
            normed, _ = center(image_ref[...].astype(jnp.float32))
            normed_ref[...] = (normed * gain_ref[...] + shift_ref[...]).astype(jnp.bfloat16)

        for part in range(3):

            @pl.when(at == part * per)
            def _(part=part):
                finish(weight.at[:, part * width : (part + 1) * width], sems.at[part])

        columns = pl.ds(aligned(at * TILE, TILE), TILE)
        total = product(normed_ref[...], weight[:, columns]) + bias_ref[...]
        scale = jnp.where(at < per, 0.125, 1.0)
        out_ref[...] = (total * scale).astype(jnp.bfloat16)

    full = lambda at, _: (0, 0)
    return pl.pallas_call(
        body,
        grid_spec=pltpu.PrefetchScalarGridSpec(
            num_scalar_prefetch=1,
            grid=(wide // TILE,),
            in_specs=[
                pl.BlockSpec((tokens, width), full),
                pl.BlockSpec((1, width), full),
                pl.BlockSpec((1, width), full),
                pl.BlockSpec((1, TILE), lambda at, _: (0, at)),
            ]
            + [ANY] * (1 + len(flat(pieces))),
            out_specs=[
                pl.BlockSpec((tokens, width), full),
                pl.BlockSpec((tokens, TILE), lambda at, _: (0, at)),
            ],
            scratch_shapes=[
                pltpu.VMEM((width, wide), jnp.bfloat16),
                pltpu.SemaphoreType.DMA((3,)),
            ],
        ),
        out_shape=[
            jax.ShapeDtypeStruct((tokens, width), jnp.bfloat16),
            jax.ShapeDtypeStruct((tokens, wide), jnp.bfloat16),
        ],
        cost_estimate=cost(2 * tokens * width * wide, 2 * width * wide),
        compiler_params=params(22),
    )(where, image, gain, shift, bias, own, *flat(pieces))


def out_forward(where, image, attended, bias, gain, shift, own, pieces, source):
    tokens, width = image.shape
    share = own.shape[0]
    groups = width // share
    chunk = 256

    def body(where_ref, image_ref, attended_ref, bias_ref, gain_ref, shift_ref, own_ref, *rest):
        piece_refs = regroup(rest[: len(flat(pieces))], pieces)
        residual_ref, normed_ref, weight, sems = rest[len(flat(pieces)) :]
        start_loads(where_ref, own_ref, piece_refs, [(source, LANES, 0)], weight, sems, ROW)
        for hop in range(groups):
            wait_rows(where_ref, weight, sems, hop, share)

        @pl.loop(0, width // chunk)
        def _(at):
            columns = pl.ds(aligned(at * chunk, chunk), chunk)
            residual_ref[:, columns] = (
                image_ref[:, columns].astype(jnp.float32)
                + product(attended_ref[...], weight[:, columns])
                + bias_ref[:, columns]
            )

        normed, _ = center(residual_ref[...])
        normed_ref[...] = (normed * gain_ref[...] + shift_ref[...]).astype(jnp.bfloat16)

    full = lambda at, _: (0, 0)
    return pl.pallas_call(
        body,
        grid_spec=pltpu.PrefetchScalarGridSpec(
            num_scalar_prefetch=1,
            grid=(1,),
            in_specs=[pl.BlockSpec((tokens, width), full)] * 2
            + [pl.BlockSpec((1, width), full)] * 3
            + [ANY] * (1 + len(flat(pieces))),
            out_specs=[pl.BlockSpec((tokens, width), full)] * 2,
            scratch_shapes=[
                pltpu.VMEM((width, width), jnp.bfloat16),
                pltpu.SemaphoreType.DMA((groups,)),
            ],
        ),
        out_shape=[
            jax.ShapeDtypeStruct((tokens, width), jnp.float32),
            jax.ShapeDtypeStruct((tokens, width), jnp.bfloat16),
        ],
        cost_estimate=cost(2 * tokens * width * width, 2 * width * width),
        compiler_params=params(32),
    )(where, image, attended, bias, gain, shift, own, *flat(pieces))


def up_forward(where, normed, bias, own, pieces):
    tokens, width = normed.shape
    wide = own.shape[1]
    size = wide // BLOCKS

    def body(where_ref, normed_ref, bias_ref, own_ref, *rest):
        piece_refs = regroup(rest[: len(flat(pieces))], pieces)
        active_ref, slope_ref, weight, sems = rest[len(flat(pieces)) :]
        at = pl.program_id(0)

        @pl.when(at == 0)
        def _():
            start_loads(where_ref, own_ref, piece_refs, [(0, size, 0)], weight, sems, BLOCK)

        for which in range(2):
            block = jnp.bitwise_xor(where_ref[0], 2 * at + which)
            finish(
                weight.at[:, pl.ds(aligned(block * size, size), size)], sems.at[2 * at + which]
            )
        pair = jnp.bitwise_xor(where_ref[0], 2 * at) // 2
        columns = pl.ds(aligned(pair * 2 * size, size), 2 * size)
        pre_act = product(normed_ref[...], weight[:, columns]) + bias_ref[...]
        cdf = 0.5 * (1.0 + lax.erf(pre_act * root_half))
        density = jnp.exp(-0.5 * pre_act * pre_act) * inv_root_tau
        active_ref[...] = (pre_act * cdf).astype(jnp.bfloat16)
        slope_ref[...] = (cdf + pre_act * density).astype(jnp.bfloat16)

    full = lambda at, _: (0, 0)
    mine = lambda at, where_ref: (0, jnp.bitwise_xor(where_ref[0], 2 * at) // 2)
    return pl.pallas_call(
        body,
        grid_spec=pltpu.PrefetchScalarGridSpec(
            num_scalar_prefetch=1,
            grid=(BLOCKS // 2,),
            in_specs=[pl.BlockSpec((tokens, width), full), pl.BlockSpec((1, 2 * size), mine)]
            + [ANY] * (1 + len(flat(pieces))),
            out_specs=[pl.BlockSpec((tokens, 2 * size), mine)] * 2,
            scratch_shapes=[
                pltpu.VMEM((width, wide), jnp.bfloat16),
                pltpu.SemaphoreType.DMA((BLOCKS,)),
            ],
        ),
        out_shape=[jax.ShapeDtypeStruct((tokens, wide), jnp.bfloat16)] * 2,
        cost_estimate=cost(2 * tokens * width * wide, 2 * width * wide),
        compiler_params=params(38),
    )(where, normed, bias, own, *flat(pieces))


def down_forward(where, residual, active, bias, own, pieces):
    tokens, wide = active.shape
    width = residual.shape[1]
    chunk = 2 * LANES

    def body(where_ref, residual_ref, active_ref, bias_ref, own_ref, *rest):
        piece_refs = regroup(rest[: len(flat(pieces))], pieces)
        out_ref, weight, sems = rest[len(flat(pieces)) :]
        at = pl.program_id(0)

        @pl.when(at == 0)
        def _():
            start_loads(where_ref, own_ref, piece_refs, [(0, LANES, 0)], weight, sems, BLOCK)

        for which in range(2):
            block = jnp.bitwise_xor(where_ref[0], 2 * at + which)
            finish(
                weight.at[:, pl.ds(aligned(block * LANES, LANES), LANES)],
                sems.at[2 * at + which],
            )
        pair = jnp.bitwise_xor(where_ref[0], 2 * at) // 2
        columns = pl.ds(aligned(pair * chunk, chunk), chunk)
        out_ref[...] = (
            residual_ref[...] + product(active_ref[...], weight[:, columns]) + bias_ref[...]
        ).astype(jnp.bfloat16)

    block = lambda at, where_ref: (0, jnp.bitwise_xor(where_ref[0], 2 * at) // 2)
    return pl.pallas_call(
        body,
        grid_spec=pltpu.PrefetchScalarGridSpec(
            num_scalar_prefetch=1,
            grid=(width // chunk,),
            in_specs=[
                pl.BlockSpec((tokens, chunk), block),
                pl.BlockSpec((tokens, wide), lambda at, _: (0, 0)),
                pl.BlockSpec((1, chunk), block),
            ]
            + [ANY] * (1 + len(flat(pieces))),
            out_specs=pl.BlockSpec((tokens, chunk), block),
            scratch_shapes=[
                pltpu.VMEM((wide, width), jnp.bfloat16),
                pltpu.SemaphoreType.DMA((BLOCKS,)),
            ],
        ),
        out_shape=jax.ShapeDtypeStruct((tokens, width), jnp.bfloat16),
        cost_estimate=cost(2 * tokens * width * wide, 2 * width * wide),
        compiler_params=params(60),
    )(where, residual, active, bias, own, *flat(pieces))


def down_backward(where, grad_block, slope, own, pieces):
    tokens, wide = slope.shape
    width = grad_block.shape[1]
    share = own.shape[0]
    groups = wide // share
    tile = min(2 * TILE, share)
    per = share // tile

    def body(where_ref, grad_ref, slope_ref, own_ref, *rest):
        piece_refs = regroup(rest[: len(flat(pieces))], pieces)
        out_ref, sum_ref, weight, sems = rest[len(flat(pieces)) :]
        at = pl.program_id(0)

        @pl.when(at == 0)
        def _():
            start_loads(where_ref, own_ref, piece_refs, [(0, LANES, 0)], weight, sems, ROW)

        hop = at // per

        @pl.when(at % per == 0)
        def _():
            wait_rows(where_ref, weight, sems, hop, share)

        row = jnp.bitwise_xor(where_ref[1], hop) * share + (at % per) * tile
        rows = pl.ds(aligned(row, tile), tile)
        grad_pre = product(grad_ref[...], weight[rows, :], NT) * slope_ref[...].astype(jnp.float32)
        out_ref[...] = grad_pre.astype(jnp.bfloat16)
        sum_ref[...] = column_sum(grad_pre)

    mine = lambda at, where_ref: (0, jnp.bitwise_xor(where_ref[1], at // per) * per + at % per)
    return pl.pallas_call(
        body,
        grid_spec=pltpu.PrefetchScalarGridSpec(
            num_scalar_prefetch=1,
            grid=(wide // tile,),
            in_specs=[
                pl.BlockSpec((tokens, width), lambda at, _: (0, 0)),
                pl.BlockSpec((tokens, tile), mine),
            ]
            + [ANY] * (1 + len(flat(pieces))),
            out_specs=[pl.BlockSpec((tokens, tile), mine), pl.BlockSpec((1, tile), mine)],
            scratch_shapes=[
                pltpu.VMEM((wide, width), jnp.bfloat16),
                pltpu.SemaphoreType.DMA((groups,)),
            ],
        ),
        out_shape=[
            jax.ShapeDtypeStruct((tokens, wide), jnp.bfloat16),
            jax.ShapeDtypeStruct((1, wide), jnp.float32),
        ],
        cost_estimate=cost(2 * tokens * width * wide, 2 * width * wide),
        compiler_params=params(60),
    )(where, grad_block, slope, own, *flat(pieces))


def middle_backward(where, grad_pre, grad_block, residual, gain, own_up, own_out, pieces, pieces_out, size):
    tokens, wide = grad_pre.shape
    width = grad_block.shape[1]
    share = own_up.shape[0]
    groups = width // share
    chunk = 256

    def body(where_ref, pre_ref, block_ref, residual_ref, gain_ref, up_ref, own_ref, *rest):
        piece_refs = regroup(rest[: len(flat(pieces))], pieces)
        rest = rest[len(flat(pieces)) :]
        out_piece_refs = regroup(rest[: len(flat(pieces_out))], pieces_out)
        rest = rest[len(flat(pieces_out)) :]
        (full_ref, half_ref, att_ref, gain_sum, shift_sum, res_sum, top_sum) = rest[:7]
        weight, weight_out, middle, sems, out_sems = rest[7:]
        at = pl.program_id(0)

        @pl.when(at == 0)
        def _():
            start_loads(where_ref, up_ref, piece_refs, [(0, size, 0)], weight, sems, ROW)
            start_loads(
                where_ref,
                own_ref,
                out_piece_refs,
                [(3 * LANES, LANES, 0)],
                weight_out,
                out_sems,
                ROW,
            )

        wait_rows(where_ref, weight, sems, at, share)
        rows = pl.ds(aligned(jnp.bitwise_xor(where_ref[1], at) * share, share), share)
        middle[:, rows] = product(pre_ref[...], weight[rows, :], NT)

        @pl.when(at == groups - 1)
        def _():
            normed, inv_std = center(residual_ref[...])
            grad_mid = middle[...]
            gain_sum[...] = column_sum(grad_mid * normed)
            shift_sum[...] = column_sum(grad_mid)
            top = block_ref[...].astype(jnp.float32)
            top_sum[...] = column_sum(top)
            grad_res = top + center_back(grad_mid, normed, inv_std, gain_ref[...])
            full_ref[...] = grad_res
            res_sum[...] = column_sum(grad_res)
            half_ref[...] = grad_res.astype(jnp.bfloat16)
            for hop in range(groups):
                wait_rows(where_ref, weight_out, out_sems, hop, share)

            @pl.loop(0, width // chunk)
            def _(step):
                part = pl.ds(aligned(step * chunk, chunk), chunk)
                att_ref[:, part] = product(half_ref[...], weight_out[part, :], NT).astype(
                    jnp.bfloat16
                )

    full = lambda at, _: (0, 0)
    line = pl.BlockSpec((1, width), full)
    square = pl.BlockSpec((tokens, width), full)
    return pl.pallas_call(
        body,
        grid_spec=pltpu.PrefetchScalarGridSpec(
            num_scalar_prefetch=1,
            grid=(groups,),
            in_specs=[pl.BlockSpec((tokens, wide), full), square, square, line]
            + [ANY] * (2 + len(flat(pieces)) + len(flat(pieces_out))),
            out_specs=[square] * 3 + [line] * 4,
            scratch_shapes=[
                pltpu.VMEM((width, wide), jnp.bfloat16),
                pltpu.VMEM((width, width), jnp.bfloat16),
                pltpu.VMEM((tokens, width), jnp.float32),
                pltpu.SemaphoreType.DMA((groups,)),
                pltpu.SemaphoreType.DMA((groups,)),
            ],
        ),
        out_shape=[
            jax.ShapeDtypeStruct((tokens, width), jnp.float32),
            jax.ShapeDtypeStruct((tokens, width), jnp.bfloat16),
            jax.ShapeDtypeStruct((tokens, width), jnp.bfloat16),
        ]
        + [jax.ShapeDtypeStruct((1, width), jnp.float32)] * 4,
        cost_estimate=cost(2 * tokens * width * (wide + width), 2 * width * (wide + width)),
        compiler_params=params(),
    )(where, grad_pre, grad_block, residual, gain, own_up, own_out, *flat(pieces), *flat(pieces_out))


def qkv_backward(where, grad_proj, image, grad_res, gain, own, pieces):
    tokens, width = image.shape
    wide = own.shape[1]
    share = own.shape[0]
    groups = width // share
    strips = [(part * LANES, LANES, part * width) for part in range(3)]

    def body(where_ref, proj_ref, image_ref, res_ref, gain_ref, own_ref, *rest):
        piece_refs = regroup(rest[: len(flat(pieces))], pieces)
        out_ref, gain_sum, shift_sum, weight, inner, sems = rest[len(flat(pieces)) :]
        at = pl.program_id(0)

        @pl.when(at == 0)
        def _():
            start_loads(where_ref, own_ref, piece_refs, strips, weight, sems, ROW)

        wait_rows(where_ref, weight, sems, at, share)
        rows = pl.ds(aligned(jnp.bitwise_xor(where_ref[1], at) * share, share), share)
        inner[:, rows] = (
            product(proj_ref[0], weight[rows, :width], NT)
            + product(proj_ref[1], weight[rows, width : 2 * width], NT)
            + product(proj_ref[2], weight[rows, 2 * width :], NT)
        )

        @pl.when(at == groups - 1)
        def _():
            normed, inv_std = center(image_ref[...].astype(jnp.float32))
            grad_in = inner[...]
            gain_sum[...] = column_sum(grad_in * normed)
            shift_sum[...] = column_sum(grad_in)
            out_ref[...] = (
                res_ref[...] + center_back(grad_in, normed, inv_std, gain_ref[...])
            ).astype(jnp.bfloat16)

    full = lambda at, _: (0, 0)
    line = pl.BlockSpec((1, width), full)
    square = pl.BlockSpec((tokens, width), full)
    return pl.pallas_call(
        body,
        grid_spec=pltpu.PrefetchScalarGridSpec(
            num_scalar_prefetch=1,
            grid=(groups,),
            in_specs=[pl.BlockSpec((3, tokens, width), lambda at, _: (0, 0, 0))]
            + [square, square, line]
            + [ANY] * (1 + len(flat(pieces))),
            out_specs=[square, line, line],
            scratch_shapes=[
                pltpu.VMEM((width, wide), jnp.bfloat16),
                pltpu.VMEM((tokens, width), jnp.float32),
                pltpu.SemaphoreType.DMA((groups,)),
            ],
        ),
        out_shape=[
            jax.ShapeDtypeStruct((tokens, width), jnp.bfloat16),
            jax.ShapeDtypeStruct((1, width), jnp.float32),
            jax.ShapeDtypeStruct((1, width), jnp.float32),
        ],
        cost_estimate=cost(2 * tokens * width * wide, 2 * width * wide),
        compiler_params=params(60),
    )(where, grad_proj, image, grad_res, gain, own, *flat(pieces))


def attention_forward(projected):
    tokens, triple = projected.shape
    width = triple // 3
    count = width // PAIR

    def body(query_ref, key_ref, value_ref, mixed_ref, total_ref):
        values = value_ref[...].T
        halves = []
        for half in range(PAIR // HD):
            lanes = slice(half * HD, (half + 1) * HD)
            scores = product(key_ref[:, lanes], query_ref[:, lanes], NT)
            top = jnp.max(scores, axis=0, keepdims=True)
            weights = jnp.exp(scores - top)
            total = jnp.sum(weights, axis=0, keepdims=True)
            halves.append(product(values[lanes, :], weights.astype(jnp.bfloat16)) / total)
            total_ref[0, half : half + 1, :] = top + jnp.log(total)
        mixed_ref[...] = jnp.concatenate(halves, axis=0).T.astype(jnp.bfloat16)

    def spec(part):
        return pl.BlockSpec((tokens, PAIR), lambda at: (0, part * count + at))

    return pl.pallas_call(
        body,
        grid=(count,),
        in_specs=[spec(0), spec(1), spec(2)],
        out_specs=[
            pl.BlockSpec((tokens, PAIR), lambda at: (0, at)),
            pl.BlockSpec((1, PAIR // HD, tokens), lambda at: (at, 0, 0)),
        ],
        out_shape=[
            jax.ShapeDtypeStruct((tokens, width), jnp.bfloat16),
            jax.ShapeDtypeStruct((count, PAIR // HD, tokens), jnp.float32),
        ],
        cost_estimate=cost(16 * tokens * tokens * width, 8 * tokens * width),
        compiler_params=params(24),
    )(projected, projected, projected)


def attention_backward(projected, grad_mixed, totals):
    tokens, triple = projected.shape
    width = triple // 3
    count = width // PAIR

    def body(query_ref, key_ref, value_ref, grad_ref, total_ref, out_ref, sq_ref, sv_ref):
        keys = key_ref[...].T
        outs_q, outs_k, outs_v = [], [], []
        for half in range(PAIR // HD):
            lanes = slice(half * HD, (half + 1) * HD)
            scores = product(key_ref[:, lanes], query_ref[:, lanes], NT)
            probs = jnp.exp(scores - total_ref[0, half : half + 1, :])
            grad_probs = product(value_ref[:, lanes], grad_ref[:, lanes], NT)
            row_dot = jnp.sum(probs * grad_probs, axis=0, keepdims=True)
            grad_scores = (probs * (grad_probs - row_dot)).astype(jnp.bfloat16)
            outs_q.append(product(keys[lanes, :], grad_scores))
            outs_k.append(product(grad_scores, query_ref[:, lanes]))
            outs_v.append(product(probs.astype(jnp.bfloat16), grad_ref[:, lanes]))
        grad_query = jnp.concatenate(outs_q, axis=0).T * 0.125
        grad_value = jnp.concatenate(outs_v, axis=1)
        out_ref[0] = grad_query.astype(jnp.bfloat16)
        out_ref[1] = jnp.concatenate(outs_k, axis=1).astype(jnp.bfloat16)
        out_ref[2] = grad_value.astype(jnp.bfloat16)
        sq_ref[...] = column_sum(grad_query)
        sv_ref[...] = column_sum(grad_value)

    def spec(part):
        return pl.BlockSpec((tokens, PAIR), lambda at: (0, part * count + at))

    block = pl.BlockSpec((tokens, PAIR), lambda at: (0, at))
    line = pl.BlockSpec((1, PAIR), lambda at: (0, at))
    return pl.pallas_call(
        body,
        grid=(count,),
        in_specs=[spec(0), spec(1), spec(2), block]
        + [pl.BlockSpec((1, PAIR // HD, tokens), lambda at: (at, 0, 0))],
        out_specs=[pl.BlockSpec((3, tokens, PAIR), lambda at: (0, 0, at)), line, line],
        out_shape=[jax.ShapeDtypeStruct((3, tokens, width), jnp.bfloat16)]
        + [jax.ShapeDtypeStruct((1, width), jnp.float32)] * 2,
        cost_estimate=cost(40 * tokens * tokens * width, 16 * tokens * width),
        compiler_params=params(60),
    )(projected, projected, projected, grad_mixed, totals)


def weight_grads(where, pairs):
    tokens, rows = pairs[0][0].shape
    sizes = [pair[4] for pair in pairs]
    parts = [pair[2].shape[0] if pair[2].ndim == 3 else 1 for pair in pairs]
    spans = [size * part for size, part in zip(sizes, parts)]
    width = sum(spans)
    step = 256
    count = rows // step
    half = count // 2
    operands, in_specs = [], []
    for left, left_pair, right, right_pair, _ in pairs:
        operands += [left, left_pair, right, right_pair]
        in_specs += [pl.BlockSpec((tokens, step), lambda at, _: (0, at))] * 2 + [ANY] * 2

    def body(where_ref, *refs):
        ins = refs[: len(operands)]
        send_a, keep_a, send_b, keep_b = refs[len(operands) : len(operands) + 4]
        joined, sems = refs[len(operands) + 4 : -1], refs[-1]
        at = pl.program_id(0)

        @pl.when(at == 0)
        def _():
            for pair, (size, part_count) in enumerate(zip(sizes, parts)):
                for side in range(2):
                    source = ins[4 * pair + 2 + side]
                    for which in range(4):
                        block = jnp.bitwise_xor(where_ref[0], 2 * which)
                        columns = pl.ds(aligned(block * size, LANES), size)
                        for part in range(part_count):
                            begin = (which * part_count + part) * size
                            taken = (
                                source.at[part, :, columns]
                                if part_count > 1
                                else source.at[:, columns]
                            )
                            pltpu.make_async_copy(
                                taken,
                                joined[2 * pair + side].at[:, begin : begin + size],
                                sems.at[2 * pair + side],
                            ).start()
            for which in range(2 * len(pairs)):
                finish(joined[which], sems.at[which])

        results = []
        for pair in range(len(pairs)):
            total = product(ins[4 * pair][...], joined[2 * pair][...], TN)
            total = total + product(ins[4 * pair + 1][...], joined[2 * pair + 1][...], TN)
            results.append(total.astype(jnp.bfloat16))

        def put(targets):
            base = 0
            for pair, span in enumerate(spans):
                for which in range(4):
                    ref, slot = targets[which]
                    ref[slot, :, base : base + span] = results[pair][
                        :, which * span : (which + 1) * span
                    ]
                base += span

        @pl.when(at < half)
        def _():
            put([(keep_a, 0), (send_a, 0), (keep_a, 1), (send_a, 1)])

        @pl.when(at >= half)
        def _():
            put([(keep_b, 0), (keep_b, 1), (send_b, 0), (send_b, 1)])

    spec_a = pl.BlockSpec((2, step, width), lambda at, _: (0, jnp.minimum(at, half - 1), 0))
    spec_b = pl.BlockSpec((2, step, width), lambda at, _: (0, jnp.maximum(at - half, 0), 0))
    return pl.pallas_call(
        body,
        grid_spec=pltpu.PrefetchScalarGridSpec(
            num_scalar_prefetch=1,
            grid=(count,),
            in_specs=in_specs,
            out_specs=[spec_a, spec_a, spec_b, spec_b],
            scratch_shapes=[
                pltpu.VMEM((tokens, 4 * span), jnp.bfloat16) for span in spans for _ in range(2)
            ]
            + [pltpu.SemaphoreType.DMA((2 * len(pairs),))],
        ),
        out_shape=[jax.ShapeDtypeStruct((2, rows // 2, width), jnp.bfloat16)] * 4,
        cost_estimate=cost(16 * rows * tokens * width, 8 * rows * width + 4 * tokens * rows),
        compiler_params=params(30),
    )(where, *operands)


def weight_grads_flipped(where, left, left_pair, right, right_pair, groups):
    tokens, rows = left.shape
    share = rows // groups
    step = min(TILE, share)
    per = share // step
    count = rows // step
    half = count // 2
    span = 4 * LANES

    def body(where_ref, left_ref, pair_ref, right_ref, right_pair_ref, *rest):
        send_a, keep_a, send_b, keep_b, joined, turned, sems = rest
        at = pl.program_id(0)

        @pl.when(at == 0)
        def _():
            for side, source in enumerate((right_ref, right_pair_ref)):
                for which in range(4):
                    block = jnp.bitwise_xor(where_ref[0], 2 * which)
                    columns = pl.ds(aligned(block * LANES, LANES), LANES)
                    pltpu.make_async_copy(
                        source.at[:, columns],
                        joined.at[side, :, which * LANES : (which + 1) * LANES],
                        sems.at[side],
                    ).start()
            for side in range(2):
                finish(joined.at[side], sems.at[side])
                turned[side] = joined[side].T

        total = product(turned[0], left_ref[...]) + product(turned[1], pair_ref[...])
        total = total.astype(jnp.bfloat16)

        def put(targets):
            for which in range(4):
                ref, slot = targets[which]
                ref[slot, 0] = total[which * LANES : (which + 1) * LANES, :]

        @pl.when(at < half)
        def _():
            put([(keep_a, 0), (send_a, 0), (keep_a, 1), (send_a, 1)])

        @pl.when(at >= half)
        def _():
            put([(keep_b, 0), (keep_b, 1), (send_b, 0), (send_b, 1)])

    def spec(clip):
        return pl.BlockSpec(
            (2, 1, LANES, step), lambda at, _: (0, clip(at) // per, 0, clip(at) % per)
        )

    spec_a = spec(lambda at: jnp.minimum(at, half - 1))
    spec_b = spec(lambda at: jnp.maximum(at - half, 0))
    return pl.pallas_call(
        body,
        grid_spec=pltpu.PrefetchScalarGridSpec(
            num_scalar_prefetch=1,
            grid=(count,),
            in_specs=[pl.BlockSpec((tokens, step), lambda at, _: (0, at))] * 2 + [ANY] * 2,
            out_specs=[spec_a, spec_a, spec_b, spec_b],
            scratch_shapes=[
                pltpu.VMEM((2, tokens, span), jnp.bfloat16),
                pltpu.VMEM((2, span, tokens), jnp.bfloat16),
                pltpu.SemaphoreType.DMA((2,)),
            ],
        ),
        out_shape=[jax.ShapeDtypeStruct((2, groups // 2, LANES, share), jnp.bfloat16)] * 4,
        cost_estimate=cost(4 * rows * tokens * span, 2 * rows * span + 4 * tokens * rows),
        compiler_params=params(22),
    )(where, left, left_pair, right, right_pair)


def finish_flipped(where, pieces):
    size, rows = pieces[0].shape
    step = min(rows, 256)

    def body(where_ref, *refs):
        for at in range(BLOCKS):
            block = jnp.bitwise_xor(where_ref[0], at)
            columns = pl.ds(aligned(block * size, LANES), size)
            refs[-1][:, columns] = refs[at][...].astype(jnp.float32).T

    return pl.pallas_call(
        body,
        grid_spec=pltpu.PrefetchScalarGridSpec(
            num_scalar_prefetch=1,
            grid=(rows // step,),
            in_specs=[pl.BlockSpec((size, step), lambda at, _: (0, at))] * BLOCKS,
            out_specs=pl.BlockSpec((step, BLOCKS * size), lambda at, _: (at, 0)),
        ),
        out_shape=jax.ShapeDtypeStruct((rows, BLOCKS * size), jnp.float32),
        compiler_params=params(12),
    )(where, *pieces)


def join_rows(arrays):
    rows, width = arrays[0].shape

    def body(*refs):
        for at, ref in enumerate(refs[:-1]):
            refs[-1][at * rows : (at + 1) * rows, :] = ref[...]

    return pl.pallas_call(
        body,
        out_shape=jax.ShapeDtypeStruct((rows * len(arrays), width), jnp.bfloat16),
        compiler_params=params(12),
    )(*arrays)


def hop_totals(where, rest, got, groups):
    half, width = rest[0].shape
    share = 2 * half // groups

    def body(where_ref, rest_a, rest_b, got_a, got_b, *outs):
        total = outs[-1]
        for at, (left, right) in enumerate(((rest_a, got_a), (rest_b, got_b))):
            total[at * half : (at + 1) * half, :] = left[...].astype(jnp.float32) + right[
                ...
            ].astype(jnp.float32)
        for hop in range(groups):
            first = jnp.bitwise_xor(where_ref[1], hop) * share
            outs[hop][...] = total[pl.ds(aligned(first, share), share), :].astype(jnp.bfloat16)

    whole = lambda shape: pl.BlockSpec(shape, lambda at, _: (0, 0))
    return pl.pallas_call(
        body,
        grid_spec=pltpu.PrefetchScalarGridSpec(
            num_scalar_prefetch=1,
            grid=(1,),
            in_specs=[whole((half, width))] * 4,
            out_specs=[whole((share, width))] * groups,
            scratch_shapes=[pltpu.VMEM((2 * half, width), jnp.float32)],
        ),
        out_shape=[jax.ShapeDtypeStruct((share, width), jnp.bfloat16)] * groups,
        compiler_params=params(12),
    )(where, *rest, *got)


def pick_blocks(where, sources, outs):
    flat_outs = [item for out in outs for item in out]

    def body(where_ref, *refs):
        in_refs, out_refs = refs[: len(flat_outs)], refs[len(flat_outs) :]
        at = 0
        for out_ref, out in zip(out_refs, outs):
            base = 0
            for _, size, _ in out:
                out_ref[:, base : base + size] = in_refs[at][...]
                base += size
                at += 1

    def mine(source, size, part):
        return pl.BlockSpec(
            (sources[source].shape[0], size),
            lambda at, where_ref: (0, part * BLOCKS + where_ref[0]),
        )

    shapes = [(sources[out[0][0]].shape[0], sum(item[1] for item in out)) for out in outs]
    return pl.pallas_call(
        body,
        grid_spec=pltpu.PrefetchScalarGridSpec(
            num_scalar_prefetch=1,
            grid=(1,),
            in_specs=[mine(*item) for item in flat_outs],
            out_specs=[pl.BlockSpec(shape, lambda at, _: (0, 0)) for shape in shapes],
        ),
        out_shape=[jax.ShapeDtypeStruct(shape, jnp.bfloat16) for shape in shapes],
        compiler_params=params(12),
    )(where, *[sources[item[0]] for item in flat_outs])


def unpack_vectors(where, sources, lengths, pair_at, width):
    groups = len(sources)
    row = sources[0].shape[1]
    outs = [3 * width if at == pair_at else length * groups for at, length in enumerate(lengths)]

    def body(where_ref, *refs):
        source_refs, out_refs = refs[:groups], refs[groups:]
        out_refs[pair_at][...] = jnp.zeros((1, 3 * width), jnp.float32)
        for hop in range(groups):
            block = source_refs[hop][...].astype(jnp.float32)
            owner = jnp.bitwise_xor(where_ref[1], hop)
            place = 0
            for which, length in enumerate(lengths):
                start = owner * length
                if which == pair_at:
                    start = start + jnp.where(start >= width, width, 0)
                for begin in range(0, length, LANES):
                    line, lane = (place + begin) // row, (place + begin) % row
                    target = pl.ds(aligned(start + begin, LANES), LANES)
                    out_refs[which][:, target] = block[line : line + 1, lane : lane + LANES]
                place += length

    return pl.pallas_call(
        body,
        grid_spec=pltpu.PrefetchScalarGridSpec(
            num_scalar_prefetch=1,
            grid=(1,),
            in_specs=[pl.BlockSpec((16, row), lambda at, _: (0, 0))] * groups,
            out_specs=[pl.BlockSpec((1, size), lambda at, _: (0, 0)) for size in outs],
        ),
        out_shape=[jax.ShapeDtypeStruct((1, size), jnp.float32) for size in outs],
        compiler_params=params(8),
    )(where, *sources)


def pack_sums(vectors, groups):
    total = sum(vec.shape[1] for vec in vectors) // groups

    def body(*refs):
        for owner in range(groups):
            pieces = []
            for ref in refs[:-1]:
                length = ref.shape[1] // groups
                pieces.append(ref[:, owner * length : (owner + 1) * length])
            refs[-1][owner : owner + 1, :] = jnp.concatenate(pieces, axis=1)

    return pl.pallas_call(
        body,
        out_shape=jax.ShapeDtypeStruct((groups, total), jnp.float32),
        compiler_params=params(8),
    )(*vectors)


def unpack_sums(where, first, second, lengths):
    groups, total = first.shape

    def body(where_ref, first_ref, second_ref, *outs):
        line = jnp.zeros((1, total), jnp.float32)
        for owner in range(groups):
            both = first_ref[owner : owner + 1, :] + second_ref[owner : owner + 1, :]
            line = jnp.where(where_ref[1] == owner, both, line)
        place = 0
        for out, length in zip(outs, lengths):
            out[...] = line[:, place : place + length]
            place += length

    whole = pl.BlockSpec((groups, total), lambda at, _: (0, 0))
    return pl.pallas_call(
        body,
        grid_spec=pltpu.PrefetchScalarGridSpec(
            num_scalar_prefetch=1,
            grid=(1,),
            in_specs=[whole, whole],
            out_specs=[pl.BlockSpec((1, length), lambda at, _: (0, 0)) for length in lengths],
        ),
        out_shape=[jax.ShapeDtypeStruct((1, length), jnp.float32) for length in lengths],
        compiler_params=params(8),
    )(where, first, second)


def finish_blocks(blocks, sizes):
    count, rows, width = blocks.shape
    step = min(rows, 128)

    def body(in_ref, *out_refs):
        base = 0
        for out_ref, size in zip(out_refs, sizes):
            for at in range(count):
                out_ref[:, at * size : (at + 1) * size] = in_ref[
                    at, :, base : base + size
                ].astype(jnp.float32)
            base += size

    return pl.pallas_call(
        body,
        grid=(rows // step,),
        in_specs=[pl.BlockSpec((count, step, width), lambda at: (0, at, 0))],
        out_specs=[pl.BlockSpec((step, count * size), lambda at: (at, 0)) for size in sizes],
        out_shape=[jax.ShapeDtypeStruct((rows, count * size), jnp.float32) for size in sizes],
        compiler_params=params(12),
    )(blocks)


def finish_grads(where, pieces, strips):
    rows = pieces[0].shape[0]
    step = min(rows, 128)
    totals = {}
    for _, size, out, base in strips:
        totals[out] = max(totals.get(out, 0), base + size * BLOCKS)

    def body(where_ref, *refs):
        piece_refs, out_refs = refs[:BLOCKS], refs[BLOCKS:]
        for at in range(BLOCKS):
            block = jnp.bitwise_xor(where_ref[0], at)
            for start, size, out, base in strips:
                target = pl.ds(aligned(base + block * size, LANES), size)
                out_refs[out][:, target] = piece_refs[at][:, start : start + size].astype(
                    jnp.float32
                )

    return pl.pallas_call(
        body,
        grid_spec=pltpu.PrefetchScalarGridSpec(
            num_scalar_prefetch=1,
            grid=(rows // step,),
            in_specs=[
                pl.BlockSpec((step, piece.shape[1]), lambda at, _: (at, 0)) for piece in pieces
            ],
            out_specs=[
                pl.BlockSpec((step, totals[out]), lambda at, _: (at, 0)) for out in sorted(totals)
            ],
        ),
        out_shape=[
            jax.ShapeDtypeStruct((rows, totals[out]), jnp.float32) for out in sorted(totals)
        ],
        compiler_params=params(12),
    )(where, *pieces)


REP, GRP = "rep", "grp"


def exchange(tensor, mask, axis=REP):
    size = lax.axis_size(axis)
    return lax.ppermute(tensor, axis, [(at, at ^ mask) for at in range(size)])


def tie(value, *others):
    return lax.optimization_barrier((value, others))[0]


def all_hops(block):
    return [exchange(block, hop, GRP) for hop in range(1, lax.axis_size(GRP))]


def spread(own):
    by_x = exchange(own, 2)
    by_y = exchange(own, 4)
    half = own.shape[0] // 2
    sent = (by_x[:half], by_y[half:])
    top = exchange(sent[0], 4)
    bottom = exchange(sent[1], 2)
    pieces = []
    for piece in ((own,), (by_x,), (by_y,), (top, bottom)):
        pair = tuple(exchange(array, 1) for array in piece)
        pieces += [piece, pair]
    return pieces, sent


def add_rounded(left, right):
    return (left.astype(jnp.float32) + right.astype(jnp.float32)).astype(jnp.bfloat16)


def first_sends(parts):
    return exchange(parts[0], 2), exchange(parts[2], 4)


def second_sends(parts, got):
    keep_a, keep_b = parts[1], parts[3]
    got_a, got_b = got
    next_a = exchange(add_rounded(keep_a[1], got_a[1]), 4)
    next_b = exchange(add_rounded(keep_b[1], got_b[1]), 2)
    rest_a = add_rounded(keep_a[0], got_a[0])
    rest_b = add_rounded(keep_b[0], got_b[0])
    return (rest_a, rest_b), (next_a, next_b)


def block_total(rest, got):
    total = jnp.concatenate([add_rounded(*pair) for pair in zip(rest, got)], axis=0)
    mask = BLOCKS
    while mask < lax.axis_size(REP):
        total = add_rounded(total, exchange(total, mask))
        mask *= 2
    return total


def scatter(total):
    return lax.psum_scatter(total, GRP, scatter_dimension=0, tiled=True)


def gather(own):
    return lax.all_gather(own, REP, axis=0, tiled=False)[:BLOCKS]


def widened(rest, got):
    mask = BLOCKS
    while mask < lax.axis_size(REP):
        rest = [add_rounded(*pair) for pair in zip(rest, got)]
        got = [exchange(array, mask) for array in rest]
        mask *= 2
    return rest, got


def sum_rounded(own, got):
    total = own.astype(jnp.float32)
    for other in got:
        total = total + other.astype(jnp.float32)
    return total.astype(jnp.bfloat16)


def layer(
    images,
    cotangent,
    ln1_gain,
    ln1_shift,
    qkv_weight,
    qv_bias,
    out_weight,
    out_bias,
    ln2_gain,
    ln2_shift,
    fc1_weight,
    fc1_bias,
    fc2_weight,
    fc2_bias,
):
    groups = lax.axis_size(GRP)
    place = jnp.bitwise_and(lax.axis_index(REP), BLOCKS - 1)
    where = jnp.stack([place, lax.axis_index(GRP)])
    _, width = out_weight.shape
    hidden_block = fc1_weight.shape[1] // BLOCKS

    (block_a,) = pick_blocks(
        where,
        [qkv_weight, out_weight],
        [[(0, LANES, part) for part in range(3)] + [(1, LANES, 0)]],
    )
    got_a = all_hops(block_a)
    vectors = (ln1_gain, ln1_shift, qv_bias, out_bias, ln2_gain, ln2_shift, fc1_bias, fc2_bias)
    sizes = [vec.shape[0] for vec in vectors]
    length = 16 * 2 * LANES
    packed, offset = jnp.zeros((length,), jnp.bfloat16), 0
    for vec, size in zip(vectors, sizes):
        packed = packed + jnp.pad(vec, (offset, length - offset - size))
        offset += size
    packed = packed.reshape(16, 2 * LANES)
    got_v = all_hops(packed)
    block_b, block_c = pick_blocks(
        where,
        [fc1_weight, fc2_weight],
        [[(0, hidden_block, 0)], [(1, LANES, 0)]],
    )
    got_b = all_hops(block_b)
    got_c = all_hops(block_c)
    pieces_a, sent_a = spread(join_rows(got_a))
    pieces_b, sent_b = spread(join_rows(tie(got_b, sent_a)))
    pieces_c, _ = spread(join_rows(tie(got_c, sent_b)))
    gain_1, shift_1, bias_in, bias_attn, gain_2, shift_2, bias_up, bias_down = unpack_vectors(
        where, [packed] + got_v, sizes, 2, width
    )

    image = images[0]
    grad_block = cotangent[0]
    cot_pair = exchange(grad_block, 1)

    normed_in, projected = qkv_forward(where, image, gain_1, shift_1, bias_in, qkv_weight, pieces_a)
    normed_pair = exchange(normed_in, 1)
    attended, totals = attention_forward(projected)
    attended_pair = exchange(attended, 1)
    residual, normed_mid = out_forward(
        where, image, attended, bias_attn, gain_2, shift_2, out_weight, pieces_a, 3 * LANES
    )
    mid_pair = exchange(normed_mid, 1)
    active, slope = up_forward(where, normed_mid, bias_up, fc1_weight, pieces_b)
    active_pair = exchange(active, 1)

    down_parts = weight_grads_flipped(
        where, active, active_pair, grad_block, cot_pair, groups
    )
    down_got = first_sends(down_parts)
    grad_pre, sum_up = down_backward(
        tie(where, down_parts), grad_block, slope, fc2_weight, pieces_c
    )
    pre_pair = exchange(grad_pre, 1)
    middle = middle_backward(
        where,
        grad_pre,
        grad_block,
        residual,
        gain_2,
        fc1_weight,
        out_weight,
        pieces_b,
        pieces_a,
        hidden_block,
    )
    grad_res, grad_res_b, grad_attended, sum_gain_2, sum_shift_2, sum_res, sum_top = middle
    res_pair = exchange(grad_res_b, 1)
    down_rest, down_got = second_sends(down_parts, tie(down_got, grad_res))
    up_parts = weight_grads(
        tie(where, grad_res, down_rest),
        [
            (normed_mid, mid_pair, grad_pre, pre_pair, hidden_block),
            (attended, attended_pair, grad_res_b, res_pair, LANES),
        ],
    )
    up_got = first_sends(up_parts)
    down_total = block_total(down_rest, tie(down_got, up_parts))
    down_own = scatter(down_total)
    grad_proj, sum_query, sum_value = attention_backward(
        projected, tie(grad_attended, up_parts, down_total), totals
    )
    proj_pair = exchange(grad_proj, 1)
    up_rest, up_got = second_sends(up_parts, tie(up_got, grad_proj))
    qkv_parts = weight_grads(
        tie(where, up_rest), [(normed_in, normed_pair, grad_proj, proj_pair, LANES)]
    )
    qkv_got = first_sends(qkv_parts)
    up_total = block_total(up_rest, tie(up_got, qkv_parts))
    up_own = scatter(up_total)
    input_grad, sum_gain_1, sum_shift_1 = qkv_backward(
        tie(where, qkv_parts, up_total),
        grad_proj,
        image,
        grad_res,
        gain_1,
        qkv_weight,
        pieces_a,
    )
    sums = pack_sums(
        [
            sum_gain_1,
            sum_shift_1,
            jnp.concatenate([sum_query, sum_value], axis=1),
            sum_res,
            sum_gain_2,
            sum_shift_2,
            sum_up,
            sum_top,
        ],
        groups,
    )
    got = exchange(sums, 1)
    qkv_rest, qkv_got = second_sends(qkv_parts, tie(qkv_got, sums))
    sums = sums + tie(got, qkv_rest)
    got = exchange(sums, 2)
    block_out = down_forward(
        tie(where, input_grad, sums, qkv_rest), residual, active, bias_down, fc2_weight, pieces_c
    )
    sums = sums + tie(got, block_out)
    mask = BLOCKS
    while mask < lax.axis_size(REP):
        sums = sums + exchange(sums, mask)
        mask *= 2
    qkv_rest, qkv_got = widened(qkv_rest, tie(qkv_got, block_out, sums))
    own, *qkv_sent = hop_totals(where, qkv_rest, qkv_got, groups)
    qkv_got = [exchange(sent, hop, GRP) for hop, sent in enumerate(qkv_sent, start=1)]
    down_own = tie(down_own, own)[0]
    down_x = exchange(down_own, 2)
    down_y = exchange(down_own, 4)
    up_blocks = gather(tie(up_own, own))
    sums = sums + exchange(tie(sums, own), 4)
    down_both = exchange(tie(down_x, sums), 4)
    own = sum_rounded(own, tie(qkv_got, sums, down_x, down_y))
    by_x = exchange(own, 2)
    by_y = exchange(own, 4)
    mask = 1
    while mask * 2 < groups:
        sums = sums + exchange(tie(sums, own), mask, GRP)
        mask *= 2
    down_pieces = []
    for piece in (down_own, down_x, down_y, down_both):
        down_pieces += [piece, exchange(piece, 1)]
    both = exchange(tie(by_x, sums), 4)
    last = exchange(tie(sums, by_x), mask, GRP)
    grad_down = finish_flipped(tie(where, own), down_pieces)
    qkv_pieces = []
    for piece in (own, by_x, by_y, both):
        qkv_pieces += [piece, exchange(piece, 1)]
    grad_up, grad_out = finish_blocks(tie(up_blocks, grad_down, by_x, by_y), [hidden_block, LANES])
    (grad_qkv,) = finish_grads(
        where, qkv_pieces, [(at * LANES, LANES, 0, at * width) for at in range(3)]
    )
    sums = [vec.reshape(-1) for vec in unpack_sums(where, sums, last, sizes)]
    return (
        block_out[None],
        input_grad[None],
        sums[0],
        sums[1],
        grad_qkv,
        sums[2],
        grad_out,
        sums[3],
        sums[4],
        sums[5],
        grad_up,
        sums[6],
        grad_down,
        sums[7],
    )


def solution(mesh):
    tokens = P((REP, GRP), None, None)
    vector, matrix = P(GRP), P(GRP, None)
    weights = (vector, vector, matrix, vector, matrix, vector)
    weights += (vector, vector, matrix, vector, matrix, vector)
    specs = (tokens, tokens) + weights
    return jax.shard_map(layer, mesh=mesh, in_specs=specs, out_specs=specs, check_vma=False)
```
